32 devices in a mesh: dp: 8 (over y, x, core), mp: 4 (over z).
Axes of the slice: x: 2, y: 2, z: 4, core: 2. Of those that a mesh axis runs over, the one named last changes fastest.
Arguments:
- tokens: bfloat16 [16384, 768], P('dp'), may hold values from -6 to 6
- segment_ids: int32 [64, 256], P('dp'), may hold values from 0 to 6, as said below
- cotangent: bfloat16 [16384, 768], P('dp'), may hold values from -6 to 6
- w_qkv: bfloat16 [3, 768, 768], P(None, None, 'mp'), may hold values from -0.21875 to 0.21875
- b_qv: float32 [2, 768], P(None, 'mp'), may hold values from -3 to 3
- w_out: bfloat16 [768, 768], P('mp'), may hold values from -0.5 to 0.5
- b_out: float32 [768], replicated, may hold values from -2 to 2
- gain_one: float32 [768], replicated, may hold values from 0.5 to 1.5
- shift_one: float32 [768], replicated, may hold values from -2 to 2
- w_up: bfloat16 [768, 3072], P(None, 'mp'), may hold values from -0.21875 to 0.21875
- b_up: float32 [3072], P('mp'), may hold values from -3 to 3
- w_down: bfloat16 [3072, 768], P('mp'), may hold values from -0.15625 to 0.15625
- b_down: float32 [768], replicated, may hold values from -2 to 2
- gain_two: float32 [768], replicated, may hold values from 0.5 to 1.5
- shift_two: float32 [768], replicated, may hold values from -2 to 2
Outputs:
- block_out: bfloat16 [16384, 768], P('dp')
- input_grad: bfloat16 [16384, 768], P('dp')
- grad_w_qkv: float32 [3, 768, 768], P(None, None, 'mp')
- grad_b_qv: float32 [2, 768], P(None, 'mp')
- grad_w_out: float32 [768, 768], P('mp')
- grad_b_out: float32 [768], replicated
- grad_gain_one: float32 [768], replicated
- grad_shift_one: float32 [768], replicated
- grad_w_up: float32 [768, 3072], P(None, 'mp')
- grad_b_up: float32 [3072], P('mp')
- grad_w_down: float32 [3072, 768], P('mp')
- grad_b_down: float32 [768], replicated
- grad_gain_two: float32 [768], replicated
- grad_shift_two: float32 [768], replicated
The draws below stay inside these ranges and needn't reach their ends.
Inputs may be any that keep to these rules, and one draw needn't show every extreme that they name: `segment_ids`: along a row, captions carry ids 1, 2, ... in order, each caption one run of 1 to 64 tokens, and padding (0) only after the last caption; in every row one caption has exactly 64 tokens.
All inputs are finite; a program needn't handle non-finite values.
Results may differ from the reference program's by a relative error of at most 0.02.
Values may be sent and summed in bfloat16 or wider, within the bound.
A program may use at most 128 MiB of HBM per device.

```python
import math
import jax
import jax.numpy as jnp
from jax import lax

D = 768
HEADS = 12
HD = 64
FF = 3072
SEQ = 256
MOST = 64
CAPS = 6
ROWS = 64
TOKENS = 16384
N_MP = 4


def draw_segment_ids(key, part):
    length_key, slot_key = jax.random.split(jax.random.fold_in(key, 7))
    lengths = jax.random.randint(length_key, (ROWS, CAPS), 1, MOST + 1)
    slot = jax.random.randint(slot_key, (ROWS, 1), 0, 3)
    lengths = jnp.where(jnp.arange(CAPS)[None, :] == slot, MOST, lengths)
    ends = jnp.cumsum(lengths, axis=1)
    places = jnp.arange(SEQ)
    ids = 1 + jnp.sum((places[None, :, None] >= ends[:, None, :]).astype(jnp.int32), axis=2)
    return jnp.where(ids > CAPS, 0, ids).astype(jnp.int32)


def block_scale(rng, extent, cuts, least, largest):
    def one(axis_at, shards_of):
        heights = jax.random.uniform(jax.random.fold_in(jax.random.fold_in(rng, 6), axis_at), (shards_of,), jnp.float32, least / len(cuts), largest / len(cuts))
        return jnp.repeat(jnp.exp(heights), extent[axis_at] // shards_of).reshape((-1,) + (1,) * (len(extent) - axis_at - 1))

    level = one(*cuts[0])
    for cut in cuts[1:]:
        level = level * one(*cut)
    return level


def noise(stream_key, dims, scale, reach, shards=(), dtype=jnp.bfloat16):
    result = jax.random.normal(stream_key, dims, jnp.float32) * scale
    if len(shards) > 0:
        result = block_scale(stream_key, dims, shards, -0.22, 0.18) * result
    return jnp.clip(result, min=-reach, max=reach).astype(dtype)


def setup_inputs(seed: int = 0) -> dict:
    streams_of = jax.random.split(jax.random.key(seed), 16)
    return {
        "tokens": noise(streams_of[0], (TOKENS, D), 1.0, 6.0, ((0, 8),)),
        "segment_ids": draw_segment_ids(jax.random.fold_in(streams_of[15], 71), 0),
        "cotangent": noise(streams_of[2], (TOKENS, D), 1.0, 6.0, ((0, 8),)),
        "w_qkv": noise(streams_of[3], (3, D, HEADS * HD), D ** -0.5, 0.21875, ((2, 4),)),
        "b_qv": noise(streams_of[4], (2, HEADS * HD), 0.5, 3.0, ((1, 4),), jnp.float32),
        "w_out": noise(streams_of[5], (HEADS * HD, D), (D // 6) ** -0.5, 0.5, ((0, 4),)),
        "b_out": noise(streams_of[6], (D,), 0.3, 2.0, (), jnp.float32),
        "gain_one": jnp.clip(1.0 + 0.1 * jax.random.normal(streams_of[7], (D,), jnp.float32), 0.5, 1.5),
        "shift_one": noise(streams_of[8], (D,), 0.3, 2.0, (), jnp.float32),
        "w_up": noise(streams_of[9], (D, FF), D ** -0.5, 0.21875, ((1, 4),)),
        "b_up": noise(streams_of[10], (FF,), 0.5, 3.0, ((0, 4),), jnp.float32),
        "w_down": noise(streams_of[11], (FF, D), (FF // 2) ** -0.5, 0.15625, ((0, 4),)),
        "b_down": noise(streams_of[12], (D,), 0.3, 2.0, (), jnp.float32),
        "gain_two": jnp.clip(1.0 + 0.1 * jax.random.normal(streams_of[13], (D,), jnp.float32), 0.5, 1.5),
        "shift_two": noise(streams_of[14], (D,), 0.3, 2.0, (), jnp.float32),
    }


@jax.custom_vjp
def low(v):
    return lax.optimization_barrier(v.astype(jnp.bfloat16)).astype(jnp.float32)

@jax.custom_vjp
def low_back(v):
    return v

def low_keep(v):
    return (low(v), None)

def low_pass(kept, grad):
    return (grad,)

def back_keep(v):
    return (v, None)

def back_low(kept, grad):
    return (low(grad),)
low.defvjp(low_keep, low_pass)
low_back.defvjp(back_keep, back_low)
EPS = 1e-06
MASKED = -1000000000.0

def norm_rows(hidden, gain, shift):
    centre = hidden - lax.optimization_barrier(jnp.mean(hidden, axis=-1, keepdims=True))
    inverse = lax.rsqrt(lax.optimization_barrier(jnp.mean(centre * centre, axis=-1, keepdims=True)) + EPS)
    return centre * inverse * gain + shift

def product(left, right):
    return jnp.dot(left, right, precision=lax.Precision.HIGHEST, preferred_element_type=jnp.float32)

def forward(params, inputs, same):
    w_qkv, b_qv, w_out, b_out, gain_one, shift_one, w_up, b_up, w_down, b_down, gain_two, shift_two = params
    rows = same.shape[0]
    local_heads = HEADS // N_MP
    width = local_heads * HD
    hidden = FF // N_MP
    scale = HD ** (-0.5)
    normed_one = low(norm_rows(inputs, gain_one, shift_one))
    attn_total = jnp.zeros_like(inputs)
    for group in range(N_MP):
        cols = slice(group * width, (group + 1) * width)
        shared = low_back(normed_one)
        query = low(low_back(product(shared, w_qkv[0][:, cols])) + b_qv[0][cols])
        keys = low(low_back(product(shared, w_qkv[1][:, cols])))
        values = low(low_back(product(shared, w_qkv[2][:, cols])) + b_qv[1][cols])
        query = query.reshape(rows, SEQ, local_heads, HD)
        keys = keys.reshape(rows, SEQ, local_heads, HD)
        values = values.reshape(rows, SEQ, local_heads, HD)
        scores = low_back(jnp.einsum('rqhd,rkhd->rhqk', query, keys, precision=lax.Precision.HIGHEST) * scale)
        scores = jnp.where(same[:, None], scores, MASKED)
        probs = low(jax.nn.softmax(scores, axis=-1))
        mixed = jnp.einsum('rhqk,rkhd->rqhd', probs, values, precision=lax.Precision.HIGHEST)
        mixed = low(low_back(mixed.reshape(rows * SEQ, width)))
        attn_total = attn_total + low(product(mixed, w_out[cols, :]))
    residual = inputs + low_back(attn_total) + b_out
    normed_two = low(norm_rows(residual, gain_two, shift_two))
    mlp_total = jnp.zeros_like(inputs)
    for group in range(N_MP):
        units = slice(group * hidden, (group + 1) * hidden)
        shared = low_back(normed_two)
        pre_act = low_back(product(shared, w_up[:, units])) + b_up[units]
        act = low(jax.nn.gelu(pre_act, approximate=True))
        mlp_total = mlp_total + low(product(act, w_down[units, :]))
    return residual + low_back(mlp_total) + b_down

def reference(tokens, segment_ids, cotangent, w_qkv, b_qv, w_out, b_out, gain_one, shift_one, w_up, b_up, w_down, b_down, gain_two, shift_two):
    params = tuple((p.astype(jnp.float32) for p in (w_qkv, b_qv, w_out, b_out, gain_one, shift_one, w_up, b_up, w_down, b_down, gain_two, shift_two)))
    group = math.gcd(ROWS, 16)
    blocks = ROWS // group
    inputs = tokens.astype(jnp.float32).reshape(blocks, group * SEQ, D)
    keep = (segment_ids != 0).astype(jnp.float32).reshape(blocks, group * SEQ, 1)
    grads_in = cotangent.astype(jnp.float32).reshape(blocks, group * SEQ, D) * keep
    segments = segment_ids.reshape(blocks, group, SEQ)

    def step(total, block):
        block_in, block_grad, block_seg = block
        same = block_seg[:, :, None] == block_seg[:, None, :]
        out, back = jax.vjp(lambda prm, inp: forward(prm, inp, same), params, block_in)
        grad_params, grad_inputs = back(block_grad)
        total = jax.tree.map(lambda a, b: a + b, total, grad_params)
        return (total, (out.astype(jnp.bfloat16), grad_inputs.astype(jnp.bfloat16)))
    zeros = jax.tree.map(jnp.zeros_like, params)
    total, (outputs, in_grads) = lax.scan(step, zeros, (inputs, grads_in, segments))
    g_qkv, g_bqv, g_wout, g_bout, g_gone, g_sone, g_wup, g_bup, g_wdown, g_bdown, g_gtwo, g_stwo = total
    return (outputs.reshape(TOKENS, D), in_grads.reshape(TOKENS, D), g_qkv, g_bqv, g_wout, g_bout, g_gone, g_sone, g_wup, g_bup, g_wdown, g_bdown, g_gtwo, g_stwo)
```

```python
import jax
import jax.numpy as jnp
from jax import lax
from jax.experimental import pallas as pl
from jax.experimental.pallas import tpu as pltpu
from jax.sharding import PartitionSpec as P

HD = 64
SEQ = 256
EPS = 1e-06
MASKED = -1000000000.0
MESH = pl.DeviceIdType.MESH
F32 = jnp.float32
BF16 = jnp.bfloat16
MP = 4
GELU_C = 0.7978845608028654
GELU_A = 0.044715
VMEM_LIMIT = 66_000_000


def nn(a, b):
    return lax.dot_general(a, b, (((1,), (0,)), ((), ())), preferred_element_type=F32)


def nt(a, b):
    return lax.dot_general(a, b, (((1,), (1,)), ((), ())), preferred_element_type=F32)


def tn(a, b):
    return lax.dot_general(a, b, (((0,), (0,)), ((), ())), preferred_element_type=F32)


def xor4(a, b):
    return (a % 2 + b % 2) % 2 + 2 * ((a // 2 + b // 2) % 2)


def places():
    d = lax.axis_index("dp")
    z = lax.axis_index("mp")
    p = d % 8
    kb, xb, yb = p % 2, (p // 2) % 2, (p // 4) % 2
    fc = d + (1 - 2 * kb)
    fx = d + 2 * (1 - 2 * xb)
    fy = d + 4 * (1 - 2 * yb)
    a = fx * (1 - kb) + fy * kb
    b = fy * (1 - kb) + fx * kb
    bit_a = xb * (1 - kb) + yb * kb
    bit_b = yb * (1 - kb) + xb * kb
    return d, z, p, kb, fc, a, b, bit_a, bit_b


def rows_at(start, size):
    return pl.ds(pl.multiple_of(start, size), size)


def norm_parts(h):
    centre = h - jnp.mean(h, axis=-1, keepdims=True)
    inverse = lax.rsqrt(jnp.mean(centre * centre, axis=-1, keepdims=True) + EPS)
    return centre * inverse, inverse


def norm_back(grad, normal, inverse, gain):
    scaled = grad * gain
    return inverse * (
        scaled
        - jnp.mean(scaled, axis=-1, keepdims=True)
        - normal * jnp.mean(scaled * normal, axis=-1, keepdims=True)
    )


def forward_kernel(
    count,
    x_hbm, cot_hbm, seg, wa_hbm, wu_hbm, wd_hbm, bp_hbm, vec,
    out_hbm, qkvr_hbm, e_hbm, n1_hbm, mixed_hbm, gres_hbm, waf_hbm, gw_ref, small,
    W, BP, xv, glv, n1v, mixv, acc, gn2, bias, rstd, gwu, gwd, stq, ste,
    load_sem, own_sem, stage_sem, out_sem, zsend, send, recv, bsend, brecv,
):
    d, z, p, kb, fc, a, b, bit_a, bit_b = places()
    chunks = count // 512
    rows = count // SEQ

    loads = []
    for c in range(chunks):
        part = pl.ds(c * 512, 512)
        loads.append((
            pltpu.make_async_copy(x_hbm.at[part], xv.at[part], load_sem.at[0, c]),
            pltpu.make_async_copy(cot_hbm.at[part], glv.at[part], load_sem.at[1, c]),
        ))
        loads[-1][0].start()
        loads[-1][1].start()
    own = [
        pltpu.make_async_copy(wa_hbm, W.at[z, pl.ds(0, 768)], own_sem.at[0]),
        pltpu.make_async_copy(wu_hbm, W.at[z, pl.ds(768, 768)], own_sem.at[1]),
        pltpu.make_async_copy(wd_hbm, W.at[z, pl.ds(1536, 768)], own_sem.at[2]),
        pltpu.make_async_copy(bp_hbm, BP.at[z], own_sem.at[3]),
    ]
    for copy in own:
        copy.start()

    peers = [(d, xor4(z, s)) for s in (1, 2, 3)] + [(fc, z), (a, z), (b, z)]
    barrier = pltpu.get_barrier_semaphore()
    for peer in peers:
        pl.semaphore_signal(barrier, inc=1, device_id=peer, device_id_type=MESH)
    pl.semaphore_wait(barrier, len(peers))

    def remote(src, dst, ss, rs, to):
        return pltpu.make_async_remote_copy(
            src_ref=src, dst_ref=dst, send_sem=ss, recv_sem=rs, device_id=to, device_id_type=MESH
        )

    def piece_rows(base, which):
        return pl.ds(pl.multiple_of(base + 96 * which, 96), 96)

    zcopies = []
    for s in (1, 2, 3):
        to = (d, xor4(z, s))
        zcopies.append(remote(bp_hbm, BP.at[z], bsend.at[s - 1], brecv.at[s - 1], to))
        zcopies.append(remote(
            wa_hbm.at[piece_rows(0, p)], W.at[z, piece_rows(0, p)], zsend.at[s - 1], recv.at[s - 1, 0], to
        ))
    for k in range(3):
        there = k + jnp.where(z <= k, 1, 0)
        order = z - jnp.where(z > there, 1, 0)
        for h, w_hbm in ((0, wu_hbm), (1, wd_hbm)):
            zcopies.append(remote(
                w_hbm.at[piece_rows(0, p)],
                W.at[z, piece_rows(768 * (h + 1), p)],
                zsend.at[3 + 2 * k + h],
                recv.at[3 + 2 * order + h, 0],
                (d, there),
            ))
    for copy in zcopies:
        copy.start()

    def step_of(t):
        if isinstance(t, int) and t < 3:
            return xor4(z, t + 1), 0
        k = (t - 3) // 2
        g = k + jnp.where(k >= z, 1, 0)
        return g, 768 + 768 * ((t - 3) % 2)

    def hop(t, index, which, to):
        g, base = step_of(t)
        part = W.at[g, piece_rows(base, which)]
        return remote(part, part, send.at[t, index], recv.at[t, index], to)

    pa, pb, pc = a % 8, b % 8, fc % 8
    pd = (a + b - d) % 8
    me = (d, z)

    def s1(t):
        hop(t, 0, p, me).wait_recv()
        hop(t, 1, p, (a, z)).start()
        hop(t, 2, p, (b, z)).start()
        hop(t, 3, p, (fc, z)).start()

    def s2(t):
        hop(t, 1, pa, me).wait_recv()
        hop(t, 4, pa, (b, z)).start()
        hop(t, 5, pa, (fc, z)).start()
        hop(t, 2, pb, me).wait_recv()
        hop(t, 6, pb, (fc, z)).start()

    def s3(t):
        hop(t, 4, pd, me).wait_recv()
        hop(t, 7, pd, (fc, z)).start()

    def core_flip(q):
        return q + 1 - 2 * (q % 2)

    def fin(t):
        hop(t, 3, core_flip(p), me).wait_recv()
        hop(t, 5, core_flip(pb), me).wait_recv()
        hop(t, 6, core_flip(pa), me).wait_recv()
        hop(t, 7, core_flip(pd), me).wait_recv()

    small[...] = jnp.zeros_like(small)
    gain_one, shift_one, b_out = vec[0:1], vec[1:2], vec[2:3]
    gain_two, shift_two, b_down = vec[3:4], vec[4:5], vec[5:6]

    def head(r, carry):
        part = rows_at(r * SEQ, SEQ)
        normal, inverse = norm_parts(xv[part].astype(F32))
        n1v[part] = (normal * gain_one + shift_one).astype(BF16)
        seg_row = seg[pl.ds(r, 1)]
        seg_col = jnp.broadcast_to(seg_row, (128, SEQ)).T
        for half in range(2):
            lanes = slice(half * 128, half * 128 + 128)
            bias[r, :, lanes] = jnp.where(seg_col == seg_row[:, lanes], 0.0, MASKED)
        for part6 in range(6):
            lanes = slice(part6 * 128, part6 * 128 + 128)
            masked = jnp.where(seg_col != 0.0, glv[part, lanes].astype(F32), 0.0)
            small[0:1, lanes] += jnp.sum(masked, axis=0, keepdims=True)
            glv[part, lanes] = masked.astype(BF16)
        return carry

    for pair in loads:
        pair[0].wait()
        pair[1].wait()
    lax.fori_loop(0, rows, head, 0)
    save_n1 = pltpu.make_async_copy(n1v, n1_hbm, out_sem.at[0])
    save_n1.start()
    for copy in own:
        copy.wait()

    lo = lax.broadcasted_iota(jnp.int32, (SEQ, 128), 1) < HD
    lo_b = lo

    def stage_copies(slot, u):
        return (
            pltpu.make_async_copy(stq.at[slot], qkvr_hbm.at[u], stage_sem.at[0, slot]),
            pltpu.make_async_copy(ste.at[slot], e_hbm.at[u], stage_sem.at[1, slot]),
        )

    plan = {
        2: [(s1, 0)],
        3: [(s2, 0), (s1, 1)],
        4: [(s3, 0), (fin, 0), (s1, 2)],
        5: [(s2, 1)],
        6: [(s3, 1), (s2, 2)],
        7: [(s3, 2), (s1, 3)],
        8: [(fin, 1), (s1, 4)],
        9: [(s2, 3)],
        10: [(s3, 3), (s2, 4)],
        11: [(s3, 4), (s1, 5)],
        12: [(fin, 2), (s1, 6)],
        13: [(s2, 5)],
        14: [(s3, 5), (s2, 6)],
        15: [(s3, 6), (s1, 7)],
    }

    def attend(i, carry):
        for when, actions in plan.items():
            @pl.when(i == when)
            def _():
                for action, t in actions:
                    action(t)

        for s in (1, 2, 3):
            @pl.when(i == 4 * s)
            def _():
                remote(bp_hbm, BP.at[xor4(z, s)], bsend.at[s - 1], brecv.at[s - 1], me).wait_recv()

        s, c = i // 4, i % 4
        g = xor4(z, s)
        slot = i % 2
        u = g * 4 + c
        tok = rows_at(c * 512, 512)

        @pl.when(i >= 2)
        def _():
            for copy in stage_copies(slot, u):
                copy.wait()

        n1c = n1v[tok]
        v_all = (nt(n1c, W[g, 0:256]) + BP[g, 2:3, 0:256]).astype(BF16)
        q_all = ((nt(n1c, W[g, 192:448]) + BP[g, 1:2, 0:256]) * 0.125).astype(BF16)
        k_all = nt(n1c, W[g, 384:640]).astype(BF16)
        stq[slot, 0] = v_all
        stq[slot, 1] = q_all
        stq[slot, 2] = k_all
        one = jnp.ones((SEQ, 128), BF16)
        zero = jnp.zeros((SEQ, 128), BF16)
        for r in range(2):
            tr = slice(r * SEQ, r * SEQ + SEQ)
            mask = bias[c * 2 + r]

            def weights(qp, kp, h):
                sc = nt(qp, kp) + mask
                e = jnp.exp(sc - jnp.max(sc, axis=-1, keepdims=True)).astype(BF16)
                ste[slot, r * 3 + h] = e
                return e

            qp, kp, vp = q_all[tr, 0:128], k_all[tr, 0:128], v_all[tr, 0:128]
            e0 = weights(qp, jnp.where(lo_b, kp, zero), 0)
            o0 = nn(e0, jnp.where(lo_b, vp, one))
            e1 = weights(qp, jnp.where(lo_b, zero, kp), 1)
            o1 = nn(e1, jnp.where(lo_b, one, vp))
            r01 = 1.0 / pltpu.roll(jnp.where(lo, o1, o0), 64, 1)
            mix01 = jnp.where(lo, o0, o1) * r01
            qp, kp, vp = q_all[tr, 128:256], k_all[tr, 128:256], v_all[tr, 128:256]
            e2 = weights(qp, jnp.where(lo_b, kp, zero), 2)
            o2 = nn(e2, jnp.where(lo_b, vp, one))
            r2 = 1.0 / jnp.where(lo, pltpu.roll(o2, 64, 1), 1.0)
            mix2 = jnp.where(lo, o2 * r2, 0.0)
            dst = rows_at(c * 512 + r * SEQ, SEQ)
            mixv[g, dst, 0:128] = mix01.astype(BF16)
            mixv[g, dst, 128:256] = mix2.astype(BF16)
            stq[slot, 3, tr, 0:128] = r01.astype(BF16)
            stq[slot, 3, tr, 128:256] = r2.astype(BF16)
        for copy in stage_copies(slot, u):
            copy.start()
        return carry

    lax.fori_loop(0, 4 * chunks, attend, 0)
    s2(7)
    s1(8)
    for slot in range(2):
        for copy in stage_copies(slot, slot):
            copy.wait()
    save_n1.wait()
    save_mixed = pltpu.make_async_copy(mixv, mixed_hbm, out_sem.at[0])
    save_mixed.start()
    save_wa = pltpu.make_async_copy(W.at[:, pl.ds(0, 768)], waf_hbm, out_sem.at[1])
    save_wa.start()

    def project(c, carry):
        tok = rows_at(c * 512, 512)
        total = nn(mixv[0, tok, 0:192], W[0, 576:768])
        for g in range(1, MP):
            total = total + nn(mixv[g, tok, 0:192], W[g, 576:768])
        hidden = xv[tok].astype(F32) + total + b_out
        acc[tok] = hidden
        normal, inverse = norm_parts(hidden)
        xv[tok] = normal.astype(BF16)
        rstd[tok] = inverse
        n1v[tok] = (normal * gain_two + shift_two).astype(BF16)
        gn2[tok] = jnp.zeros((512, 768), F32)
        return carry

    lax.fori_loop(0, chunks, project, 0)
    s3(7)
    s2(8)
    gwu[...] = jnp.zeros_like(gwu)
    gwd[...] = jnp.zeros_like(gwd)

    def feed(j, carry):
        g, c = j // 4, j % 4

        @pl.when((c == 0) & (g != z))
        def _():
            k = g - jnp.where(g > z, 1, 0)
            fin(3 + 2 * k)
            fin(4 + 2 * k)

        @pl.when(j == 1)
        def _():
            s3(8)

        tok = rows_at(c * 512, 512)
        n2c = n1v[tok]
        glc = glv[tok]
        acts, lows, sums = [], [], []
        for n in range(3):
            cols = slice(n * 256, n * 256 + 256)
            pre = nn(n2c, W[g, 768:1536, cols]) + BP[g, 0:1, cols]
            grad_act = nt(glc, W[g, 1536 + n * 256 : 1792 + n * 256])
            square = pre * pre
            t = jnp.tanh(pre * (GELU_C + (GELU_C * GELU_A) * square))
            half = 0.5 + 0.5 * t
            slope = half + pre * (0.5 - 0.5 * (t * t)) * (GELU_C + (3.0 * GELU_C * GELU_A) * square)
            grad_pre = grad_act * slope
            acts.append((pre * half).astype(BF16))
            lows.append(grad_pre.astype(BF16))
            sums.append(jnp.sum(grad_pre, axis=0, keepdims=True))
        act = jnp.concatenate(acts, axis=1)
        low = jnp.concatenate(lows, axis=1)
        acc[tok] += nn(act, W[g, 1536:2304])
        gn2[tok] += nt(low, W[g, 768:1536])

        @pl.when(g == z)
        def _():
            gwu[...] += tn(n2c, low)
            gwd[...] += tn(act, glc)
            for n in range(3):
                small[1:2, n * 256 : n * 256 + 256] += sums[n]

        return carry

    lax.fori_loop(0, MP * chunks, feed, 0)
    gw_ref[0:768] = gwu[...].astype(BF16)
    gw_ref[768:1536] = gwd[...].astype(BF16)

    def close(r, carry):
        tok = rows_at(r * SEQ, SEQ)
        normal = xv[tok].astype(F32)
        xv[tok] = (acc[tok] + b_down).astype(BF16)
        grad = gn2[tok]
        small[2:3] += jnp.sum(grad * normal, axis=0, keepdims=True)
        small[3:4] += jnp.sum(grad, axis=0, keepdims=True)
        total = glv[tok].astype(F32) + norm_back(grad, normal, rstd[tok], gain_two)
        small[4:5] += jnp.sum(total, axis=0, keepdims=True)
        gn2[tok] = total
        return carry

    lax.fori_loop(0, rows, close, 0)
    save_out = pltpu.make_async_copy(xv, out_hbm, out_sem.at[2])
    save_out.start()
    save_gres = pltpu.make_async_copy(gn2, gres_hbm, out_sem.at[3])
    save_gres.start()
    for copy in zcopies:
        copy.wait_send()
    for t in range(9):
        hop(t, 1, p, (a, z)).wait_send()
        hop(t, 2, p, (b, z)).wait_send()
        hop(t, 3, p, (fc, z)).wait_send()
        hop(t, 4, pa, (b, z)).wait_send()
        hop(t, 5, pa, (fc, z)).wait_send()
        hop(t, 6, pb, (fc, z)).wait_send()
        hop(t, 7, pd, (fc, z)).wait_send()
    save_mixed.wait()
    save_wa.wait()
    save_out.wait()
    save_gres.wait()


def backward_kernel(
    count, extra,
    qkvr_hbm, e_hbm, n1_hbm, mixed_hbm, gres_hbm, x_hbm, waf_hbm, gw_hbm, small_in, vec,
    ig_hbm, gw_out, ga_out, small,
    WA, n1v, mixv, gresv, xv, dqkv, stq, ste,
    cur_w, ag_w, rec_w, cur_a, ag_a, rec_a, ga, small_rec,
    load_sem, stage_sem, out_sem, rs_send, rs_recv, ag_send, ag_recv, sm_send, sm_recv,
):
    d, z, p, kb, fc, a, b, bit_a, bit_b = places()
    chunks = count // 512
    rows = count // SEQ
    me = (d, z)

    loads = [
        pltpu.make_async_copy(gw_hbm, cur_w, load_sem.at[0]),
        pltpu.make_async_copy(waf_hbm, WA, load_sem.at[1]),
        pltpu.make_async_copy(gres_hbm, gresv, load_sem.at[2]),
        pltpu.make_async_copy(mixed_hbm, mixv, load_sem.at[3]),
        pltpu.make_async_copy(n1_hbm, n1v, load_sem.at[4]),
        pltpu.make_async_copy(x_hbm, xv, load_sem.at[5]),
    ]

    def unit_of(i):
        return xor4(z, i // 4) * 4 + i % 4

    def fetch(i, slot):
        u = unit_of(i)
        return (
            pltpu.make_async_copy(qkvr_hbm.at[u], stq.at[slot], stage_sem.at[0, slot]),
            pltpu.make_async_copy(e_hbm.at[u], ste.at[slot], stage_sem.at[1, slot]),
        )

    for copy in fetch(0, 0):
        copy.start()
    for copy in loads:
        copy.start()

    partners = [fc, a, b]
    bits = [kb, bit_a, bit_b]
    for m in range(extra):
        step = 8 << m
        partners.append(d + step * (1 - 2 * ((d // step) % 2)))
    barrier = pltpu.get_barrier_semaphore()
    for peer in partners:
        pl.semaphore_signal(barrier, inc=1, device_id=(peer, z), device_id_type=MESH)
    pl.semaphore_wait(barrier, len(partners))

    def remote(src, dst, ss, rs, to):
        return pltpu.make_async_remote_copy(
            src_ref=src, dst_ref=dst, send_sem=ss, recv_sem=rs, device_id=to, device_id_type=MESH
        )

    class Reduce:
        def __init__(self, which, height, cur, ag, rec):
            self.which, self.cur, self.ag, self.rec = which, cur, ag, rec
            self.half = [height // 2, height // 4, height // 8]
            self.off = [0]
            for k in range(3):
                self.off.append(self.off[k] + bits[k] * self.half[k])
            self.place = [0, self.half[0], self.half[0] + self.half[1]]

        def at(self, ref, start, size):
            if isinstance(start, int):
                return ref.at[pl.ds(start, size)]
            return ref.at[pl.ds(pl.multiple_of(start, 32), size)]

        def rs(self, k):
            theirs = self.off[k] + (1 - bits[k]) * self.half[k]
            return remote(
                self.at(self.cur, theirs, self.half[k]),
                self.at(self.rec, self.place[k], self.half[k]),
                rs_send.at[self.which, k], rs_recv.at[self.which, k], (partners[k], z),
            )

        def send(self, k):
            self.rs(k).start()

        def add(self, start, place, size):
            for q in range(size // 96):
                mine = pl.ds(pl.multiple_of(start + q * 96, 32), 96)
                other = self.rec[place + q * 96 : place + q * 96 + 96]
                self.cur[mine] = (self.cur[mine].astype(F32) + other.astype(F32)).astype(BF16)

        def take(self, k):
            self.rs(k).wait_recv()
            self.add(self.off[k + 1], self.place[k], self.half[k])

        def middle(self):
            size = self.half[2]
            block = self.at(self.cur, self.off[3], size)
            for m in range(extra):
                place = self.place[2] + size * (m + 1)
                copy = remote(
                    block, self.at(self.rec, place, size),
                    rs_send.at[self.which, 3 + m], rs_recv.at[self.which, 3 + m], (partners[3 + m], z),
                )
                copy.start()
                copy.wait()
                self.add(self.off[3], place, size)
            mine = pl.ds(pl.multiple_of(self.off[3], 32), size)
            self.ag[mine] = self.cur[mine]

        def gather(self, k, start):
            part = self.at(self.ag, start, self.half[k])
            return remote(part, part, ag_send.at[self.which, k], ag_recv.at[self.which, k], (partners[k], z))

        def give(self, k):
            self.gather(k, self.off[k + 1]).start()

        def get(self, k):
            self.gather(k, self.off[k] + (1 - bits[k]) * self.half[k]).wait_recv()

        def drain(self):
            for k in range(3):
                self.rs(k).wait_send()
                self.gather(k, self.off[k + 1]).wait_send()

    big = Reduce(0, 1536, cur_w, ag_w, rec_w)
    att = Reduce(1, 768, cur_a, ag_a, rec_a)

    loads[0].wait()
    big.send(0)
    small[...] = small_in[...]
    gain_one = vec[0:1]
    lo = lax.broadcasted_iota(jnp.int32, (SEQ, 128), 1) < HD
    ga[...] = jnp.zeros_like(ga)
    spread = (
        lax.broadcasted_iota(jnp.int32, (192, 384), 0) // HD
        == lax.broadcasted_iota(jnp.int32, (192, 384), 1) // 128
    ).astype(F32).astype(BF16)
    for copy in loads[1:]:
        copy.wait()

    def own_ready():
        n1c = n1v[...]
        for c in range(3):
            ga[c * 192 : c * 192 + 192] += tn(dqkv[c, z, :, 0:192], n1c)
        cur_a[...] = ga[...].astype(BF16)
        att.send(0)

    def both(*steps):
        def run():
            for step in steps:
                step()
        return run

    plan = {
        2: lambda: (big.take(0), big.send(1)),
        4: own_ready,
        5: lambda: (big.take(1), big.send(2)),
        7: lambda: (big.take(2), big.middle(), big.give(2), att.take(0), att.send(1)),
        9: lambda: (big.get(2), big.give(1)),
        10: lambda: (att.take(1), att.send(2)),
        12: lambda: (big.get(1), big.give(0), att.take(2), att.middle(), att.give(2)),
        14: lambda: (att.get(2), att.give(1)),
    }

    def unit(i, carry):
        for when, action in plan.items():
            @pl.when(i == when)
            def _():
                action()

        slot = i % 2
        for copy in fetch(i, slot):
            copy.wait()

        @pl.when(i + 1 < 4 * chunks)
        def _():
            for copy in fetch(i + 1, 1 - slot):
                copy.start()

        g, c = xor4(z, i // 4), i % 4
        tok = rows_at(c * 512, 512)
        low = gresv[tok].astype(BF16)
        mixed = mixv[g, tok, 0:192]
        grad_mixed = nt(low, WA[g, 576:768]).astype(BF16).astype(F32)

        @pl.when(i < 4)
        def _():
            ga[576:768] += tn(mixed, low)

        scaled = (grad_mixed * stq[slot, 3, :, 0:192].astype(F32)).astype(BF16)
        delta = nn((scaled.astype(F32) * mixed.astype(F32)).astype(BF16), spread)
        zero = jnp.zeros((SEQ, 128), BF16)
        for r in range(2):
            tr = slice(r * SEQ, r * SEQ + SEQ)
            dst = rows_at(c * 512 + r * SEQ, SEQ)
            vp, qp, kp = (stq[slot, n, tr, 0:128] for n in range(3))
            dp = scaled[tr, 0:128]
            res = []
            for h in range(2):
                e = ste[slot, r * 3 + h]
                mine = jnp.where(lo, vp, zero) if h == 0 else jnp.where(lo, zero, vp)
                dh = delta[tr, h * 128 : h * 128 + 128]
                grad = nt(dp, mine) - jnp.concatenate([dh, dh], axis=1)
                ds = (e.astype(F32) * grad).astype(BF16)
                res.append((tn(e, dp), nn(ds, kp), tn(ds, qp)))
            pairs = [jnp.where(lo, x0, x1) for x0, x1 in zip(res[0], res[1])]
            dv, dq, dk = pairs[0], pairs[1] * 0.125, pairs[2]
            for n, value in enumerate((dv, dq, dk)):
                dqkv[n, g, dst, 0:128] = value.astype(BF16)

            v2, q2, k2 = (stq[slot, n, tr, 128:192] for n in range(3))
            d2 = scaled[tr, 128:192]
            e = ste[slot, r * 3 + 2]
            dh = delta[tr, 256:384]
            ds = (e.astype(F32) * (nt(d2, v2) - jnp.concatenate([dh, dh], axis=1))).astype(BF16)
            dv2, dq2, dk2 = tn(e, d2), nn(ds, k2) * 0.125, tn(ds, q2)
            for n, value in enumerate((dv2, dq2, dk2)):
                dqkv[n, g, dst, 128:192] = value.astype(BF16)

            @pl.when(i < 4)
            def _():
                small[6:7, 0:128] += jnp.sum(dq, axis=0, keepdims=True)
                small[6:7, 128:192] += jnp.sum(dq2, axis=0, keepdims=True)
                small[7:8, 0:128] += jnp.sum(dv, axis=0, keepdims=True)
                small[7:8, 128:192] += jnp.sum(dv2, axis=0, keepdims=True)

        return carry

    lax.fori_loop(0, 4 * chunks, unit, 0)
    big.get(0)
    att.get(1)
    att.give(0)
    save_w = pltpu.make_async_copy(ag_w, gw_out, out_sem.at[0])
    save_w.start()

    def last(c, carry):
        tok = rows_at(c * 512, 512)
        total = nn(dqkv[0, 0, tok, 0:192], WA[0, 0:192])
        for g in range(MP):
            for n in range(3):
                if g + n > 0:
                    total = total + nn(dqkv[n, g, tok, 0:192], WA[g, n * 192 : n * 192 + 192])
        normal, inverse = norm_parts(xv[tok].astype(F32))
        small[5:6] += jnp.sum(total * normal, axis=0, keepdims=True)
        small[8:9] += jnp.sum(total, axis=0, keepdims=True)
        xv[tok] = (gresv[tok] + norm_back(total, normal, inverse, gain_one)).astype(BF16)
        return carry

    lax.fori_loop(0, chunks, last, 0)
    save_x = pltpu.make_async_copy(xv, ig_hbm, out_sem.at[1])
    save_x.start()

    for k, peer in enumerate(partners):
        copy = remote(small, small_rec.at[k], sm_send.at[k], sm_recv.at[k], (peer, z))
        copy.start()
        copy.wait()
        small[...] += small_rec[k]
    att.get(0)
    save_a = pltpu.make_async_copy(ag_a, ga_out, out_sem.at[2])
    save_a.start()
    big.drain()
    att.drain()
    save_w.wait()
    save_x.wait()
    save_a.wait()


def layer(n_dp, tokens, segment_ids, cotangent, w_qkv, b_qv, w_out, b_out, gain_one, shift_one, w_up, b_up, w_down, b_down, gain_two, shift_two):
    count, width = tokens.shape[0], w_qkv.shape[2]
    rows = segment_ids.shape[0]
    units = MP * (count // 512)
    extra = (n_dp // 8).bit_length() - 1
    any_space = pl.BlockSpec(memory_space=pl.ANY)
    in_vmem = pl.BlockSpec(memory_space=pltpu.VMEM)
    wt = jnp.transpose(w_qkv, (0, 2, 1))
    wa = jnp.concatenate([wt[2], wt[0], wt[1], w_out], axis=0)
    bp = jnp.zeros((8, 768), F32)
    bp = bp.at[0].set(b_up).at[1, :width].set(b_qv[0]).at[2, :width].set(b_qv[1])
    zero_row = jnp.zeros_like(b_out)
    vec = jnp.stack([gain_one, shift_one, b_out, gain_two, shift_two, b_down, zero_row, zero_row])
    seg = segment_ids.astype(F32)
    dma = pltpu.SemaphoreType.DMA

    def sds(shape, dtype):
        return jax.ShapeDtypeStruct(shape, dtype)

    def fwd(*refs):
        return forward_kernel(count, *refs)

    block_out, qkvr, e, n1, mixed, gres, waf, gw, small = pl.pallas_call(
        fwd,
        name="forward",
        out_shape=(
            sds((count, 768), BF16),
            sds((units, 4, 512, 256), BF16),
            sds((units, 6, SEQ, SEQ), BF16),
            sds((count, 768), BF16),
            sds((MP, count, 256), BF16),
            sds((count, 768), F32),
            sds((MP, 768, 768), BF16),
            sds((1536, 768), BF16),
            sds((16, 768), F32),
        ),
        in_specs=[any_space, any_space, in_vmem, any_space, any_space, any_space, any_space, in_vmem],
        out_specs=(any_space,) * 7 + (in_vmem, in_vmem),
        scratch_shapes=[
            pltpu.VMEM((MP, 2304, 768), BF16),
            pltpu.VMEM((MP, 8, 768), F32),
            pltpu.VMEM((count, 768), BF16),
            pltpu.VMEM((count, 768), BF16),
            pltpu.VMEM((count, 768), BF16),
            pltpu.VMEM((MP, count, 256), BF16),
            pltpu.VMEM((count, 768), F32),
            pltpu.VMEM((count, 768), F32),
            pltpu.VMEM((rows, SEQ, SEQ), F32),
            pltpu.VMEM((count, 1), F32),
            pltpu.VMEM((768, 768), F32),
            pltpu.VMEM((768, 768), F32),
            pltpu.VMEM((2, 4, 512, 256), BF16),
            pltpu.VMEM((2, 6, SEQ, SEQ), BF16),
            dma((2, count // 512)), dma((4,)), dma((2, 2)), dma((4,)),
            dma((9,)), dma((9, 8)), dma((9, 8)), dma((3,)), dma((3,)),
        ],
        compiler_params=pltpu.CompilerParams(collective_id=0, has_side_effects=True, vmem_limit_bytes=VMEM_LIMIT),
    )(tokens, cotangent, seg, wa, w_up, w_down, bp, vec)

    def bwd(*refs):
        return backward_kernel(count, extra, *refs)

    input_grad, gw_full, ga_full, small = pl.pallas_call(
        bwd,
        name="backward",
        out_shape=(
            sds((count, 768), BF16),
            sds((1536, 768), BF16),
            sds((768, 768), BF16),
            sds((16, 768), F32),
        ),
        in_specs=[any_space] * 8 + [in_vmem, in_vmem],
        out_specs=(any_space,) * 3 + (in_vmem,),
        scratch_shapes=[
            pltpu.VMEM((MP, 768, 768), BF16),
            pltpu.VMEM((count, 768), BF16),
            pltpu.VMEM((MP, count, 256), BF16),
            pltpu.VMEM((count, 768), F32),
            pltpu.VMEM((count, 768), BF16),
            pltpu.VMEM((3, MP, count, 256), BF16),
            pltpu.VMEM((2, 4, 512, 256), BF16),
            pltpu.VMEM((2, 6, SEQ, SEQ), BF16),
            pltpu.VMEM((1536, 768), BF16),
            pltpu.VMEM((1536, 768), BF16),
            pltpu.VMEM((1344 + 192 * extra, 768), BF16),
            pltpu.VMEM((768, 768), BF16),
            pltpu.VMEM((768, 768), BF16),
            pltpu.VMEM((672 + 96 * extra, 768), BF16),
            pltpu.VMEM((768, 768), F32),
            pltpu.VMEM((3 + extra, 16, 768), F32),
            dma((6,)), dma((2, 2)), dma((3,)),
            dma((2, 3 + extra)), dma((2, 3 + extra)), dma((2, 3)), dma((2, 3)),
            dma((3 + extra,)), dma((3 + extra,)),
        ],
        compiler_params=pltpu.CompilerParams(collective_id=1, has_side_effects=True, vmem_limit_bytes=VMEM_LIMIT),
    )(qkvr, e, n1, mixed, gres, tokens, waf, gw, small, vec)

    gw_full = gw_full.astype(F32)
    ga_full = ga_full.astype(F32)
    grad_qkv = jnp.transpose(jnp.stack([ga_full[192:384], ga_full[384:576], ga_full[0:192]]), (0, 2, 1))
    return (
        block_out,
        input_grad,
        grad_qkv,
        small[6:8, :width],
        ga_full[576:768],
        small[4],
        small[5],
        small[8],
        gw_full[0:768],
        small[1],
        gw_full[768:1536],
        small[0],
        small[2],
        small[3],
    )


def solution(mesh):
    n_dp = mesh.shape["dp"]

    def run(*args):
        return layer(n_dp, *args)

    placed = (
        P("dp", None), P("dp", None), P("dp", None), P(None, None, "mp"), P(None, "mp"), P("mp", None), P(), P(), P(),
        P(None, "mp"), P("mp"), P("mp", None), P(), P(), P(),
    )
    return jax.shard_map(
        run,
        mesh=mesh,
        in_specs=placed,
        out_specs=(
            P("dp", None), P("dp", None), P(None, None, "mp"), P(None, "mp"), P("mp", None), P(), P(), P(),
            P(None, "mp"), P("mp"), P("mp", None), P(), P(), P(),
        ),
        check_vma=False,
    )
```

```python
import jax
import jax.numpy as jnp
from jax import lax
from jax.experimental import pallas as pl
from jax.experimental.pallas import tpu as pltpu
from jax.sharding import PartitionSpec as P

HD = 64
SEQ = 256
EPS = 1e-06
MASKED = -1000000000.0
MESH = pl.DeviceIdType.MESH
F32 = jnp.float32
BF16 = jnp.bfloat16
MP = 4
GELU_C = 0.7978845608028654
GELU_A = 0.044715
VMEM_LIMIT = 66_000_000


def nn(a, b):
    return lax.dot_general(a, b, (((1,), (0,)), ((), ())), preferred_element_type=F32)


def nt(a, b):
    return lax.dot_general(a, b, (((1,), (1,)), ((), ())), preferred_element_type=F32)


def tn(a, b):
    return lax.dot_general(a, b, (((0,), (0,)), ((), ())), preferred_element_type=F32)


def xor4(a, b):
    return (a % 2 + b % 2) % 2 + 2 * ((a // 2 + b // 2) % 2)


def places():
    d = lax.axis_index("dp")
    z = lax.axis_index("mp")
    p = d % 8
    kb, xb, yb = p % 2, (p // 2) % 2, (p // 4) % 2
    fc = d + (1 - 2 * kb)
    fx = d + 2 * (1 - 2 * xb)
    fy = d + 4 * (1 - 2 * yb)
    a = fx * (1 - kb) + fy * kb
    b = fy * (1 - kb) + fx * kb
    bit_a = xb * (1 - kb) + yb * kb
    bit_b = yb * (1 - kb) + xb * kb
    return d, z, p, kb, fc, a, b, bit_a, bit_b


def rows_at(start, size):
    return pl.ds(pl.multiple_of(start, size), size)


def norm_parts(h):
    centre = h - jnp.mean(h, axis=-1, keepdims=True)
    inverse = lax.rsqrt(jnp.mean(centre * centre, axis=-1, keepdims=True) + EPS)
    return centre * inverse, inverse


def norm_back(grad, normal, inverse, gain):
    scaled = grad * gain
    return inverse * (
        scaled
        - jnp.mean(scaled, axis=-1, keepdims=True)
        - normal * jnp.mean(scaled * normal, axis=-1, keepdims=True)
    )


def forward_kernel(
    count,
    x_hbm, cot_hbm, seg, wqkv_hbm, wo_hbm, wu_hbm, wd_hbm, bu_hbm, bqv, g1, s1_ref, bo, g2, s2_ref, bd,
    out_hbm, qkvr_hbm, e_hbm, n1_hbm, mixed_hbm, gres_hbm, waf_hbm, gw_ref, small,
    W, BQ, BU, xv, glv, n1v, mixv, acc, gn2, bias, rstd, gwu, gwd, stq, ste,
    load_sem, own_sem, stage_sem, out_sem, zsend, send, recv, bsend, brecv,
):
    d, z, p, kb, fc, a, b, bit_a, bit_b = places()
    chunks = count // 512
    rows = count // SEQ

    loads = []
    for c in range(chunks):
        part = pl.ds(c * 512, 512)
        loads.append((
            pltpu.make_async_copy(x_hbm.at[part], xv.at[part], load_sem.at[0, c]),
            pltpu.make_async_copy(cot_hbm.at[part], glv.at[part], load_sem.at[1, c]),
        ))
        loads[-1][0].start()
        loads[-1][1].start()
    own = [
        pltpu.make_async_copy(wqkv_hbm.at[2], W.at[z, pl.ds(0, 192)], own_sem.at[0]),
        pltpu.make_async_copy(wqkv_hbm.at[0], W.at[z, pl.ds(192, 192)], own_sem.at[1]),
        pltpu.make_async_copy(wqkv_hbm.at[1], W.at[z, pl.ds(384, 192)], own_sem.at[2]),
        pltpu.make_async_copy(wo_hbm, W.at[z, pl.ds(576, 192)], own_sem.at[3]),
        pltpu.make_async_copy(bu_hbm, BU.at[z, 0], own_sem.at[4]),
        pltpu.make_async_copy(wu_hbm, W.at[z, pl.ds(768, 768)], own_sem.at[5]),
        pltpu.make_async_copy(wd_hbm, W.at[z, pl.ds(1536, 768)], own_sem.at[6]),
    ]
    for copy in own:
        copy.start()
    BQ[z] = jnp.zeros((2, 256), F32)
    BQ[z, :, 0:192] = bqv[...]

    peers = [(d, xor4(z, s)) for s in (1, 2, 3)] + [(fc, z), (a, z), (b, z)]
    barrier = pltpu.get_barrier_semaphore()
    for peer in peers:
        pl.semaphore_signal(barrier, inc=1, device_id=peer, device_id_type=MESH)
    pl.semaphore_wait(barrier, len(peers))
    for copy in own:
        copy.wait()

    def remote(src, dst, ss, rs, to):
        return pltpu.make_async_remote_copy(
            src_ref=src, dst_ref=dst, send_sem=ss, recv_sem=rs, device_id=to, device_id_type=MESH
        )

    def piece_rows(base, which):
        return pl.ds(pl.multiple_of(base + 96 * which, 96), 96)

    zcopies = []
    for s in (1, 2, 3):
        to = (d, xor4(z, s))
        zcopies.append(remote(BQ.at[z], BQ.at[z], bsend.at[s - 1], brecv.at[s - 1], to))
        zcopies.append(remote(BU.at[z], BU.at[z], bsend.at[s + 2], brecv.at[s + 2], to))
        part = W.at[z, piece_rows(0, p)]
        zcopies.append(remote(part, part, zsend.at[s - 1], recv.at[s - 1, 0], to))
    for k in range(3):
        there = k + jnp.where(z <= k, 1, 0)
        order = z - jnp.where(z > there, 1, 0)
        for h in range(2):
            part = W.at[z, piece_rows(768 * (h + 1), p)]
            zcopies.append(remote(
                part,
                part,
                zsend.at[3 + 2 * k + h],
                recv.at[3 + 2 * order + h, 0],
                (d, there),
            ))
    for copy in zcopies:
        copy.start()

    def step_of(t):
        late = jnp.maximum(t - 3, 0)
        k = late // 2
        g = jnp.where(t < 3, xor4(z, t + 1), k + jnp.where(k >= z, 1, 0))
        return g, jnp.where(t < 3, 0, 768 + 768 * (late % 2))

    def hop(t, index, which, to):
        g, base = step_of(t)
        part = W.at[g, piece_rows(base, which)]
        return remote(part, part, send.at[t, index], recv.at[t, index], to)

    pa, pb, pc = a % 8, b % 8, fc % 8
    pd = (a + b - d) % 8
    me = (d, z)

    def s1(t):
        hop(t, 0, p, me).wait_recv()
        hop(t, 1, p, (a, z)).start()
        hop(t, 2, p, (b, z)).start()
        hop(t, 3, p, (fc, z)).start()

    def s2(t):
        hop(t, 1, pa, me).wait_recv()
        hop(t, 4, pa, (b, z)).start()
        hop(t, 5, pa, (fc, z)).start()
        hop(t, 2, pb, me).wait_recv()
        hop(t, 6, pb, (fc, z)).start()

    def s3(t):
        hop(t, 4, pd, me).wait_recv()
        hop(t, 7, pd, (fc, z)).start()

    def core_flip(q):
        return q + 1 - 2 * (q % 2)

    def fin(t):
        hop(t, 3, core_flip(p), me).wait_recv()
        hop(t, 5, core_flip(pb), me).wait_recv()
        hop(t, 6, core_flip(pa), me).wait_recv()
        hop(t, 7, core_flip(pd), me).wait_recv()

    small[...] = jnp.zeros_like(small)
    gain_one, shift_one, b_out, gain_two, shift_two, b_down = (
        ref[...].reshape(1, 768) for ref in (g1, s1_ref, bo, g2, s2_ref, bd)
    )

    def head(r, carry):
        part = rows_at(r * SEQ, SEQ)
        normal, inverse = norm_parts(xv[part].astype(F32))
        n1v[part] = (normal * gain_one + shift_one).astype(BF16)
        seg_row = seg[pl.ds(r, 1)].astype(F32)
        seg_col = jnp.broadcast_to(seg_row, (128, SEQ)).T
        for half in range(2):
            lanes = slice(half * 128, half * 128 + 128)
            bias[r, :, lanes] = jnp.where(seg_col == seg_row[:, lanes], 0.0, MASKED)
        for part6 in range(6):
            lanes = slice(part6 * 128, part6 * 128 + 128)
            masked = jnp.where(seg_col != 0.0, glv[part, lanes].astype(F32), 0.0)
            small[0:1, lanes] += jnp.sum(masked, axis=0, keepdims=True)
            glv[part, lanes] = masked.astype(BF16)
        return carry

    for pair in loads:
        pair[0].wait()
        pair[1].wait()
    lax.fori_loop(0, rows, head, 0)
    save_n1 = pltpu.make_async_copy(n1v, n1_hbm, out_sem.at[0, 0])
    save_n1.start()

    lo = lax.broadcasted_iota(jnp.int32, (SEQ, 128), 1) < HD
    lo_b = lo

    def stage_copies(slot, u):
        return (
            pltpu.make_async_copy(stq.at[slot], qkvr_hbm.at[u], stage_sem.at[0, slot]),
            pltpu.make_async_copy(ste.at[slot], e_hbm.at[u], stage_sem.at[1, slot]),
        )

    plan = (
        (s2, (3, 5, 6, 9, 10, 13, 14)),
        (s3, (4, 6, 7, 10, 11, 14, 15)),
        (fin, (4, 8, 12)),
        (s1, (2, 3, 4, 7, 8, 11, 12, 15)),
    )

    def attend(i, carry):
        for action, whens in plan:
            def act(t, carry):
                action(t)
                return carry

            first = sum(jnp.where(i > when, 1, 0) for when in whens)
            lax.fori_loop(first, sum(jnp.where(i >= when, 1, 0) for when in whens), act, 0)

        @pl.when((i >= 4) & (i % 4 == 0))
        def _():
            there = i // 4
            for ref, first in ((BQ, -1), (BU, 2)):
                block = ref.at[xor4(z, there)]
                remote(block, block, bsend.at[first + there], brecv.at[first + there], me).wait_recv()

        s, c = i // 4, i % 4
        g = xor4(z, s)
        slot = i % 2
        u = g * 4 + c
        tok = rows_at(c * 512, 512)

        @pl.when(i >= 2)
        def _():
            for copy in stage_copies(slot, u):
                copy.wait()

        n1c = n1v[tok]
        v_all = (nt(n1c, W[g, 0:256]) + BQ[g, 1:2]).astype(BF16)
        q_all = ((nt(n1c, W[g, 192:448]) + BQ[g, 0:1]) * 0.125).astype(BF16)
        k_all = nt(n1c, W[g, 384:640]).astype(BF16)
        stq[slot, 0] = v_all
        stq[slot, 1] = q_all
        stq[slot, 2] = k_all
        one = jnp.ones((SEQ, 128), BF16)
        zero = jnp.zeros((SEQ, 128), BF16)
        for r in range(2):
            tr = slice(r * SEQ, r * SEQ + SEQ)
            mask = bias[c * 2 + r]

            def weights(qp, kp, h):
                sc = nt(qp, kp) + mask
                e = jnp.exp(sc - jnp.max(sc, axis=-1, keepdims=True)).astype(BF16)
                ste[slot, r * 3 + h] = e
                return e

            qp, kp, vp = q_all[tr, 0:128], k_all[tr, 0:128], v_all[tr, 0:128]
            e0 = weights(qp, jnp.where(lo_b, kp, zero), 0)
            o0 = nn(e0, jnp.where(lo_b, vp, one))
            e1 = weights(qp, jnp.where(lo_b, zero, kp), 1)
            o1 = nn(e1, jnp.where(lo_b, one, vp))
            r01 = 1.0 / pltpu.roll(jnp.where(lo, o1, o0), 64, 1)
            mix01 = jnp.where(lo, o0, o1) * r01
            qp, kp, vp = q_all[tr, 128:256], k_all[tr, 128:256], v_all[tr, 128:256]
            e2 = weights(qp, jnp.where(lo_b, kp, zero), 2)
            o2 = nn(e2, jnp.where(lo_b, vp, one))
            r2 = 1.0 / jnp.where(lo, pltpu.roll(o2, 64, 1), 1.0)
            mix2 = jnp.where(lo, o2 * r2, 0.0)
            dst = rows_at(c * 512 + r * SEQ, SEQ)
            mixv[g, dst, 0:128] = mix01.astype(BF16)
            mixv[g, dst, 128:256] = mix2.astype(BF16)
            stq[slot, 3, tr, 0:128] = r01.astype(BF16)
            stq[slot, 3, tr, 128:256] = r2.astype(BF16)
        for copy in stage_copies(slot, u):
            copy.start()
        return carry

    lax.fori_loop(0, 4 * chunks, attend, 0)
    s2(7)
    s1(8)
    for slot in range(2):
        for copy in stage_copies(slot, slot):
            copy.wait()
    save_n1.wait()
    save_mixed = pltpu.make_async_copy(mixv, mixed_hbm, out_sem.at[0, 0])
    save_mixed.start()
    save_wa = pltpu.make_async_copy(W.at[:, pl.ds(0, 768)], waf_hbm, out_sem.at[1, 0])
    save_wa.start()

    def project(c, carry):
        tok = rows_at(c * 512, 512)
        total = nn(mixv[0, tok, 0:192], W[0, 576:768])
        for g in range(1, MP):
            total = total + nn(mixv[g, tok, 0:192], W[g, 576:768])
        hidden = xv[tok].astype(F32) + total + b_out
        acc[tok] = hidden
        normal, inverse = norm_parts(hidden)
        xv[tok] = normal.astype(BF16)
        rstd[tok] = inverse
        n1v[tok] = (normal * gain_two + shift_two).astype(BF16)
        gn2[tok] = jnp.zeros((512, 768), F32)
        return carry

    lax.fori_loop(0, chunks, project, 0)
    s3(7)
    s2(8)
    gwu[...] = jnp.zeros_like(gwu)
    gwd[...] = jnp.zeros_like(gwd)

    def feed(j, carry):
        g, c = j // 4, j % 4

        @pl.when((c == 0) & (g != z))
        def _():
            k = g - jnp.where(g > z, 1, 0)
            fin(3 + 2 * k)
            fin(4 + 2 * k)

        @pl.when(j == 1)
        def _():
            s3(8)

        tok = rows_at(c * 512, 512)
        n2c = n1v[tok]
        glc = glv[tok]
        acts, lows, sums = [], [], []
        for n in range(3):
            cols = slice(n * 256, n * 256 + 256)
            pre = nn(n2c, W[g, 768:1536, cols]) + BU[g, 0:1, cols]
            grad_act = nt(glc, W[g, 1536 + n * 256 : 1792 + n * 256])
            square = pre * pre
            t = jnp.tanh(pre * (GELU_C + (GELU_C * GELU_A) * square))
            half = 0.5 + 0.5 * t
            slope = half + pre * (0.5 - 0.5 * (t * t)) * (GELU_C + (3.0 * GELU_C * GELU_A) * square)
            grad_pre = grad_act * slope
            acts.append((pre * half).astype(BF16))
            lows.append(grad_pre.astype(BF16))
            sums.append(jnp.sum(grad_pre, axis=0, keepdims=True))
        act = jnp.concatenate(acts, axis=1)
        low = jnp.concatenate(lows, axis=1)
        acc[tok] += nn(act, W[g, 1536:2304])
        gn2[tok] += nt(low, W[g, 768:1536])

        @pl.when(g == z)
        def _():
            gwu[...] += tn(n2c, low)
            gwd[...] += tn(act, glc)
            for n in range(3):
                small[1:2, n * 256 : n * 256 + 256] += sums[n]

        return carry

    lax.fori_loop(0, MP * chunks, feed, 0)
    gw_ref[0:768] = gwu[...].astype(BF16)
    gw_ref[768:1536] = gwd[...].astype(BF16)

    def closed_copies(r):
        tok = rows_at(r * SEQ, SEQ)
        return (
            pltpu.make_async_copy(xv.at[tok], out_hbm.at[tok], out_sem.at[0, 1 + r]),
            pltpu.make_async_copy(glv.at[tok], gres_hbm.at[tok], out_sem.at[1, 1 + r]),
        )

    def close(r, carry):
        tok = rows_at(r * SEQ, SEQ)
        normal = xv[tok].astype(F32)
        xv[tok] = (acc[tok] + b_down).astype(BF16)
        grad = gn2[tok]
        small[2:3] += jnp.sum(grad * normal, axis=0, keepdims=True)
        small[3:4] += jnp.sum(grad, axis=0, keepdims=True)
        total = glv[tok].astype(F32) + norm_back(grad, normal, rstd[tok], gain_two)
        small[4:5] += jnp.sum(total, axis=0, keepdims=True)
        glv[tok] = total.astype(BF16)
        for copy in closed_copies(r):
            copy.start()
        return carry

    lax.fori_loop(0, rows, close, 0)
    for copy in zcopies:
        copy.wait_send()
    for t in range(9):
        hop(t, 1, p, (a, z)).wait_send()
        hop(t, 2, p, (b, z)).wait_send()
        hop(t, 3, p, (fc, z)).wait_send()
        hop(t, 4, pa, (b, z)).wait_send()
        hop(t, 5, pa, (fc, z)).wait_send()
        hop(t, 6, pb, (fc, z)).wait_send()
        hop(t, 7, pd, (fc, z)).wait_send()
    save_mixed.wait()
    save_wa.wait()

    def closed(r, carry):
        for copy in closed_copies(r):
            copy.wait()
        return carry

    lax.fori_loop(0, rows, closed, 0)


def backward_kernel(
    count, extra,
    qkvr_hbm, e_hbm, n1_hbm, mixed_hbm, gres_hbm, x_hbm, waf_hbm, gw_hbm, small_in, g1,
    ig_hbm, gw_out, ga_out, small,
    WA, n1v, mixv, gresv, xv, dqkv, stq, ste,
    cur_w, ag_w, rec_w, cur_a, ag_a, rec_a, ga, head, head_rec, tail, tail_rec,
    load_sem, stage_sem, out_sem, rs_send, rs_recv, ag_send, ag_recv, sm_send, sm_recv,
):
    d, z, p, kb, fc, a, b, bit_a, bit_b = places()
    xb, yb = p // 2 % 2, p // 4
    chunks = count // 512

    def load(src, dst, n):
        return pltpu.make_async_copy(src, dst, load_sem.at[n])

    top, rest = pl.ds(0, 512), pl.ds(512, count - 512)
    load_first = [
        load(waf_hbm.at[:, pl.ds(576, 192)], WA.at[:, pl.ds(576, 192)], 0),
        load(gres_hbm.at[top], gresv.at[top], 1),
        load(mixed_hbm.at[z], mixv.at[z], 2),
    ]
    load_grads = load(gw_hbm, cur_w, 3)
    load_next = [load(gres_hbm.at[rest], gresv.at[rest], 4)] + [
        load(mixed_hbm.at[xor4(z, s)], mixv.at[xor4(z, s)], 4 + s) for s in (1, 2, 3)
    ]
    load_n1 = load(n1_hbm, n1v, 8)
    load_last = [
        load(waf_hbm.at[:, pl.ds(0, 576)], WA.at[:, pl.ds(0, 576)], 9),
        load(x_hbm, xv, 10),
    ]

    def unit_of(i):
        return xor4(z, i // 4) * 4 + i % 4

    def fetch(i, slot):
        u = unit_of(i)
        return (
            pltpu.make_async_copy(qkvr_hbm.at[u], stq.at[slot], stage_sem.at[0, slot]),
            pltpu.make_async_copy(e_hbm.at[u], ste.at[slot], stage_sem.at[1, slot]),
        )

    for copy in fetch(0, 0):
        copy.start()
    for copy in load_first + [load_grads] + load_next + [load_n1] + load_last:
        copy.start()

    partners = [fc, a, b]
    bits = [kb, bit_a, bit_b]
    for m in range(extra):
        step = 8 << m
        partners.append(d + step * (1 - 2 * ((d // step) % 2)))
    peers = [
        d - p + (1 - kb if k % 2 else kb) + 2 * (1 - xb if k // 2 % 2 else xb) + 4 * (1 - yb if k // 4 else yb)
        for k in range(1, 8)
    ]
    barrier = pltpu.get_barrier_semaphore()
    for peer in peers + partners[3:]:
        pl.semaphore_signal(barrier, inc=1, device_id=(peer, z), device_id_type=MESH)
    pl.semaphore_wait(barrier, 7 + extra)

    def remote(src, dst, ss, rs, to):
        return pltpu.make_async_remote_copy(
            src_ref=src, dst_ref=dst, send_sem=ss, recv_sem=rs, device_id=to, device_id_type=MESH
        )

    class Reduce:
        def __init__(self, which, height, cur, ag, rec):
            self.which, self.cur, self.ag, self.rec = which, cur, ag, rec
            self.half = [height // 2, height // 4, height // 8]
            self.off = [0]
            for k in range(3):
                self.off.append(self.off[k] + bits[k] * self.half[k])
            self.place = [0, self.half[0], self.half[0] + self.half[1]]

        def at(self, ref, start, size):
            if isinstance(start, int):
                return ref.at[pl.ds(start, size)]
            return ref.at[pl.ds(pl.multiple_of(start, 32), size)]

        def rs(self, k):
            theirs = self.off[k] + (1 - bits[k]) * self.half[k]
            return remote(
                self.at(self.cur, theirs, self.half[k]),
                self.at(self.rec, self.place[k], self.half[k]),
                rs_send.at[self.which, k], rs_recv.at[self.which, k], (partners[k], z),
            )

        def send(self, k):
            self.rs(k).start()

        def add(self, start, place, size):
            for q in range(size // 96):
                mine = pl.ds(pl.multiple_of(start + q * 96, 32), 96)
                other = self.rec[place + q * 96 : place + q * 96 + 96]
                self.cur[mine] = (self.cur[mine].astype(F32) + other.astype(F32)).astype(BF16)

        def take(self, k):
            self.rs(k).wait_recv()
            self.add(self.off[k + 1], self.place[k], self.half[k])

        def middle(self):
            size = self.half[2]
            block = self.at(self.cur, self.off[3], size)
            for m in range(extra):
                place = self.place[2] + size * (m + 1)
                copy = remote(
                    block, self.at(self.rec, place, size),
                    rs_send.at[self.which, 3 + m], rs_recv.at[self.which, 3 + m], (partners[3 + m], z),
                )
                copy.start()
                copy.wait()
                self.add(self.off[3], place, size)
            mine = pl.ds(pl.multiple_of(self.off[3], 32), size)
            self.ag[mine] = self.cur[mine]

        def gather(self, k, start):
            part = self.at(self.ag, start, self.half[k])
            return remote(part, part, ag_send.at[self.which, k], ag_recv.at[self.which, k], (partners[k], z))

        def give(self, k):
            self.gather(k, self.off[k + 1]).start()

        def get(self, k):
            self.gather(k, self.off[k] + (1 - bits[k]) * self.half[k]).wait_recv()

        def drain(self):
            for k in range(3):
                self.rs(k).wait_send()
                self.gather(k, self.off[k + 1]).wait_send()

    big = Reduce(0, 1536, cur_w, ag_w, rec_w)
    att = Reduce(1, 768, cur_a, ag_a, rec_a)

    load_grads.wait()
    big.send(0)
    small[...] = small_in[...]
    tail[...] = jnp.zeros_like(tail)
    gain_one = g1[...].reshape(1, 768)
    lo = lax.broadcasted_iota(jnp.int32, (SEQ, 128), 1) < HD
    ga[...] = jnp.zeros_like(ga)
    spread = (
        lax.broadcasted_iota(jnp.int32, (192, 384), 0) // HD
        == lax.broadcasted_iota(jnp.int32, (192, 384), 1) // 128
    ).astype(F32).astype(BF16)
    for copy in load_first:
        copy.wait()

    def own_ready():
        load_n1.wait()
        n1c = n1v[...]
        for c in range(3):
            ga[c * 192 : c * 192 + 192] += tn(dqkv[c, z, :, 0:192], n1c)
        cur_a[...] = ga[...].astype(BF16)
        att.send(0)

    def next_ready():
        for copy in load_next:
            copy.wait()

    plan = {
        1: next_ready,
        2: lambda: (big.take(0), big.send(1)),
        4: own_ready,
        5: lambda: (big.take(1), big.send(2)),
        7: lambda: (big.take(2), big.middle(), big.give(2), att.take(0), att.send(1)),
        9: lambda: (big.get(2), big.give(1)),
        10: lambda: (att.take(1), att.send(2)),
        12: lambda: (big.get(1), big.give(0), att.take(2), att.middle(), att.give(2)),
        14: lambda: (att.get(2), att.give(1)),
    }

    def unit(i, carry):
        for when, action in plan.items():
            @pl.when(i == when)
            def _():
                action()

        slot = i % 2
        for copy in fetch(i, slot):
            copy.wait()

        @pl.when(i + 1 < 4 * chunks)
        def _():
            for copy in fetch(i + 1, 1 - slot):
                copy.start()

        g, c = xor4(z, i // 4), i % 4
        tok = rows_at(c * 512, 512)
        low = gresv[tok]
        mixed = mixv[g, tok, 0:192]
        grad_mixed = nt(low, WA[g, 576:768]).astype(BF16).astype(F32)

        @pl.when(i < 4)
        def _():
            ga[576:768] += tn(mixed, low)

        scaled = (grad_mixed * stq[slot, 3, :, 0:192].astype(F32)).astype(BF16)
        delta = nn((scaled.astype(F32) * mixed.astype(F32)).astype(BF16), spread)
        zero = jnp.zeros((SEQ, 128), BF16)
        for r in range(2):
            tr = slice(r * SEQ, r * SEQ + SEQ)
            dst = rows_at(c * 512 + r * SEQ, SEQ)
            vp, qp, kp = (stq[slot, n, tr, 0:128] for n in range(3))
            dp = scaled[tr, 0:128]
            res = []
            for h in range(2):
                e = ste[slot, r * 3 + h]
                mine = jnp.where(lo, vp, zero) if h == 0 else jnp.where(lo, zero, vp)
                dh = delta[tr, h * 128 : h * 128 + 128]
                grad = nt(dp, mine) - jnp.concatenate([dh, dh], axis=1)
                ds = (e.astype(F32) * grad).astype(BF16)
                res.append((tn(e, dp), nn(ds, kp), tn(ds, qp)))
            pairs = [jnp.where(lo, x0, x1) for x0, x1 in zip(res[0], res[1])]
            dv, dq, dk = pairs[0], pairs[1] * 0.125, pairs[2]
            for n, value in enumerate((dv, dq, dk)):
                dqkv[n, g, dst, 0:128] = value.astype(BF16)

            v2, q2, k2 = (stq[slot, n, tr, 128:192] for n in range(3))
            d2 = scaled[tr, 128:192]
            e = ste[slot, r * 3 + 2]
            dh = delta[tr, 256:384]
            ds = (e.astype(F32) * (nt(d2, v2) - jnp.concatenate([dh, dh], axis=1))).astype(BF16)
            dv2, dq2, dk2 = tn(e, d2), nn(ds, k2) * 0.125, tn(ds, q2)
            for n, value in enumerate((dv2, dq2, dk2)):
                dqkv[n, g, dst, 128:192] = value.astype(BF16)

            @pl.when(i < 4)
            def _():
                small[6:7, 0:128] += jnp.sum(dq, axis=0, keepdims=True)
                small[6:7, 128:192] += jnp.sum(dq2, axis=0, keepdims=True)
                small[7:8, 0:128] += jnp.sum(dv, axis=0, keepdims=True)
                small[7:8, 128:192] += jnp.sum(dv2, axis=0, keepdims=True)

        return carry

    lax.fori_loop(0, 4 * chunks, unit, 0)
    big.get(0)
    att.get(1)
    att.give(0)
    save_w = pltpu.make_async_copy(ag_w, gw_out, out_sem.at[0])
    save_w.start()

    def exchange(ref, rec, which):
        mine = [remote(ref, rec.at[p], sm_send.at[which, k], sm_recv.at[which, p], (peer, z)) for k, peer in enumerate(peers)]
        for copy in mine:
            copy.start()
        return mine

    def total_of(ref, rec, which, mine):
        for copy in mine:
            copy.wait_send()
        for k, peer in enumerate(peers):
            other = peer - (d - p)
            remote(ref, rec.at[other], sm_send.at[which, k], sm_recv.at[which, other], (peer, z)).wait_recv()
        rec[p] = ref[...]
        ref[...] = sum(rec[k] for k in range(1, 8)) + rec[0]
        for m in range(extra):
            copy = remote(ref, rec.at[8 + m], sm_send.at[which, 7 + m], sm_recv.at[which, 8 + m], (partners[3 + m], z))
            copy.start()
            copy.wait()
            ref[...] += rec[8 + m]

    head[...] = small[0:8]
    sent_head = exchange(head, head_rec, 0)
    for copy in load_last:
        copy.wait()

    def last(c, carry):
        tok = rows_at(c * 512, 512)
        total = nn(dqkv[0, 0, tok, 0:192], WA[0, 0:192])
        for g in range(MP):
            for n in range(3):
                if g + n > 0:
                    total = total + nn(dqkv[n, g, tok, 0:192], WA[g, n * 192 : n * 192 + 192])
        normal, inverse = norm_parts(xv[tok].astype(F32))
        tail[0:1] += jnp.sum(total * normal, axis=0, keepdims=True)
        tail[1:2] += jnp.sum(total, axis=0, keepdims=True)
        xv[tok] = (gresv[tok].astype(F32) + norm_back(total, normal, inverse, gain_one)).astype(BF16)
        return carry

    lax.fori_loop(0, chunks, last, 0)
    save_x = pltpu.make_async_copy(xv, ig_hbm, out_sem.at[1])
    save_x.start()

    sent_tail = exchange(tail, tail_rec, 1)
    total_of(head, head_rec, 0, sent_head)
    small[0:8] = head[...]
    att.get(0)
    save_a = pltpu.make_async_copy(ag_a, ga_out, out_sem.at[2])
    save_a.start()
    total_of(tail, tail_rec, 1, sent_tail)
    small[8:10] = tail[...]
    big.drain()
    att.drain()
    save_w.wait()
    save_x.wait()
    save_a.wait()


def finish_kernel(
    bo_in, ig_in, gw_in, ga_in, small,
    bo_out, ig_out, gqkv, gbqv, gwo, gwu, gwd, g_b_out, g_gain_one, g_shift_one, g_b_up, g_b_down, g_gain_two, g_shift_two,
    bov, igv, gwv, gav, fw, fa, in_sem, out_sem,
):
    half = bov.shape[0] // 2
    load_w = [
        pltpu.make_async_copy(gw_in.at[pl.ds(768 * h, 768)], gwv.at[pl.ds(768 * h, 768)], in_sem.at[h]) for h in range(2)
    ]
    load_a = pltpu.make_async_copy(ga_in, gav, in_sem.at[2])
    load_bo = pltpu.make_async_copy(bo_in, bov, in_sem.at[3])
    load_ig = pltpu.make_async_copy(ig_in, igv, in_sem.at[4])
    for copy in load_w + [load_a, load_bo, load_ig]:
        copy.start()
    gbqv[...] = small[6:8, 0 : gbqv.shape[1]]
    for ref, n in ((g_b_out, 4), (g_gain_one, 8), (g_shift_one, 9), (g_b_up, 1), (g_b_down, 0), (g_gain_two, 2), (g_shift_two, 3)):
        ref[...] = small[n : n + 1].reshape(768)
    saves = []

    def save(src, dst):
        saves.append(pltpu.make_async_copy(src, dst, out_sem.at[len(saves)]))
        saves[-1].start()

    for h, dst in enumerate((gwu, gwd)):
        load_w[h].wait()
        for q in range(2):
            part = pl.ds(768 * h + 384 * q, 384)
            fw[part] = gwv[part].astype(F32)
            save(fw.at[part], dst.at[pl.ds(384 * q, 384)])
    load_a.wait()
    for n, dst in enumerate((gqkv.at[2], gqkv.at[0], gqkv.at[1], gwo)):
        part = pl.ds(192 * n, 192)
        fa[part] = gav[part].astype(F32)
        save(fa.at[part], dst)
    load_bo.wait()
    save(bov, bo_out)
    load_ig.wait()
    save(igv, ig_out)
    for copy in saves:
        copy.wait()


def layer(n_dp, tokens, segment_ids, cotangent, w_qkv, b_qv, w_out, b_out, gain_one, shift_one, w_up, b_up, w_down, b_down, gain_two, shift_two):
    count, width = tokens.shape[0], w_qkv.shape[2]
    rows = segment_ids.shape[0]
    units = MP * (count // 512)
    extra = (n_dp // 8).bit_length() - 1
    any_space = pl.BlockSpec(memory_space=pl.ANY)
    in_vmem = pl.BlockSpec(memory_space=pltpu.VMEM)
    wt = jnp.transpose(w_qkv, (0, 2, 1))
    dma = pltpu.SemaphoreType.DMA

    def sds(shape, dtype):
        return jax.ShapeDtypeStruct(shape, dtype)

    def fwd(*refs):
        return forward_kernel(count, *refs)

    block_out, qkvr, e, n1, mixed, gres, waf, gw, small = pl.pallas_call(
        fwd,
        name="forward",
        out_shape=(
            sds((count, 768), BF16),
            sds((units, 4, 512, 256), BF16),
            sds((units, 6, SEQ, SEQ), BF16),
            sds((count, 768), BF16),
            sds((MP, count, 256), BF16),
            sds((count, 768), BF16),
            sds((MP, 768, 768), BF16),
            sds((1536, 768), BF16),
            sds((16, 768), F32),
        ),
        in_specs=[any_space, any_space, in_vmem] + [any_space] * 5 + [in_vmem] * 7,
        out_specs=(any_space,) * 7 + (in_vmem, in_vmem),
        scratch_shapes=[
            pltpu.VMEM((MP, 2304, 768), BF16),
            pltpu.VMEM((MP, 2, 256), F32),
            pltpu.VMEM((MP, 1, 768), F32),
            pltpu.VMEM((count, 768), BF16),
            pltpu.VMEM((count, 768), BF16),
            pltpu.VMEM((count, 768), BF16),
            pltpu.VMEM((MP, count, 256), BF16),
            pltpu.VMEM((count, 768), F32),
            pltpu.VMEM((count, 768), F32),
            pltpu.VMEM((rows, SEQ, SEQ), F32),
            pltpu.VMEM((count, 1), F32),
            pltpu.VMEM((768, 768), F32),
            pltpu.VMEM((768, 768), F32),
            pltpu.VMEM((2, 4, 512, 256), BF16),
            pltpu.VMEM((2, 6, SEQ, SEQ), BF16),
            dma((2, count // 512)), dma((7,)), dma((2, 2)), dma((2, 1 + rows)),
            dma((9,)), dma((9, 8)), dma((9, 8)), dma((6,)), dma((6,)),
        ],
        compiler_params=pltpu.CompilerParams(collective_id=0, has_side_effects=True, vmem_limit_bytes=VMEM_LIMIT),
    )(
        tokens, cotangent, segment_ids, wt, w_out, w_up, w_down, b_up, b_qv,
        gain_one, shift_one, b_out, gain_two, shift_two, b_down,
    )

    def bwd(*refs):
        return backward_kernel(count, extra, *refs)

    input_grad, gw_full, ga_full, small = pl.pallas_call(
        bwd,
        name="backward",
        out_shape=(
            sds((count, 768), BF16),
            sds((1536, 768), BF16),
            sds((768, 768), BF16),
            sds((16, 768), F32),
        ),
        in_specs=[any_space] * 8 + [in_vmem, in_vmem],
        out_specs=(any_space,) * 3 + (in_vmem,),
        scratch_shapes=[
            pltpu.VMEM((MP, 768, 768), BF16),
            pltpu.VMEM((count, 768), BF16),
            pltpu.VMEM((MP, count, 256), BF16),
            pltpu.VMEM((count, 768), BF16),
            pltpu.VMEM((count, 768), BF16),
            pltpu.VMEM((3, MP, count, 256), BF16),
            pltpu.VMEM((2, 4, 512, 256), BF16),
            pltpu.VMEM((2, 6, SEQ, SEQ), BF16),
            pltpu.VMEM((1536, 768), BF16),
            pltpu.VMEM((1536, 768), BF16),
            pltpu.VMEM((1344 + 192 * extra, 768), BF16),
            pltpu.VMEM((768, 768), BF16),
            pltpu.VMEM((768, 768), BF16),
            pltpu.VMEM((672 + 96 * extra, 768), BF16),
            pltpu.VMEM((768, 768), F32),
            pltpu.VMEM((8, 768), F32),
            pltpu.VMEM((8 + extra, 8, 768), F32),
            pltpu.VMEM((2, 768), F32),
            pltpu.VMEM((8 + extra, 2, 768), F32),
            dma((11,)), dma((2, 2)), dma((3,)),
            dma((2, 3 + extra)), dma((2, 3 + extra)), dma((2, 3)), dma((2, 3)),
            dma((2, 7 + extra)), dma((2, 8 + extra)),
        ],
        compiler_params=pltpu.CompilerParams(collective_id=1, has_side_effects=True, vmem_limit_bytes=VMEM_LIMIT),
    )(qkvr, e, n1, mixed, gres, tokens, waf, gw, small, gain_one)

    row = sds((768,), F32)
    block_out, input_grad, grad_qkv, b_qv_grad, grad_out, grad_up, grad_down, *vectors = pl.pallas_call(
        finish_kernel,
        name="finish",
        out_shape=(
            sds((count, 768), BF16), sds((count, 768), BF16), sds((3, width, 768), F32), sds((2, width), F32),
            sds((width, 768), F32), sds((768, 768), F32), sds((768, 768), F32),
        ) + (row,) * 7,
        in_specs=[any_space] * 4 + [in_vmem],
        out_specs=(any_space,) * 3 + (in_vmem,) + (any_space,) * 3 + (in_vmem,) * 7,
        scratch_shapes=[
            pltpu.VMEM((count, 768), BF16), pltpu.VMEM((count, 768), BF16),
            pltpu.VMEM((1536, 768), BF16), pltpu.VMEM((768, 768), BF16),
            pltpu.VMEM((1536, 768), F32), pltpu.VMEM((768, 768), F32),
            dma((5,)), dma((14,)),
        ],
        compiler_params=pltpu.CompilerParams(vmem_limit_bytes=VMEM_LIMIT),
    )(block_out, input_grad, gw_full, ga_full, small)
    g_b_out, g_gain_one, g_shift_one, g_b_up, g_b_down, g_gain_two, g_shift_two = vectors
    return (
        block_out,
        input_grad,
        jnp.transpose(grad_qkv, (0, 2, 1)),
        b_qv_grad,
        grad_out,
        g_b_out,
        g_gain_one,
        g_shift_one,
        grad_up,
        g_b_up,
        grad_down,
        g_b_down,
        g_gain_two,
        g_shift_two,
    )


def solution(mesh):
    n_dp = mesh.shape["dp"]

    def run(*args):
        return layer(n_dp, *args)

    placed = (
        P("dp", None), P("dp", None), P("dp", None), P(None, None, "mp"), P(None, "mp"), P("mp", None), P(), P(), P(),
        P(None, "mp"), P("mp"), P("mp", None), P(), P(), P(),
    )
    return jax.shard_map(
        run,
        mesh=mesh,
        in_specs=placed,
        out_specs=(
            P("dp", None), P("dp", None), P(None, None, "mp"), P(None, "mp"), P("mp", None), P(), P(), P(),
            P(None, "mp"), P("mp"), P("mp", None), P(), P(), P(),
        ),
        check_vma=False,
    )
```

```python
import jax
import jax.numpy as jnp
from jax import lax
from jax.experimental import pallas as pl
from jax.experimental.pallas import tpu as pltpu
from jax.sharding import PartitionSpec as P

HD = 64
SEQ = 256
EPS = 1e-06
MASKED = -1000000000.0
MESH = pl.DeviceIdType.MESH
F32 = jnp.float32
BF16 = jnp.bfloat16
MP = 4
GELU_C = 0.7978845608028654
GELU_A = 0.044715
VMEM_LIMIT = 66_000_000


def nn(a, b):
    return lax.dot_general(a, b, (((1,), (0,)), ((), ())), preferred_element_type=F32)


def nt(a, b):
    return lax.dot_general(a, b, (((1,), (1,)), ((), ())), preferred_element_type=F32)


def tn(a, b):
    return lax.dot_general(a, b, (((0,), (0,)), ((), ())), preferred_element_type=F32)


def xor4(a, b):
    return (a % 2 + b % 2) % 2 + 2 * ((a // 2 + b // 2) % 2)


def places():
    d = lax.axis_index("dp")
    z = lax.axis_index("mp")
    p = d % 8
    kb, xb, yb = p % 2, (p // 2) % 2, (p // 4) % 2
    fc = d + (1 - 2 * kb)
    fx = d + 2 * (1 - 2 * xb)
    fy = d + 4 * (1 - 2 * yb)
    a = fx * (1 - kb) + fy * kb
    b = fy * (1 - kb) + fx * kb
    bit_a = xb * (1 - kb) + yb * kb
    bit_b = yb * (1 - kb) + xb * kb
    return d, z, p, kb, fc, a, b, bit_a, bit_b


def rows_at(start, size):
    return pl.ds(pl.multiple_of(start, size), size)


def norm_parts(h):
    centre = h - jnp.mean(h, axis=-1, keepdims=True)
    inverse = lax.rsqrt(jnp.mean(centre * centre, axis=-1, keepdims=True) + EPS)
    return centre * inverse, inverse


def norm_back(grad, normal, inverse, gain):
    scaled = grad * gain
    return inverse * (
        scaled
        - jnp.mean(scaled, axis=-1, keepdims=True)
        - normal * jnp.mean(scaled * normal, axis=-1, keepdims=True)
    )


def forward_kernel(
    count,
    x_hbm, cot_hbm, seg, wqkv_hbm, wo_hbm, wu_hbm, wd_hbm, bu_hbm, bqv, g1, s1_ref, bo, g2, s2_ref, bd,
    out_hbm, qkvr_hbm, e_hbm, n1_hbm, mixed_hbm, gres_hbm, waf_hbm, gw_ref, small,
    W, BQ, BU, xv, glv, n1v, mixv, acc, gn2, bias, rstd, gwu, gwd, stq, ste,
    load_sem, own_sem, stage_sem, out_sem, zsend, send, recv, bsend, brecv,
):
    d, z, p, kb, fc, a, b, bit_a, bit_b = places()
    chunks = count // 512
    rows = count // SEQ

    loads = []
    for c in range(chunks):
        part = pl.ds(c * 512, 512)
        loads.append((
            pltpu.make_async_copy(x_hbm.at[part], xv.at[part], load_sem.at[0, c]),
            pltpu.make_async_copy(cot_hbm.at[part], glv.at[part], load_sem.at[1, c]),
        ))
        loads[-1][0].start()
        loads[-1][1].start()
    own = [
        pltpu.make_async_copy(wqkv_hbm.at[2], W.at[z, pl.ds(0, 192)], own_sem.at[0]),
        pltpu.make_async_copy(wqkv_hbm.at[0], W.at[z, pl.ds(192, 192)], own_sem.at[1]),
        pltpu.make_async_copy(wqkv_hbm.at[1], W.at[z, pl.ds(384, 192)], own_sem.at[2]),
        pltpu.make_async_copy(wo_hbm, W.at[z, pl.ds(576, 192)], own_sem.at[3]),
        pltpu.make_async_copy(bu_hbm, BU.at[z, 0], own_sem.at[4]),
        pltpu.make_async_copy(wu_hbm, W.at[z, pl.ds(768, 768)], own_sem.at[5]),
        pltpu.make_async_copy(wd_hbm, W.at[z, pl.ds(1536, 768)], own_sem.at[6]),
    ]
    for copy in own:
        copy.start()
    BQ[z] = jnp.zeros((2, 256), F32)
    BQ[z, :, 0:192] = bqv[...]

    peers = [(d, xor4(z, s)) for s in (1, 2, 3)] + [(fc, z), (a, z), (b, z)]
    barrier = pltpu.get_barrier_semaphore()
    for peer in peers:
        pl.semaphore_signal(barrier, inc=1, device_id=peer, device_id_type=MESH)
    pl.semaphore_wait(barrier, len(peers))
    for copy in own:
        copy.wait()

    def remote(src, dst, ss, rs, to):
        return pltpu.make_async_remote_copy(
            src_ref=src, dst_ref=dst, send_sem=ss, recv_sem=rs, device_id=to, device_id_type=MESH
        )

    def piece_rows(base, which):
        return pl.ds(pl.multiple_of(base + 96 * which, 96), 96)

    zcopies = []
    for s in (1, 2, 3):
        to = (d, xor4(z, s))
        zcopies.append(remote(BQ.at[z], BQ.at[z], bsend.at[s - 1], brecv.at[s - 1], to))
        zcopies.append(remote(BU.at[z], BU.at[z], bsend.at[s + 2], brecv.at[s + 2], to))
        part = W.at[z, piece_rows(0, p)]
        zcopies.append(remote(part, part, zsend.at[s - 1], recv.at[s - 1, 0], to))
    for s in (1, 2, 3):
        for h in range(2):
            t = 1 + 2 * s + h
            part = W.at[z, piece_rows(768 * (h + 1), p)]
            zcopies.append(remote(part, part, zsend.at[t], recv.at[t, 0], (d, xor4(z, s))))
    for copy in zcopies:
        copy.start()

    def step_of(t):
        late = jnp.maximum(t - 3, 0)
        g = xor4(z, jnp.where(t < 3, t, late // 2) + 1)
        return g, jnp.where(t < 3, 0, 768 + 768 * (late % 2))

    def hop(t, index, which, to):
        g, base = step_of(t)
        part = W.at[g, piece_rows(base, which)]
        return remote(part, part, send.at[t, index], recv.at[t, index], to)

    pa, pb, pc = a % 8, b % 8, fc % 8
    pd = (a + b - d) % 8
    me = (d, z)

    def s1(t):
        hop(t, 0, p, me).wait_recv()
        hop(t, 1, p, (a, z)).start()
        hop(t, 2, p, (b, z)).start()
        hop(t, 3, p, (fc, z)).start()

    def s2(t):
        hop(t, 1, pa, me).wait_recv()
        hop(t, 4, pa, (b, z)).start()
        hop(t, 5, pa, (fc, z)).start()
        hop(t, 2, pb, me).wait_recv()
        hop(t, 6, pb, (fc, z)).start()

    def s3(t):
        hop(t, 4, pd, me).wait_recv()
        hop(t, 7, pd, (fc, z)).start()

    def core_flip(q):
        return q + 1 - 2 * (q % 2)

    def fin(t):
        hop(t, 3, core_flip(p), me).wait_recv()
        hop(t, 5, core_flip(pb), me).wait_recv()
        hop(t, 6, core_flip(pa), me).wait_recv()
        hop(t, 7, core_flip(pd), me).wait_recv()

    small[...] = jnp.zeros_like(small)
    gain_one, shift_one, b_out, gain_two, shift_two, b_down = (
        ref[...].reshape(1, 768) for ref in (g1, s1_ref, bo, g2, s2_ref, bd)
    )

    def head(r, carry):
        part = rows_at(r * SEQ, SEQ)
        normal, inverse = norm_parts(xv[part].astype(F32))
        n1v[part] = (normal * gain_one + shift_one).astype(BF16)
        seg_row = seg[pl.ds(r, 1)].astype(F32)
        seg_col = jnp.broadcast_to(seg_row, (128, SEQ)).T
        for half in range(2):
            lanes = slice(half * 128, half * 128 + 128)
            bias[r, :, lanes] = jnp.where(seg_col == seg_row[:, lanes], 0.0, MASKED)
        for part6 in range(6):
            lanes = slice(part6 * 128, part6 * 128 + 128)
            masked = jnp.where(seg_col != 0.0, glv[part, lanes].astype(F32), 0.0)
            small[0:1, lanes] += jnp.sum(masked, axis=0, keepdims=True)
            glv[part, lanes] = masked.astype(BF16)
        return carry

    for pair in loads:
        pair[0].wait()
        pair[1].wait()
    lax.fori_loop(0, rows, head, 0)
    save_n1 = pltpu.make_async_copy(n1v, n1_hbm, out_sem.at[0, 0])
    save_n1.start()

    lo = lax.broadcasted_iota(jnp.int32, (SEQ, 128), 1) < HD
    lo_b = lo

    def stage_copies(slot, u):
        return (
            pltpu.make_async_copy(stq.at[slot], qkvr_hbm.at[u], stage_sem.at[0, slot]),
            pltpu.make_async_copy(ste.at[slot], e_hbm.at[u], stage_sem.at[1, slot]),
        )

    plan = (
        (s2, (3, 6, 9, 13, 16, 19, 22, 24, 26)),
        (s3, (4, 7, 11, 15, 18, 21, 24, 26, 28)),
        (s1, (1, 4, 7, 10, 13, 16, 19, 21, 23)),
        (fin, (4, 8, 12, 24, 24, 28, 28, 32, 32)),
    )

    def tick(i):
        for action, whens in plan:
            def act(t, carry):
                action(t)
                return carry

            first = sum(jnp.where(i > when, 1, 0) for when in whens)
            lax.fori_loop(first, sum(jnp.where(i >= when, 1, 0) for when in whens), act, 0)

    def attend(i, carry):
        tick(i)

        @pl.when((i >= 4) & (i % 4 == 0))
        def _():
            there = i // 4
            for ref, first in ((BQ, -1), (BU, 2)):
                block = ref.at[xor4(z, there)]
                remote(block, block, bsend.at[first + there], brecv.at[first + there], me).wait_recv()

        s, c = i // 4, i % 4
        g = xor4(z, s)
        slot = i % 2
        u = g * 4 + c
        tok = rows_at(c * 512, 512)

        @pl.when(i >= 2)
        def _():
            for copy in stage_copies(slot, u):
                copy.wait()

        n1c = n1v[tok]
        v_all = (nt(n1c, W[g, 0:256]) + BQ[g, 1:2]).astype(BF16)
        q_all = ((nt(n1c, W[g, 192:448]) + BQ[g, 0:1]) * 0.125).astype(BF16)
        k_all = nt(n1c, W[g, 384:640]).astype(BF16)
        stq[slot, 0] = v_all
        stq[slot, 1] = q_all
        stq[slot, 2] = k_all
        one = jnp.ones((SEQ, 128), BF16)
        zero = jnp.zeros((SEQ, 128), BF16)
        for r in range(2):
            tr = slice(r * SEQ, r * SEQ + SEQ)
            mask = bias[c * 2 + r]

            def weights(qp, kp, h):
                sc = nt(qp, kp) + mask
                e = jnp.exp(sc - jnp.max(sc, axis=-1, keepdims=True)).astype(BF16)
                ste[slot, r * 3 + h] = e
                return e

            qp, kp, vp = q_all[tr, 0:128], k_all[tr, 0:128], v_all[tr, 0:128]
            e0 = weights(qp, jnp.where(lo_b, kp, zero), 0)
            o0 = nn(e0, jnp.where(lo_b, vp, one))
            e1 = weights(qp, jnp.where(lo_b, zero, kp), 1)
            o1 = nn(e1, jnp.where(lo_b, one, vp))
            r01 = 1.0 / pltpu.roll(jnp.where(lo, o1, o0), 64, 1)
            mix01 = jnp.where(lo, o0, o1) * r01
            qp, kp, vp = q_all[tr, 128:256], k_all[tr, 128:256], v_all[tr, 128:256]
            e2 = weights(qp, jnp.where(lo_b, kp, zero), 2)
            o2 = nn(e2, jnp.where(lo_b, vp, one))
            r2 = 1.0 / jnp.where(lo, pltpu.roll(o2, 64, 1), 1.0)
            mix2 = jnp.where(lo, o2 * r2, 0.0)
            dst = rows_at(c * 512 + r * SEQ, SEQ)
            mixv[g, dst, 0:128] = mix01.astype(BF16)
            mixv[g, dst, 128:256] = mix2.astype(BF16)
            stq[slot, 3, tr, 0:128] = r01.astype(BF16)
            stq[slot, 3, tr, 128:256] = r2.astype(BF16)
        for copy in stage_copies(slot, u):
            copy.start()
        return carry

    lax.fori_loop(0, 4 * chunks, attend, 0)
    for slot in range(2):
        for copy in stage_copies(slot, slot):
            copy.wait()
    save_n1.wait()
    save_mixed = pltpu.make_async_copy(mixv, mixed_hbm, out_sem.at[0, 0])
    save_mixed.start()
    save_wa = pltpu.make_async_copy(W.at[:, pl.ds(0, 768)], waf_hbm, out_sem.at[1, 0])
    save_wa.start()

    def project(c, carry):
        tick(4 * chunks + c)
        tok = rows_at(c * 512, 512)
        total = nn(mixv[0, tok, 0:192], W[0, 576:768])
        for g in range(1, MP):
            total = total + nn(mixv[g, tok, 0:192], W[g, 576:768])
        hidden = xv[tok].astype(F32) + total + b_out
        acc[tok] = hidden
        normal, inverse = norm_parts(hidden)
        xv[tok] = normal.astype(BF16)
        rstd[tok] = inverse
        n1v[tok] = (normal * gain_two + shift_two).astype(BF16)
        gn2[tok] = jnp.zeros((512, 768), F32)
        return carry

    lax.fori_loop(0, chunks, project, 0)
    gwu[...] = jnp.zeros_like(gwu)
    gwd[...] = jnp.zeros_like(gwd)

    def feed(j, carry):
        tick(5 * chunks + j)
        g, c = xor4(z, j // 4), j % 4
        tok = rows_at(c * 512, 512)
        n2c = n1v[tok]
        glc = glv[tok]
        acts, lows, sums = [], [], []
        for n in range(3):
            cols = slice(n * 256, n * 256 + 256)
            pre = nn(n2c, W[g, 768:1536, cols]) + BU[g, 0:1, cols]
            grad_act = nt(glc, W[g, 1536 + n * 256 : 1792 + n * 256])
            square = pre * pre
            t = jnp.tanh(pre * (GELU_C + (GELU_C * GELU_A) * square))
            half = 0.5 + 0.5 * t
            slope = half + pre * (0.5 - 0.5 * (t * t)) * (GELU_C + (3.0 * GELU_C * GELU_A) * square)
            grad_pre = grad_act * slope
            acts.append((pre * half).astype(BF16))
            lows.append(grad_pre.astype(BF16))
            sums.append(jnp.sum(grad_pre, axis=0, keepdims=True))
        act = jnp.concatenate(acts, axis=1)
        low = jnp.concatenate(lows, axis=1)
        acc[tok] += nn(act, W[g, 1536:2304])
        gn2[tok] += nt(low, W[g, 768:1536])

        @pl.when(g == z)
        def _():
            gwu[...] += tn(n2c, low)
            gwd[...] += tn(act, glc)
            for n in range(3):
                small[1:2, n * 256 : n * 256 + 256] += sums[n]

        return carry

    lax.fori_loop(0, MP * chunks, feed, 0)
    gw_ref[0:768] = gwu[...].astype(BF16)
    gw_ref[768:1536] = gwd[...].astype(BF16)

    def closed_copies(r):
        tok = rows_at(r * SEQ, SEQ)
        return (
            pltpu.make_async_copy(xv.at[tok], out_hbm.at[tok], out_sem.at[0, 1 + r]),
            pltpu.make_async_copy(glv.at[tok], gres_hbm.at[tok], out_sem.at[1, 1 + r]),
        )

    def close(r, carry):
        tok = rows_at(r * SEQ, SEQ)
        normal = xv[tok].astype(F32)
        xv[tok] = (acc[tok] + b_down).astype(BF16)
        grad = gn2[tok]
        small[2:3] += jnp.sum(grad * normal, axis=0, keepdims=True)
        small[3:4] += jnp.sum(grad, axis=0, keepdims=True)
        total = glv[tok].astype(F32) + norm_back(grad, normal, rstd[tok], gain_two)
        small[4:5] += jnp.sum(total, axis=0, keepdims=True)
        glv[tok] = total.astype(BF16)
        for copy in closed_copies(r):
            copy.start()
        return carry

    lax.fori_loop(0, rows, close, 0)
    for copy in zcopies:
        copy.wait_send()
    for t in range(9):
        hop(t, 1, p, (a, z)).wait_send()
        hop(t, 2, p, (b, z)).wait_send()
        hop(t, 3, p, (fc, z)).wait_send()
        hop(t, 4, pa, (b, z)).wait_send()
        hop(t, 5, pa, (fc, z)).wait_send()
        hop(t, 6, pb, (fc, z)).wait_send()
        hop(t, 7, pd, (fc, z)).wait_send()
    save_mixed.wait()
    save_wa.wait()

    def closed(r, carry):
        for copy in closed_copies(r):
            copy.wait()
        return carry

    lax.fori_loop(0, rows, closed, 0)


def backward_kernel(
    count, extra,
    qkvr_hbm, e_hbm, n1_hbm, mixed_hbm, gres_hbm, x_hbm, waf_hbm, gw_hbm, small_in, g1,
    ig_hbm, gw_out, ga_out, small,
    WA, n1v, mixv, gresv, xv, dqkv, stq, ste,
    cur_w, ag_w, rec_w, cur_a, ag_a, rec_a, ga, head, head_rec, tail, tail_rec,
    load_sem, stage_sem, out_sem, rs_send, rs_recv, ag_send, ag_recv, sm_send, sm_recv,
):
    d, z, p, kb, fc, a, b, bit_a, bit_b = places()
    xb, yb = p // 2 % 2, p // 4
    chunks = count // 512

    def load(src, dst, n):
        return pltpu.make_async_copy(src, dst, load_sem.at[n])

    top, rest = pl.ds(0, 512), pl.ds(512, count - 512)
    load_first = [
        load(waf_hbm.at[:, pl.ds(576, 192)], WA.at[:, pl.ds(576, 192)], 0),
        load(gres_hbm.at[top], gresv.at[top], 1),
        load(mixed_hbm.at[z], mixv.at[z], 2),
    ]
    load_grads = load(gw_hbm, cur_w, 3)
    load_next = [load(gres_hbm.at[rest], gresv.at[rest], 4)] + [
        load(mixed_hbm.at[xor4(z, s)], mixv.at[xor4(z, s)], 4 + s) for s in (1, 2, 3)
    ]
    load_n1 = load(n1_hbm, n1v, 8)
    load_last = [
        load(waf_hbm.at[:, pl.ds(0, 576)], WA.at[:, pl.ds(0, 576)], 9),
        load(x_hbm, xv, 10),
    ]

    def unit_of(i):
        return xor4(z, i // 4) * 4 + i % 4

    def fetch(i, slot):
        u = unit_of(i)
        return (
            pltpu.make_async_copy(qkvr_hbm.at[u], stq.at[slot], stage_sem.at[0, slot]),
            pltpu.make_async_copy(e_hbm.at[u], ste.at[slot], stage_sem.at[1, slot]),
        )

    for copy in fetch(0, 0):
        copy.start()
    for copy in load_first + [load_grads] + load_next + [load_n1] + load_last:
        copy.start()

    partners = [fc, a, b]
    bits = [kb, bit_a, bit_b]
    for m in range(extra):
        step = 8 << m
        partners.append(d + step * (1 - 2 * ((d // step) % 2)))
    peers = [
        d - p + (1 - kb if k % 2 else kb) + 2 * (1 - xb if k // 2 % 2 else xb) + 4 * (1 - yb if k // 4 else yb)
        for k in range(1, 8)
    ]
    barrier = pltpu.get_barrier_semaphore()
    for peer in peers + partners[3:]:
        pl.semaphore_signal(barrier, inc=1, device_id=(peer, z), device_id_type=MESH)
    pl.semaphore_wait(barrier, 7 + extra)

    def remote(src, dst, ss, rs, to):
        return pltpu.make_async_remote_copy(
            src_ref=src, dst_ref=dst, send_sem=ss, recv_sem=rs, device_id=to, device_id_type=MESH
        )

    class Reduce:
        def __init__(self, which, height, cur, ag, rec):
            self.which, self.cur, self.ag, self.rec = which, cur, ag, rec
            self.half = [height // 2, height // 4, height // 8]
            self.off = [0]
            for k in range(3):
                self.off.append(self.off[k] + bits[k] * self.half[k])
            self.place = [0, self.half[0], self.half[0] + self.half[1]]

        def at(self, ref, start, size):
            if isinstance(start, int):
                return ref.at[pl.ds(start, size)]
            return ref.at[pl.ds(pl.multiple_of(start, 32), size)]

        def rs(self, k):
            theirs = self.off[k] + (1 - bits[k]) * self.half[k]
            return remote(
                self.at(self.cur, theirs, self.half[k]),
                self.at(self.rec, self.place[k], self.half[k]),
                rs_send.at[self.which, k], rs_recv.at[self.which, k], (partners[k], z),
            )

        def send(self, k):
            self.rs(k).start()

        def add(self, start, place, size):
            for q in range(size // 96):
                mine = pl.ds(pl.multiple_of(start + q * 96, 32), 96)
                other = self.rec[place + q * 96 : place + q * 96 + 96]
                self.cur[mine] = (self.cur[mine].astype(F32) + other.astype(F32)).astype(BF16)

        def take(self, k):
            self.rs(k).wait_recv()
            self.add(self.off[k + 1], self.place[k], self.half[k])

        def middle(self):
            size = self.half[2]
            block = self.at(self.cur, self.off[3], size)
            for m in range(extra):
                place = self.place[2] + size * (m + 1)
                copy = remote(
                    block, self.at(self.rec, place, size),
                    rs_send.at[self.which, 3 + m], rs_recv.at[self.which, 3 + m], (partners[3 + m], z),
                )
                copy.start()
                copy.wait()
                self.add(self.off[3], place, size)
            mine = pl.ds(pl.multiple_of(self.off[3], 32), size)
            self.ag[mine] = self.cur[mine]

        def gather(self, k, start):
            part = self.at(self.ag, start, self.half[k])
            return remote(part, part, ag_send.at[self.which, k], ag_recv.at[self.which, k], (partners[k], z))

        def give(self, k):
            self.gather(k, self.off[k + 1]).start()

        def get(self, k):
            self.gather(k, self.off[k] + (1 - bits[k]) * self.half[k]).wait_recv()

        def drain(self):
            for k in range(3):
                self.rs(k).wait_send()
                self.gather(k, self.off[k + 1]).wait_send()

    big = Reduce(0, 1536, cur_w, ag_w, rec_w)
    att = Reduce(1, 768, cur_a, ag_a, rec_a)

    load_grads.wait()
    big.send(0)
    small[...] = small_in[...]
    tail[...] = jnp.zeros_like(tail)
    gain_one = g1[...].reshape(1, 768)
    lo = lax.broadcasted_iota(jnp.int32, (SEQ, 128), 1) < HD
    ga[...] = jnp.zeros_like(ga)
    spread = (
        lax.broadcasted_iota(jnp.int32, (192, 384), 0) // HD
        == lax.broadcasted_iota(jnp.int32, (192, 384), 1) // 128
    ).astype(F32).astype(BF16)
    for copy in load_first:
        copy.wait()

    def own_ready():
        load_n1.wait()
        n1c = n1v[...]
        for c in range(3):
            ga[c * 192 : c * 192 + 192] += tn(dqkv[c, z, :, 0:192], n1c)
        cur_a[...] = ga[...].astype(BF16)
        att.send(0)

    def next_ready():
        for copy in load_next:
            copy.wait()

    plan = {
        1: next_ready,
        2: lambda: (big.take(0), big.send(1)),
        4: own_ready,
        5: lambda: (big.take(1), big.send(2)),
        7: lambda: (big.take(2), big.middle(), big.give(2), att.take(0), att.send(1)),
        9: lambda: (big.get(2), big.give(1)),
        10: lambda: (att.take(1), att.send(2)),
        12: lambda: (big.get(1), big.give(0), att.take(2), att.middle(), att.give(2)),
        14: lambda: (att.get(2), att.give(1)),
    }

    def unit(i, carry):
        for when, action in plan.items():
            @pl.when(i == when)
            def _():
                action()

        slot = i % 2
        for copy in fetch(i, slot):
            copy.wait()

        @pl.when(i + 1 < 4 * chunks)
        def _():
            for copy in fetch(i + 1, 1 - slot):
                copy.start()

        g, c = xor4(z, i // 4), i % 4
        tok = rows_at(c * 512, 512)
        low = gresv[tok]
        mixed = mixv[g, tok, 0:192]
        grad_mixed = nt(low, WA[g, 576:768]).astype(BF16).astype(F32)

        @pl.when(i < 4)
        def _():
            ga[576:768] += tn(mixed, low)

        scaled = (grad_mixed * stq[slot, 3, :, 0:192].astype(F32)).astype(BF16)
        delta = nn((scaled.astype(F32) * mixed.astype(F32)).astype(BF16), spread)
        zero = jnp.zeros((SEQ, 128), BF16)
        for r in range(2):
            tr = slice(r * SEQ, r * SEQ + SEQ)
            dst = rows_at(c * 512 + r * SEQ, SEQ)
            vp, qp, kp = (stq[slot, n, tr, 0:128] for n in range(3))
            dp = scaled[tr, 0:128]
            res = []
            for h in range(2):
                e = ste[slot, r * 3 + h]
                mine = jnp.where(lo, vp, zero) if h == 0 else jnp.where(lo, zero, vp)
                dh = delta[tr, h * 128 : h * 128 + 128]
                grad = nt(dp, mine) - jnp.concatenate([dh, dh], axis=1)
                ds = (e.astype(F32) * grad).astype(BF16)
                res.append((tn(e, dp), nn(ds, kp), tn(ds, qp)))
            pairs = [jnp.where(lo, x0, x1) for x0, x1 in zip(res[0], res[1])]
            dv, dq, dk = pairs[0], pairs[1] * 0.125, pairs[2]
            for n, value in enumerate((dv, dq, dk)):
                dqkv[n, g, dst, 0:128] = value.astype(BF16)

            v2, q2, k2 = (stq[slot, n, tr, 128:192] for n in range(3))
            d2 = scaled[tr, 128:192]
            e = ste[slot, r * 3 + 2]
            dh = delta[tr, 256:384]
            ds = (e.astype(F32) * (nt(d2, v2) - jnp.concatenate([dh, dh], axis=1))).astype(BF16)
            dv2, dq2, dk2 = tn(e, d2), nn(ds, k2) * 0.125, tn(ds, q2)
            for n, value in enumerate((dv2, dq2, dk2)):
                dqkv[n, g, dst, 128:192] = value.astype(BF16)

            @pl.when(i < 4)
            def _():
                small[6:7, 0:128] += jnp.sum(dq, axis=0, keepdims=True)
                small[6:7, 128:192] += jnp.sum(dq2, axis=0, keepdims=True)
                small[7:8, 0:128] += jnp.sum(dv, axis=0, keepdims=True)
                small[7:8, 128:192] += jnp.sum(dv2, axis=0, keepdims=True)

        return carry

    lax.fori_loop(0, 4 * chunks, unit, 0)
    big.get(0)
    att.get(1)
    att.give(0)
    save_w = pltpu.make_async_copy(ag_w, gw_out, out_sem.at[0])
    save_w.start()

    def exchange(ref, rec, which):
        mine = [remote(ref, rec.at[p], sm_send.at[which, k], sm_recv.at[which, p], (peer, z)) for k, peer in enumerate(peers)]
        for copy in mine:
            copy.start()
        return mine

    def total_of(ref, rec, which, mine):
        for copy in mine:
            copy.wait_send()
        for k, peer in enumerate(peers):
            other = peer - (d - p)
            remote(ref, rec.at[other], sm_send.at[which, k], sm_recv.at[which, other], (peer, z)).wait_recv()
        rec[p] = ref[...]
        ref[...] = sum(rec[k] for k in range(1, 8)) + rec[0]
        for m in range(extra):
            copy = remote(ref, rec.at[8 + m], sm_send.at[which, 7 + m], sm_recv.at[which, 8 + m], (partners[3 + m], z))
            copy.start()
            copy.wait()
            ref[...] += rec[8 + m]

    head[...] = small[0:8]
    sent_head = exchange(head, head_rec, 0)
    for copy in load_last:
        copy.wait()

    def last(c, carry):
        tok = rows_at(c * 512, 512)
        total = nn(dqkv[0, 0, tok, 0:192], WA[0, 0:192])
        for g in range(MP):
            for n in range(3):
                if g + n > 0:
                    total = total + nn(dqkv[n, g, tok, 0:192], WA[g, n * 192 : n * 192 + 192])
        normal, inverse = norm_parts(xv[tok].astype(F32))
        tail[0:1] += jnp.sum(total * normal, axis=0, keepdims=True)
        tail[1:2] += jnp.sum(total, axis=0, keepdims=True)
        xv[tok] = (gresv[tok].astype(F32) + norm_back(total, normal, inverse, gain_one)).astype(BF16)
        return carry

    lax.fori_loop(0, chunks, last, 0)
    save_x = pltpu.make_async_copy(xv, ig_hbm, out_sem.at[1])
    save_x.start()

    sent_tail = exchange(tail, tail_rec, 1)
    total_of(head, head_rec, 0, sent_head)
    small[0:8] = head[...]
    att.get(0)
    save_a = pltpu.make_async_copy(ag_a, ga_out, out_sem.at[2])
    save_a.start()
    total_of(tail, tail_rec, 1, sent_tail)
    small[8:10] = tail[...]
    big.drain()
    att.drain()
    save_w.wait()
    save_x.wait()
    save_a.wait()


def finish_kernel(
    bo_in, ig_in, gw_in, ga_in, small,
    bo_out, ig_out, gqkv, gbqv, gwo, gwu, gwd, g_b_out, g_gain_one, g_shift_one, g_b_up, g_b_down, g_gain_two, g_shift_two,
    bov, igv, gwv, gav, fw, fa, in_sem, out_sem,
):
    half = bov.shape[0] // 2
    load_w = [
        pltpu.make_async_copy(gw_in.at[pl.ds(768 * h, 768)], gwv.at[pl.ds(768 * h, 768)], in_sem.at[h]) for h in range(2)
    ]
    load_a = pltpu.make_async_copy(ga_in, gav, in_sem.at[2])
    load_bo = pltpu.make_async_copy(bo_in, bov, in_sem.at[3])
    load_ig = pltpu.make_async_copy(ig_in, igv, in_sem.at[4])
    for copy in load_w + [load_a, load_bo, load_ig]:
        copy.start()
    gbqv[...] = small[6:8, 0 : gbqv.shape[1]]
    for ref, n in ((g_b_out, 4), (g_gain_one, 8), (g_shift_one, 9), (g_b_up, 1), (g_b_down, 0), (g_gain_two, 2), (g_shift_two, 3)):
        ref[...] = small[n : n + 1].reshape(768)
    saves = []

    def save(src, dst):
        saves.append(pltpu.make_async_copy(src, dst, out_sem.at[len(saves)]))
        saves[-1].start()

    for h, dst in enumerate((gwu, gwd)):
        load_w[h].wait()
        for q in range(2):
            part = pl.ds(768 * h + 384 * q, 384)
            fw[part] = gwv[part].astype(F32)
            save(fw.at[part], dst.at[pl.ds(384 * q, 384)])
    load_a.wait()
    for n, dst in enumerate((gqkv.at[2], gqkv.at[0], gqkv.at[1], gwo)):
        part = pl.ds(192 * n, 192)
        fa[part] = gav[part].astype(F32)
        save(fa.at[part], dst)
    load_bo.wait()
    save(bov, bo_out)
    load_ig.wait()
    save(igv, ig_out)
    for copy in saves:
        copy.wait()


def layer(n_dp, tokens, segment_ids, cotangent, w_qkv, b_qv, w_out, b_out, gain_one, shift_one, w_up, b_up, w_down, b_down, gain_two, shift_two):
    count, width = tokens.shape[0], w_qkv.shape[2]
    rows = segment_ids.shape[0]
    units = MP * (count // 512)
    extra = (n_dp // 8).bit_length() - 1
    any_space = pl.BlockSpec(memory_space=pl.ANY)
    in_vmem = pl.BlockSpec(memory_space=pltpu.VMEM)
    wt = jnp.transpose(w_qkv, (0, 2, 1))
    dma = pltpu.SemaphoreType.DMA

    def sds(shape, dtype):
        return jax.ShapeDtypeStruct(shape, dtype)

    def fwd(*refs):
        return forward_kernel(count, *refs)

    block_out, qkvr, e, n1, mixed, gres, waf, gw, small = pl.pallas_call(
        fwd,
        name="forward",
        out_shape=(
            sds((count, 768), BF16),
            sds((units, 4, 512, 256), BF16),
            sds((units, 6, SEQ, SEQ), BF16),
            sds((count, 768), BF16),
            sds((MP, count, 256), BF16),
            sds((count, 768), BF16),
            sds((MP, 768, 768), BF16),
            sds((1536, 768), BF16),
            sds((16, 768), F32),
        ),
        in_specs=[any_space, any_space, in_vmem] + [any_space] * 5 + [in_vmem] * 7,
        out_specs=(any_space,) * 7 + (in_vmem, in_vmem),
        scratch_shapes=[
            pltpu.VMEM((MP, 2304, 768), BF16),
            pltpu.VMEM((MP, 2, 256), F32),
            pltpu.VMEM((MP, 1, 768), F32),
            pltpu.VMEM((count, 768), BF16),
            pltpu.VMEM((count, 768), BF16),
            pltpu.VMEM((count, 768), BF16),
            pltpu.VMEM((MP, count, 256), BF16),
            pltpu.VMEM((count, 768), F32),
            pltpu.VMEM((count, 768), F32),
            pltpu.VMEM((rows, SEQ, SEQ), F32),
            pltpu.VMEM((count, 1), F32),
            pltpu.VMEM((768, 768), F32),
            pltpu.VMEM((768, 768), F32),
            pltpu.VMEM((2, 4, 512, 256), BF16),
            pltpu.VMEM((2, 6, SEQ, SEQ), BF16),
            dma((2, count // 512)), dma((7,)), dma((2, 2)), dma((2, 1 + rows)),
            dma((9,)), dma((9, 8)), dma((9, 8)), dma((6,)), dma((6,)),
        ],
        compiler_params=pltpu.CompilerParams(collective_id=0, has_side_effects=True, vmem_limit_bytes=VMEM_LIMIT),
    )(
        tokens, cotangent, segment_ids, wt, w_out, w_up, w_down, b_up, b_qv,
        gain_one, shift_one, b_out, gain_two, shift_two, b_down,
    )

    def bwd(*refs):
        return backward_kernel(count, extra, *refs)

    input_grad, gw_full, ga_full, small = pl.pallas_call(
        bwd,
        name="backward",
        out_shape=(
            sds((count, 768), BF16),
            sds((1536, 768), BF16),
            sds((768, 768), BF16),
            sds((16, 768), F32),
        ),
        in_specs=[any_space] * 8 + [in_vmem, in_vmem],
        out_specs=(any_space,) * 3 + (in_vmem,),
        scratch_shapes=[
            pltpu.VMEM((MP, 768, 768), BF16),
            pltpu.VMEM((count, 768), BF16),
            pltpu.VMEM((MP, count, 256), BF16),
            pltpu.VMEM((count, 768), BF16),
            pltpu.VMEM((count, 768), BF16),
            pltpu.VMEM((3, MP, count, 256), BF16),
            pltpu.VMEM((2, 4, 512, 256), BF16),
            pltpu.VMEM((2, 6, SEQ, SEQ), BF16),
            pltpu.VMEM((1536, 768), BF16),
            pltpu.VMEM((1536, 768), BF16),
            pltpu.VMEM((1344 + 192 * extra, 768), BF16),
            pltpu.VMEM((768, 768), BF16),
            pltpu.VMEM((768, 768), BF16),
            pltpu.VMEM((672 + 96 * extra, 768), BF16),
            pltpu.VMEM((768, 768), F32),
            pltpu.VMEM((8, 768), F32),
            pltpu.VMEM((8 + extra, 8, 768), F32),
            pltpu.VMEM((2, 768), F32),
            pltpu.VMEM((8 + extra, 2, 768), F32),
            dma((11,)), dma((2, 2)), dma((3,)),
            dma((2, 3 + extra)), dma((2, 3 + extra)), dma((2, 3)), dma((2, 3)),
            dma((2, 7 + extra)), dma((2, 8 + extra)),
        ],
        compiler_params=pltpu.CompilerParams(collective_id=1, has_side_effects=True, vmem_limit_bytes=VMEM_LIMIT),
    )(qkvr, e, n1, mixed, gres, tokens, waf, gw, small, gain_one)

    row = sds((768,), F32)
    block_out, input_grad, grad_qkv, b_qv_grad, grad_out, grad_up, grad_down, *vectors = pl.pallas_call(
        finish_kernel,
        name="finish",
        out_shape=(
            sds((count, 768), BF16), sds((count, 768), BF16), sds((3, width, 768), F32), sds((2, width), F32),
            sds((width, 768), F32), sds((768, 768), F32), sds((768, 768), F32),
        ) + (row,) * 7,
        in_specs=[any_space] * 4 + [in_vmem],
        out_specs=(any_space,) * 3 + (in_vmem,) + (any_space,) * 3 + (in_vmem,) * 7,
        scratch_shapes=[
            pltpu.VMEM((count, 768), BF16), pltpu.VMEM((count, 768), BF16),
            pltpu.VMEM((1536, 768), BF16), pltpu.VMEM((768, 768), BF16),
            pltpu.VMEM((1536, 768), F32), pltpu.VMEM((768, 768), F32),
            dma((5,)), dma((14,)),
        ],
        compiler_params=pltpu.CompilerParams(vmem_limit_bytes=VMEM_LIMIT),
    )(block_out, input_grad, gw_full, ga_full, small)
    g_b_out, g_gain_one, g_shift_one, g_b_up, g_b_down, g_gain_two, g_shift_two = vectors
    return (
        block_out,
        input_grad,
        jnp.transpose(grad_qkv, (0, 2, 1)),
        b_qv_grad,
        grad_out,
        g_b_out,
        g_gain_one,
        g_shift_one,
        grad_up,
        g_b_up,
        grad_down,
        g_b_down,
        g_gain_two,
        g_shift_two,
    )


def solution(mesh):
    n_dp = mesh.shape["dp"]

    def run(*args):
        return layer(n_dp, *args)

    placed = (
        P("dp", None), P("dp", None), P("dp", None), P(None, None, "mp"), P(None, "mp"), P("mp", None), P(), P(), P(),
        P(None, "mp"), P("mp"), P("mp", None), P(), P(), P(),
    )
    return jax.shard_map(
        run,
        mesh=mesh,
        in_specs=placed,
        out_specs=(
            P("dp", None), P("dp", None), P(None, None, "mp"), P(None, "mp"), P("mp", None), P(), P(), P(),
            P(None, "mp"), P("mp"), P("mp", None), P(), P(), P(),
        ),
        check_vma=False,
    )
```

```python
import jax
import jax.numpy as jnp
from jax import lax
from jax.experimental import pallas as pl
from jax.experimental.pallas import tpu as pltpu
from jax.sharding import PartitionSpec as P

HD = 64
LOG2E = 1.4426950408889634
SEQ = 256
EPS = 1e-06
MASKED = -1000000000.0
MESH = pl.DeviceIdType.MESH
F32 = jnp.float32
BF16 = jnp.bfloat16
MP = 4
GELU_C = 0.7978845608028654
GELU_A = 0.044715
VMEM_LIMIT = 66_000_000


def nn(a, b):
    return lax.dot_general(a, b, (((1,), (0,)), ((), ())), preferred_element_type=F32)


def nt(a, b):
    return lax.dot_general(a, b, (((1,), (1,)), ((), ())), preferred_element_type=F32)


def tn(a, b):
    return lax.dot_general(a, b, (((0,), (0,)), ((), ())), preferred_element_type=F32)


def xor4(a, b):
    return (a % 2 + b % 2) % 2 + 2 * ((a // 2 + b // 2) % 2)


def places():
    d = lax.axis_index("dp")
    z = lax.axis_index("mp")
    p = d % 8
    kb, xb, yb = p % 2, (p // 2) % 2, (p // 4) % 2
    fc = d + (1 - 2 * kb)
    fx = d + 2 * (1 - 2 * xb)
    fy = d + 4 * (1 - 2 * yb)
    a = fx * (1 - kb) + fy * kb
    b = fy * (1 - kb) + fx * kb
    bit_a = xb * (1 - kb) + yb * kb
    bit_b = yb * (1 - kb) + xb * kb
    return d, z, p, kb, fc, a, b, bit_a, bit_b


def rows_at(start, size):
    return pl.ds(pl.multiple_of(start, size), size)


def norm_parts(h):
    centre = h - jnp.mean(h, axis=-1, keepdims=True)
    inverse = lax.rsqrt(jnp.mean(centre * centre, axis=-1, keepdims=True) + EPS)
    return centre * inverse, inverse


def norm_back(grad, normal, inverse, gain):
    scaled = grad * gain
    return inverse * (
        scaled
        - jnp.mean(scaled, axis=-1, keepdims=True)
        - normal * jnp.mean(scaled * normal, axis=-1, keepdims=True)
    )


def forward_kernel(
    count,
    x_hbm, cot_hbm, seg, wqkv_hbm, wo_hbm, wu_hbm, wd_hbm, bu_hbm, bqv, g1, s1_ref, bo, g2, s2_ref, bd,
    out_hbm, qkvr_hbm, e_hbm, n1_hbm, mixed_hbm, gres_hbm, waf_hbm, gw_ref, small,
    W, BQ, BU, xv, glv, n1v, mixv, acc, gn2, code_q, code_k, rstd, gwu, gwd, stq, str_, ste,
    load_sem, own_sem, stage_sem, out_sem, zsend, send, recv, bsend, brecv,
):
    d, z, p, kb, fc, a, b, bit_a, bit_b = places()
    chunks = count // 512
    rows = count // SEQ

    loads = []
    for c in range(chunks):
        part = pl.ds(c * 512, 512)
        loads.append((
            pltpu.make_async_copy(x_hbm.at[part], xv.at[part], load_sem.at[0, c]),
            pltpu.make_async_copy(cot_hbm.at[part], glv.at[part], load_sem.at[1, c]),
        ))
        loads[-1][0].start()
        loads[-1][1].start()
    own = [
        pltpu.make_async_copy(wqkv_hbm.at[2], W.at[z, pl.ds(0, 192)], own_sem.at[0]),
        pltpu.make_async_copy(wqkv_hbm.at[0], W.at[z, pl.ds(192, 192)], own_sem.at[1]),
        pltpu.make_async_copy(wqkv_hbm.at[1], W.at[z, pl.ds(384, 192)], own_sem.at[2]),
        pltpu.make_async_copy(wo_hbm, W.at[z, pl.ds(576, 192)], own_sem.at[3]),
        pltpu.make_async_copy(bu_hbm, BU.at[z, 0], own_sem.at[4]),
        pltpu.make_async_copy(wu_hbm, W.at[z, pl.ds(768, 768)], own_sem.at[5]),
        pltpu.make_async_copy(wd_hbm, W.at[z, pl.ds(1536, 768)], own_sem.at[6]),
    ]
    for copy in own:
        copy.start()
    BQ[z] = jnp.zeros((2, 256), F32)
    BQ[z, :, 0:192] = bqv[...]

    peers = [(d, xor4(z, s)) for s in (1, 2, 3)] + [(fc, z), (a, z), (b, z)]
    barrier = pltpu.get_barrier_semaphore()
    for peer in peers:
        pl.semaphore_signal(barrier, inc=1, device_id=peer, device_id_type=MESH)
    pl.semaphore_wait(barrier, len(peers))
    for copy in own:
        copy.wait()

    def remote(src, dst, ss, rs, to):
        return pltpu.make_async_remote_copy(
            src_ref=src, dst_ref=dst, send_sem=ss, recv_sem=rs, device_id=to, device_id_type=MESH
        )

    def piece_rows(base, which):
        return pl.ds(pl.multiple_of(base + 96 * which, 96), 96)

    zcopies = []
    for s in (1, 2, 3):
        to = (d, xor4(z, s))
        zcopies.append(remote(BQ.at[z], BQ.at[z], bsend.at[s - 1], brecv.at[s - 1], to))
        zcopies.append(remote(BU.at[z], BU.at[z], bsend.at[s + 2], brecv.at[s + 2], to))
        part = W.at[z, piece_rows(0, p)]
        zcopies.append(remote(part, part, zsend.at[s - 1], recv.at[s - 1, 0], to))
    for s in (1, 2, 3):
        for h in range(2):
            t = 1 + 2 * s + h
            part = W.at[z, piece_rows(768 * (h + 1), p)]
            zcopies.append(remote(part, part, zsend.at[t], recv.at[t, 0], (d, xor4(z, s))))
    for copy in zcopies:
        copy.start()

    def step_of(t):
        late = jnp.maximum(t - 3, 0)
        g = xor4(z, jnp.where(t < 3, t, late // 2) + 1)
        return g, jnp.where(t < 3, 0, 768 + 768 * (late % 2))

    def hop(t, index, which, to):
        g, base = step_of(t)
        part = W.at[g, piece_rows(base, which)]
        return remote(part, part, send.at[t, index], recv.at[t, index], to)

    pa, pb, pc = a % 8, b % 8, fc % 8
    pd = (a + b - d) % 8
    me = (d, z)

    def s1(t):
        hop(t, 0, p, me).wait_recv()
        hop(t, 1, p, (a, z)).start()
        hop(t, 2, p, (b, z)).start()
        hop(t, 3, p, (fc, z)).start()

    def s2(t):
        hop(t, 1, pa, me).wait_recv()
        hop(t, 4, pa, (b, z)).start()
        hop(t, 5, pa, (fc, z)).start()
        hop(t, 2, pb, me).wait_recv()
        hop(t, 6, pb, (fc, z)).start()

    def s3(t):
        hop(t, 4, pd, me).wait_recv()
        hop(t, 7, pd, (fc, z)).start()

    def core_flip(q):
        return q + 1 - 2 * (q % 2)

    def fin(t):
        @pl.when(t < 3)
        def _():
            there = xor4(z, t + 1)
            for ref, first in ((BQ, 0), (BU, 3)):
                block = ref.at[there]
                remote(block, block, bsend.at[first + t], brecv.at[first + t], me).wait_recv()

        hop(t, 3, core_flip(p), me).wait_recv()
        hop(t, 5, core_flip(pb), me).wait_recv()
        hop(t, 6, core_flip(pa), me).wait_recv()
        hop(t, 7, core_flip(pd), me).wait_recv()

    small[...] = jnp.zeros_like(small)
    gain_one, shift_one, b_out, gain_two, shift_two, b_down = (
        ref[...].reshape(1, 768) for ref in (g1, s1_ref, bo, g2, s2_ref, bd)
    )

    lane = (lax.broadcasted_iota(jnp.int32, (SEQ, 128), 1) % HD).astype(F32)

    def head(r, carry):
        part = rows_at(r * SEQ, SEQ)
        normal, inverse = norm_parts(xv[part].astype(F32))
        n1v[part] = (normal * gain_one + shift_one).astype(BF16)
        seg_row = seg[pl.ds(r, 1)].astype(F32)
        seg_col = jnp.broadcast_to(seg_row, (128, SEQ)).T
        same = seg_col == lane
        code_q[part] = jnp.where(same, 0.0, MASKED).astype(BF16)
        code_k[part] = jnp.where(same, 1.0, 0.0).astype(BF16)
        for part6 in range(6):
            lanes = slice(part6 * 128, part6 * 128 + 128)
            masked = jnp.where(seg_col != 0.0, glv[part, lanes].astype(F32), 0.0)
            small[0:1, lanes] += jnp.sum(masked, axis=0, keepdims=True)
            glv[part, lanes] = masked.astype(BF16)
        return carry

    for pair in loads:
        pair[0].wait()
        pair[1].wait()
    lax.fori_loop(0, rows, head, 0)
    save_n1 = pltpu.make_async_copy(n1v, n1_hbm, out_sem.at[0, 0])
    save_n1.start()

    lo = lax.broadcasted_iota(jnp.int32, (SEQ, 128), 1) < HD
    lo_b = lo

    def unit_of(i):
        return xor4(z, i // 4) * 4 + i % 4

    def qkv_copy(slot, i):
        return pltpu.make_async_copy(stq.at[slot], qkvr_hbm.at[unit_of(i), pl.ds(0, 3)], stage_sem.at[0, slot])

    def soft_copies(slot, i):
        u = unit_of(i)
        return (
            pltpu.make_async_copy(str_.at[slot], qkvr_hbm.at[u, 3], stage_sem.at[1, slot]),
            pltpu.make_async_copy(ste.at[slot], e_hbm.at[u], stage_sem.at[2, slot]),
        )

    plan = (
        (s2, (2, 4, 8, 12, 14, 16, 18, 21, 22)),
        (s3, (3, 6, 9, 14, 16, 18, 20, 23, 24)),
        (s1, (1, 2, 5, 9, 11, 13, 15, 18, 20)),
        (fin, (3, 7, 11, 24, 24, 28, 28, 32, 32)),
    )

    def tick(i):
        for action, whens in plan:
            def act(t, carry):
                action(t)
                return carry

            first = sum(jnp.where(i > when, 1, 0) for when in whens)
            lax.fori_loop(first, sum(jnp.where(i >= when, 1, 0) for when in whens), act, 0)

    def project_heads(i, slot):
        g = xor4(z, i // 4 % 4)
        n1c = n1v[rows_at(i % 4 * 512, 512)]
        stq[slot, 0] = (nt(n1c, W[g, 0:256]) + BQ[g, 1:2]).astype(BF16)
        stq[slot, 1] = ((nt(n1c, W[g, 192:448]) + BQ[g, 0:1]) * (0.125 * LOG2E)).astype(BF16)
        stq[slot, 2] = nt(n1c, W[g, 384:640]).astype(BF16)

    def attend(i, slot):
        g, c = xor4(z, i // 4), i % 4
        one = jnp.ones((SEQ, 128), BF16)
        for r in range(2):
            tr = slice(r * SEQ, r * SEQ + SEQ)
            dst = rows_at(c * 512 + r * SEQ, SEQ)
            cq, ck = code_q[dst], code_k[dst]

            def weights(qp, kp, h):
                sc = nt(qp, kp)
                e = jnp.exp2(sc - jnp.max(sc, axis=-1, keepdims=True)).astype(BF16)
                ste[slot, r * 3 + h] = e
                return e

            vp, qp, kp = (stq[slot, n, tr, 0:128] for n in range(3))
            e0 = weights(jnp.where(lo_b, qp, cq), jnp.where(lo_b, kp, ck), 0)
            o0 = nn(e0, jnp.where(lo_b, vp, one))
            e1 = weights(jnp.where(lo_b, cq, qp), jnp.where(lo_b, ck, kp), 1)
            o1 = nn(e1, jnp.where(lo_b, one, vp))
            r01 = 1.0 / pltpu.roll(jnp.where(lo, o1, o0), 64, 1)
            mix01 = jnp.where(lo, o0, o1) * r01
            vp, qp, kp = (stq[slot, n, tr, 128:256] for n in range(3))
            e2 = weights(jnp.where(lo_b, qp, cq), jnp.where(lo_b, kp, ck), 2)
            o2 = nn(e2, jnp.where(lo_b, vp, one))
            r2 = 1.0 / jnp.where(lo, pltpu.roll(o2, 64, 1), 1.0)
            mix2 = jnp.where(lo, o2 * r2, 0.0)
            mixv[g, dst, 0:128] = mix01.astype(BF16)
            mixv[g, dst, 128:256] = mix2.astype(BF16)
            str_[slot, tr, 0:128] = r01.astype(BF16)
            str_[slot, tr, 128:256] = r2.astype(BF16)

    def attend_pair(pair, carry):
        for slot in range(2):
            i = 2 * pair + slot
            tick(i)

            @pl.when(i >= 2)
            def _():
                for copy in soft_copies(slot, i):
                    copy.wait()

            @pl.when(i >= 1)
            def _():
                qkv_copy(1 - slot, i).wait()

            project_heads(i + 1, 1 - slot)
            attend(i, slot)
            for copy in soft_copies(slot, i):
                copy.start()

            @pl.when(i + 1 < 4 * chunks)
            def _():
                qkv_copy(1 - slot, i + 1).start()

        return carry

    project_heads(0, 0)
    qkv_copy(0, 0).start()
    lax.fori_loop(0, 2 * chunks, attend_pair, 0)
    qkv_copy(1, 0).wait()
    for slot in range(2):
        for copy in soft_copies(slot, 0):
            copy.wait()
    save_n1.wait()
    save_mixed = pltpu.make_async_copy(mixv, mixed_hbm, out_sem.at[0, 0])
    save_mixed.start()
    save_wa = pltpu.make_async_copy(W.at[:, pl.ds(0, 768)], waf_hbm, out_sem.at[1, 0])
    save_wa.start()

    def project(c, carry):
        tick(4 * chunks + c)
        tok = rows_at(c * 512, 512)
        total = nn(mixv[0, tok, 0:192], W[0, 576:768])
        for g in range(1, MP):
            total = total + nn(mixv[g, tok, 0:192], W[g, 576:768])
        hidden = xv[tok].astype(F32) + total + b_out
        acc[tok] = hidden
        normal, inverse = norm_parts(hidden)
        xv[tok] = normal.astype(BF16)
        rstd[tok] = inverse
        n1v[tok] = (normal * gain_two + shift_two).astype(BF16)
        gn2[tok] = jnp.zeros((512, 768), F32)
        return carry

    lax.fori_loop(0, chunks, project, 0)
    gwu[...] = jnp.zeros_like(gwu)
    gwd[...] = jnp.zeros_like(gwd)

    def feed(j, carry):
        tick(5 * chunks + j)
        g, c = xor4(z, j // 4), j % 4
        tok = rows_at(c * 512, 512)
        n2c = n1v[tok]
        glc = glv[tok]
        acts, lows, sums = [], [], []
        for n in range(3):
            cols = slice(n * 256, n * 256 + 256)
            pre = nn(n2c, W[g, 768:1536, cols]) + BU[g, 0:1, cols]
            grad_act = nt(glc, W[g, 1536 + n * 256 : 1792 + n * 256])
            square = pre * pre
            t = jnp.tanh(pre * (GELU_C + (GELU_C * GELU_A) * square))
            half = 0.5 + 0.5 * t
            slope = half + pre * (0.5 - 0.5 * (t * t)) * (GELU_C + (3.0 * GELU_C * GELU_A) * square)
            grad_pre = grad_act * slope
            acts.append((pre * half).astype(BF16))
            lows.append(grad_pre.astype(BF16))
            sums.append(jnp.sum(grad_pre, axis=0, keepdims=True))
        act = jnp.concatenate(acts, axis=1)
        low = jnp.concatenate(lows, axis=1)
        acc[tok] += nn(act, W[g, 1536:2304])
        gn2[tok] += nt(low, W[g, 768:1536])

        @pl.when(g == z)
        def _():
            gwu[...] += tn(n2c, low)
            gwd[...] += tn(act, glc)
            for n in range(3):
                small[1:2, n * 256 : n * 256 + 256] += sums[n]

        return carry

    lax.fori_loop(0, MP * chunks, feed, 0)
    gw_ref[0:768] = gwu[...].astype(BF16)
    gw_ref[768:1536] = gwd[...].astype(BF16)

    def closed_copies(r):
        tok = rows_at(r * SEQ, SEQ)
        return (
            pltpu.make_async_copy(xv.at[tok], out_hbm.at[tok], out_sem.at[0, 1 + r]),
            pltpu.make_async_copy(glv.at[tok], gres_hbm.at[tok], out_sem.at[1, 1 + r]),
        )

    def close(r, carry):
        tok = rows_at(r * SEQ, SEQ)
        normal = xv[tok].astype(F32)
        xv[tok] = (acc[tok] + b_down).astype(BF16)
        grad = gn2[tok]
        small[2:3] += jnp.sum(grad * normal, axis=0, keepdims=True)
        small[3:4] += jnp.sum(grad, axis=0, keepdims=True)
        total = glv[tok].astype(F32) + norm_back(grad, normal, rstd[tok], gain_two)
        small[4:5] += jnp.sum(total, axis=0, keepdims=True)
        glv[tok] = total.astype(BF16)
        for copy in closed_copies(r):
            copy.start()
        return carry

    lax.fori_loop(0, rows, close, 0)
    for copy in zcopies:
        copy.wait_send()
    for t in range(9):
        hop(t, 1, p, (a, z)).wait_send()
        hop(t, 2, p, (b, z)).wait_send()
        hop(t, 3, p, (fc, z)).wait_send()
        hop(t, 4, pa, (b, z)).wait_send()
        hop(t, 5, pa, (fc, z)).wait_send()
        hop(t, 6, pb, (fc, z)).wait_send()
        hop(t, 7, pd, (fc, z)).wait_send()
    save_mixed.wait()
    save_wa.wait()

    def closed(r, carry):
        for copy in closed_copies(r):
            copy.wait()
        return carry

    lax.fori_loop(0, rows, closed, 0)


def backward_kernel(
    count, extra,
    qkvr_hbm, e_hbm, n1_hbm, mixed_hbm, gres_hbm, x_hbm, waf_hbm, gw_hbm, small_in, g1,
    ig_hbm, gw_out, ga_out, small,
    WA, n1v, mixv, gresv, xv, dqkv, stq, ste,
    cur_w, ag_w, rec_w, cur_a, ag_a, rec_a, ga, head, head_rec, tail, tail_rec,
    load_sem, stage_sem, out_sem, row_sem, rs_send, rs_recv, ag_send, ag_recv, sm_send, sm_recv,
):
    d, z, p, kb, fc, a, b, bit_a, bit_b = places()
    xb, yb = p // 2 % 2, p // 4
    chunks = count // 512

    def load(src, dst, n):
        return pltpu.make_async_copy(src, dst, load_sem.at[n])

    top, rest = pl.ds(0, 512), pl.ds(512, count - 512)
    load_first = [
        load(waf_hbm.at[:, pl.ds(576, 192)], WA.at[:, pl.ds(576, 192)], 0),
        load(gres_hbm.at[top], gresv.at[top], 1),
        load(mixed_hbm.at[z], mixv.at[z], 2),
    ]
    load_grads = load(gw_hbm, cur_w, 3)
    load_next = [load(gres_hbm.at[rest], gresv.at[rest], 4)] + [
        load(mixed_hbm.at[xor4(z, s)], mixv.at[xor4(z, s)], 4 + s) for s in (1, 2, 3)
    ]
    load_n1 = load(n1_hbm, n1v, 8)
    load_last = [
        load(waf_hbm.at[:, pl.ds(0, 576)], WA.at[:, pl.ds(0, 576)], 9),
        load(x_hbm, xv, 10),
    ]

    def unit_of(i):
        return xor4(z, i // 4) * 4 + i % 4

    def fetch(i, slot):
        u = unit_of(i)
        return (
            pltpu.make_async_copy(qkvr_hbm.at[u], stq.at[slot], stage_sem.at[0, slot]),
            pltpu.make_async_copy(e_hbm.at[u], ste.at[slot], stage_sem.at[1, slot]),
        )

    for copy in fetch(0, 0):
        copy.start()
    for copy in load_first + [load_grads] + load_next + [load_n1] + load_last:
        copy.start()

    partners = [fc, a, b]
    bits = [kb, bit_a, bit_b]
    for m in range(extra):
        step = 8 << m
        partners.append(d + step * (1 - 2 * ((d // step) % 2)))
    peers = [
        d - p + (1 - kb if k % 2 else kb) + 2 * (1 - xb if k // 2 % 2 else xb) + 4 * (1 - yb if k // 4 else yb)
        for k in range(1, 8)
    ]
    barrier = pltpu.get_barrier_semaphore()
    for peer in peers + partners[3:]:
        pl.semaphore_signal(barrier, inc=1, device_id=(peer, z), device_id_type=MESH)
    pl.semaphore_wait(barrier, 7 + extra)

    def remote(src, dst, ss, rs, to):
        return pltpu.make_async_remote_copy(
            src_ref=src, dst_ref=dst, send_sem=ss, recv_sem=rs, device_id=to, device_id_type=MESH
        )

    class Reduce:
        def __init__(self, which, height, cur, ag, rec):
            self.which, self.cur, self.ag, self.rec = which, cur, ag, rec
            self.half = [height // 2, height // 4, height // 8]
            self.off = [0]
            for k in range(3):
                self.off.append(self.off[k] + bits[k] * self.half[k])
            self.place = [0, self.half[0], self.half[0] + self.half[1]]

        def at(self, ref, start, size):
            if isinstance(start, int):
                return ref.at[pl.ds(start, size)]
            return ref.at[pl.ds(pl.multiple_of(start, 32), size)]

        def rs(self, k):
            theirs = self.off[k] + (1 - bits[k]) * self.half[k]
            return remote(
                self.at(self.cur, theirs, self.half[k]),
                self.at(self.rec, self.place[k], self.half[k]),
                rs_send.at[self.which, k], rs_recv.at[self.which, k], (partners[k], z),
            )

        def send(self, k):
            self.rs(k).start()

        def add(self, start, place, size):
            for q in range(size // 96):
                mine = pl.ds(pl.multiple_of(start + q * 96, 32), 96)
                other = self.rec[place + q * 96 : place + q * 96 + 96]
                self.cur[mine] = (self.cur[mine].astype(F32) + other.astype(F32)).astype(BF16)

        def take(self, k):
            self.rs(k).wait_recv()
            self.add(self.off[k + 1], self.place[k], self.half[k])

        def middle(self):
            size = self.half[2]
            block = self.at(self.cur, self.off[3], size)
            for m in range(extra):
                place = self.place[2] + size * (m + 1)
                copy = remote(
                    block, self.at(self.rec, place, size),
                    rs_send.at[self.which, 3 + m], rs_recv.at[self.which, 3 + m], (partners[3 + m], z),
                )
                copy.start()
                copy.wait()
                self.add(self.off[3], place, size)
            mine = pl.ds(pl.multiple_of(self.off[3], 32), size)
            self.ag[mine] = self.cur[mine]

        def gather(self, k, start):
            part = self.at(self.ag, start, self.half[k])
            return remote(part, part, ag_send.at[self.which, k], ag_recv.at[self.which, k], (partners[k], z))

        def give(self, k):
            self.gather(k, self.off[k + 1]).start()

        def get(self, k):
            self.gather(k, self.off[k] + (1 - bits[k]) * self.half[k]).wait_recv()

        def drain(self):
            for k in range(3):
                self.rs(k).wait_send()
                self.gather(k, self.off[k + 1]).wait_send()

    big = Reduce(0, 1536, cur_w, ag_w, rec_w)
    att = Reduce(1, 768, cur_a, ag_a, rec_a)

    load_grads.wait()
    big.send(0)
    small[...] = small_in[...]
    tail[...] = jnp.zeros_like(tail)
    gain_one = g1[...].reshape(1, 768)
    lo = lax.broadcasted_iota(jnp.int32, (SEQ, 128), 1) < HD
    spread = (
        lax.broadcasted_iota(jnp.int32, (192, 384), 0) // HD
        == lax.broadcasted_iota(jnp.int32, (192, 384), 1) // 128
    ).astype(F32).astype(BF16)
    for copy in load_first:
        copy.wait()

    def own_ready():
        load_n1.wait()
        n1c = n1v[...]
        for c in range(3):
            ga[c * 192 : c * 192 + 192] = tn(dqkv[c, z, :, 0:192], n1c)
        ga[576:768] = tn(mixv[z, :, 0:192], gresv[...])
        for n, c in ((6, 1), (7, 0)):
            small[n : n + 1, 0:256] = jnp.sum(dqkv[c, z].astype(F32), axis=0, keepdims=True)
        cur_a[...] = ga[...].astype(BF16)
        att.send(0)

    def next_ready():
        for copy in load_next:
            copy.wait()

    plan = {
        1: next_ready,
        2: lambda: (big.take(0), big.send(1)),
        4: own_ready,
        6: lambda: (big.take(1), big.send(2)),
        7: lambda: (att.take(0), att.send(1)),
        9: lambda: (big.take(2), big.middle(), big.give(2)),
        10: lambda: (att.take(1), att.send(2)),
        12: lambda: (big.get(2), big.give(1)),
        13: lambda: (att.take(2), att.middle(), att.give(2)),
        15: lambda: (att.get(2),),
    }

    def unit(i, carry):
        for when, action in plan.items():
            @pl.when(i == when)
            def _():
                action()

        slot = i % 2
        for copy in fetch(i, slot):
            copy.wait()

        @pl.when(i + 1 < 4 * chunks)
        def _():
            for copy in fetch(i + 1, 1 - slot):
                copy.start()

        g, c = xor4(z, i // 4), i % 4
        tok = rows_at(c * 512, 512)
        low = gresv[tok]
        mixed = mixv[g, tok, 0:192]
        grad_mixed = nt(low, WA[g, 576:768]).astype(BF16).astype(F32)

        scaled = (grad_mixed * stq[slot, 3, :, 0:192].astype(F32)).astype(BF16)
        delta = nn((scaled.astype(F32) * mixed.astype(F32)).astype(BF16), spread)
        zero = jnp.zeros((SEQ, 128), BF16)
        for r in range(2):
            tr = slice(r * SEQ, r * SEQ + SEQ)
            dst = rows_at(c * 512 + r * SEQ, SEQ)
            vp, qp, kp = (stq[slot, n, tr, 0:128] for n in range(3))
            dp = scaled[tr, 0:128]
            res = []
            for h in range(2):
                e = ste[slot, r * 3 + h]
                mine = jnp.where(lo, vp, zero) if h == 0 else jnp.where(lo, zero, vp)
                dh = delta[tr, h * 128 : h * 128 + 128]
                grad = nt(dp, mine) - jnp.concatenate([dh, dh], axis=1)
                ds = (e.astype(F32) * grad).astype(BF16)
                res.append((tn(e, dp), nn(ds, kp), tn(ds, qp)))
            pairs = [jnp.where(lo, x0, x1) for x0, x1 in zip(res[0], res[1])]
            dv, dq, dk = pairs[0], pairs[1] * 0.125, pairs[2] * (1.0 / LOG2E)
            for n, value in enumerate((dv, dq, dk)):
                dqkv[n, g, dst, 0:128] = value.astype(BF16)

            v2, q2, k2 = (stq[slot, n, tr, 128:192] for n in range(3))
            d2 = scaled[tr, 128:192]
            e = ste[slot, r * 3 + 2]
            dh = delta[tr, 256:384]
            ds = (e.astype(F32) * (nt(d2, v2) - jnp.concatenate([dh, dh], axis=1))).astype(BF16)
            dv2, dq2, dk2 = tn(e, d2), nn(ds, k2) * 0.125, tn(ds, q2) * (1.0 / LOG2E)
            for n, value in enumerate((dv2, dq2, dk2)):
                dqkv[n, g, dst, 128:192] = value.astype(BF16)

        return carry

    lax.fori_loop(0, 4 * chunks, unit, 0)
    att.give(1)

    def exchange(ref, rec, which):
        mine = [remote(ref, rec.at[p], sm_send.at[which, k], sm_recv.at[which, p], (peer, z)) for k, peer in enumerate(peers)]
        for copy in mine:
            copy.start()
        return mine

    def total_of(ref, rec, which, mine):
        for copy in mine:
            copy.wait_send()
        for k, peer in enumerate(peers):
            other = peer - (d - p)
            remote(ref, rec.at[other], sm_send.at[which, k], sm_recv.at[which, other], (peer, z)).wait_recv()
        rec[p] = ref[...]
        ref[...] = sum(rec[k] for k in range(1, 8)) + rec[0]
        for m in range(extra):
            copy = remote(ref, rec.at[8 + m], sm_send.at[which, 7 + m], sm_recv.at[which, 8 + m], (partners[3 + m], z))
            copy.start()
            copy.wait()
            ref[...] += rec[8 + m]

    head[...] = small[0:8]
    sent_head = exchange(head, head_rec, 0)
    for copy in load_last:
        copy.wait()

    def save_rows(c):
        tok = rows_at(c * 512, 512)
        return pltpu.make_async_copy(xv.at[tok], ig_hbm.at[tok], row_sem.at[c])

    def last(c, carry):
        @pl.when(c == 1)
        def _():
            big.get(1)
            big.give(0)

        @pl.when(c == 3)
        def _():
            att.get(1)
            att.give(0)

        tok = rows_at(c * 512, 512)
        total = nn(dqkv[0, 0, tok, 0:192], WA[0, 0:192])
        for g in range(MP):
            for n in range(3):
                if g + n > 0:
                    total = total + nn(dqkv[n, g, tok, 0:192], WA[g, n * 192 : n * 192 + 192])
        normal, inverse = norm_parts(xv[tok].astype(F32))
        tail[0:1] += jnp.sum(total * normal, axis=0, keepdims=True)
        tail[1:2] += jnp.sum(total, axis=0, keepdims=True)
        xv[tok] = (gresv[tok].astype(F32) + norm_back(total, normal, inverse, gain_one)).astype(BF16)
        save_rows(c).start()
        return carry

    lax.fori_loop(0, chunks, last, 0)

    sent_tail = exchange(tail, tail_rec, 1)
    big.get(0)
    save_w = pltpu.make_async_copy(ag_w, gw_out, out_sem.at[0])
    save_w.start()
    att.get(0)
    save_a = pltpu.make_async_copy(ag_a, ga_out, out_sem.at[2])
    save_a.start()
    total_of(head, head_rec, 0, sent_head)
    small[0:8] = head[...]
    total_of(tail, tail_rec, 1, sent_tail)
    small[8:10] = tail[...]
    big.drain()
    att.drain()
    save_w.wait()
    for c in range(chunks):
        save_rows(c).wait()
    save_a.wait()


def finish_kernel(
    bo_in, ig_in, gw_in, ga_in, small,
    bo_out, ig_out, gqkv, gbqv, gwo, gwu, gwd, g_b_out, g_gain_one, g_shift_one, g_b_up, g_b_down, g_gain_two, g_shift_two,
    bov, igv, gwv, gav, fw, fa, in_sem, out_sem,
):
    half = bov.shape[0] // 2
    load_w = [
        pltpu.make_async_copy(gw_in.at[pl.ds(768 * h, 768)], gwv.at[pl.ds(768 * h, 768)], in_sem.at[h]) for h in range(2)
    ]
    load_a = pltpu.make_async_copy(ga_in, gav, in_sem.at[2])
    load_rows = []
    for src, buf, dst in ((bo_in, bov, bo_out), (ig_in, igv, ig_out)):
        for q in range(4):
            part = pl.ds(q * (half // 2), half // 2)
            copy = pltpu.make_async_copy(src.at[part], buf.at[part], in_sem.at[3 + len(load_rows)])
            load_rows.append((copy, buf.at[part], dst.at[part]))
    for copy in load_w + [load_a] + [rows[0] for rows in load_rows]:
        copy.start()
    gbqv[...] = small[6:8, 0 : gbqv.shape[1]]
    for ref, n in ((g_b_out, 4), (g_gain_one, 8), (g_shift_one, 9), (g_b_up, 1), (g_b_down, 0), (g_gain_two, 2), (g_shift_two, 3)):
        ref[...] = small[n : n + 1].reshape(768)
    saves = []

    def save(src, dst):
        saves.append(pltpu.make_async_copy(src, dst, out_sem.at[len(saves)]))
        saves[-1].start()

    for h, dst in enumerate((gwu, gwd)):
        load_w[h].wait()
        for q in range(2):
            part = pl.ds(768 * h + 384 * q, 384)
            fw[part] = gwv[part].astype(F32)
            save(fw.at[part], dst.at[pl.ds(384 * q, 384)])
    load_a.wait()
    for n, dst in enumerate((gqkv.at[2], gqkv.at[0], gqkv.at[1], gwo)):
        part = pl.ds(192 * n, 192)
        fa[part] = gav[part].astype(F32)
        save(fa.at[part], dst)
    for copy, buf, dst in load_rows:
        copy.wait()
        save(buf, dst)
    for copy in saves:
        copy.wait()


def layer(n_dp, tokens, segment_ids, cotangent, w_qkv, b_qv, w_out, b_out, gain_one, shift_one, w_up, b_up, w_down, b_down, gain_two, shift_two):
    count, width = tokens.shape[0], w_qkv.shape[2]
    rows = segment_ids.shape[0]
    units = MP * (count // 512)
    extra = (n_dp // 8).bit_length() - 1
    any_space = pl.BlockSpec(memory_space=pl.ANY)
    in_vmem = pl.BlockSpec(memory_space=pltpu.VMEM)
    wt = jnp.transpose(w_qkv, (0, 2, 1))
    dma = pltpu.SemaphoreType.DMA

    def sds(shape, dtype):
        return jax.ShapeDtypeStruct(shape, dtype)

    def fwd(*refs):
        return forward_kernel(count, *refs)

    block_out, qkvr, e, n1, mixed, gres, waf, gw, small = pl.pallas_call(
        fwd,
        name="forward",
        out_shape=(
            sds((count, 768), BF16),
            sds((units, 4, 512, 256), BF16),
            sds((units, 6, SEQ, SEQ), BF16),
            sds((count, 768), BF16),
            sds((MP, count, 256), BF16),
            sds((count, 768), BF16),
            sds((MP, 768, 768), BF16),
            sds((1536, 768), BF16),
            sds((16, 768), F32),
        ),
        in_specs=[any_space, any_space, in_vmem] + [any_space] * 5 + [in_vmem] * 7,
        out_specs=(any_space,) * 7 + (in_vmem, in_vmem),
        scratch_shapes=[
            pltpu.VMEM((MP, 2304, 768), BF16),
            pltpu.VMEM((MP, 2, 256), F32),
            pltpu.VMEM((MP, 1, 768), F32),
            pltpu.VMEM((count, 768), BF16),
            pltpu.VMEM((count, 768), BF16),
            pltpu.VMEM((count, 768), BF16),
            pltpu.VMEM((MP, count, 256), BF16),
            pltpu.VMEM((count, 768), F32),
            pltpu.VMEM((count, 768), F32),
            pltpu.VMEM((count, 128), BF16),
            pltpu.VMEM((count, 128), BF16),
            pltpu.VMEM((count, 1), F32),
            pltpu.VMEM((768, 768), F32),
            pltpu.VMEM((768, 768), F32),
            pltpu.VMEM((2, 3, 512, 256), BF16),
            pltpu.VMEM((2, 512, 256), BF16),
            pltpu.VMEM((2, 6, SEQ, SEQ), BF16),
            dma((2, count // 512)), dma((7,)), dma((3, 2)), dma((2, 1 + rows)),
            dma((9,)), dma((9, 8)), dma((9, 8)), dma((6,)), dma((6,)),
        ],
        compiler_params=pltpu.CompilerParams(collective_id=0, has_side_effects=True, vmem_limit_bytes=VMEM_LIMIT),
    )(
        tokens, cotangent, segment_ids, wt, w_out, w_up, w_down, b_up, b_qv,
        gain_one, shift_one, b_out, gain_two, shift_two, b_down,
    )

    def bwd(*refs):
        return backward_kernel(count, extra, *refs)

    input_grad, gw_full, ga_full, small = pl.pallas_call(
        bwd,
        name="backward",
        out_shape=(
            sds((count, 768), BF16),
            sds((1536, 768), BF16),
            sds((768, 768), BF16),
            sds((16, 768), F32),
        ),
        in_specs=[any_space] * 8 + [in_vmem, in_vmem],
        out_specs=(any_space,) * 3 + (in_vmem,),
        scratch_shapes=[
            pltpu.VMEM((MP, 768, 768), BF16),
            pltpu.VMEM((count, 768), BF16),
            pltpu.VMEM((MP, count, 256), BF16),
            pltpu.VMEM((count, 768), BF16),
            pltpu.VMEM((count, 768), BF16),
            pltpu.VMEM((3, MP, count, 256), BF16),
            pltpu.VMEM((2, 4, 512, 256), BF16),
            pltpu.VMEM((2, 6, SEQ, SEQ), BF16),
            pltpu.VMEM((1536, 768), BF16),
            pltpu.VMEM((1536, 768), BF16),
            pltpu.VMEM((1344 + 192 * extra, 768), BF16),
            pltpu.VMEM((768, 768), BF16),
            pltpu.VMEM((768, 768), BF16),
            pltpu.VMEM((672 + 96 * extra, 768), BF16),
            pltpu.VMEM((768, 768), F32),
            pltpu.VMEM((8, 768), F32),
            pltpu.VMEM((8 + extra, 8, 768), F32),
            pltpu.VMEM((2, 768), F32),
            pltpu.VMEM((8 + extra, 2, 768), F32),
            dma((11,)), dma((2, 2)), dma((3,)), dma((count // 512,)),
            dma((2, 3 + extra)), dma((2, 3 + extra)), dma((2, 3)), dma((2, 3)),
            dma((2, 7 + extra)), dma((2, 8 + extra)),
        ],
        compiler_params=pltpu.CompilerParams(collective_id=1, has_side_effects=True, vmem_limit_bytes=VMEM_LIMIT),
    )(qkvr, e, n1, mixed, gres, tokens, waf, gw, small, gain_one)

    row = sds((768,), F32)
    block_out, input_grad, grad_qkv, b_qv_grad, grad_out, grad_up, grad_down, *vectors = pl.pallas_call(
        finish_kernel,
        name="finish",
        out_shape=(
            sds((count, 768), BF16), sds((count, 768), BF16), sds((3, width, 768), F32), sds((2, width), F32),
            sds((width, 768), F32), sds((768, 768), F32), sds((768, 768), F32),
        ) + (row,) * 7,
        in_specs=[any_space] * 4 + [in_vmem],
        out_specs=(any_space,) * 3 + (in_vmem,) + (any_space,) * 3 + (in_vmem,) * 7,
        scratch_shapes=[
            pltpu.VMEM((count, 768), BF16), pltpu.VMEM((count, 768), BF16),
            pltpu.VMEM((1536, 768), BF16), pltpu.VMEM((768, 768), BF16),
            pltpu.VMEM((1536, 768), F32), pltpu.VMEM((768, 768), F32),
            dma((11,)), dma((16,)),
        ],
        compiler_params=pltpu.CompilerParams(vmem_limit_bytes=VMEM_LIMIT),
    )(block_out, input_grad, gw_full, ga_full, small)
    g_b_out, g_gain_one, g_shift_one, g_b_up, g_b_down, g_gain_two, g_shift_two = vectors
    return (
        block_out,
        input_grad,
        jnp.transpose(grad_qkv, (0, 2, 1)),
        b_qv_grad,
        grad_out,
        g_b_out,
        g_gain_one,
        g_shift_one,
        grad_up,
        g_b_up,
        grad_down,
        g_b_down,
        g_gain_two,
        g_shift_two,
    )


def solution(mesh):
    n_dp = mesh.shape["dp"]

    def run(*args):
        return layer(n_dp, *args)

    placed = (
        P("dp", None), P("dp", None), P("dp", None), P(None, None, "mp"), P(None, "mp"), P("mp", None), P(), P(), P(),
        P(None, "mp"), P("mp"), P("mp", None), P(), P(), P(),
    )
    return jax.shard_map(
        run,
        mesh=mesh,
        in_specs=placed,
        out_specs=(
            P("dp", None), P("dp", None), P(None, None, "mp"), P(None, "mp"), P("mp", None), P(), P(), P(),
            P(None, "mp"), P("mp"), P("mp", None), P(), P(), P(),
        ),
        check_vma=False,
    )
```

```python
import jax
import jax.numpy as jnp
from jax import lax
from jax.experimental import pallas as pl
from jax.experimental.pallas import tpu as pltpu
from jax.sharding import PartitionSpec as P

HD = 64
LOG2E = 1.4426950408889634
SEQ = 256
EPS = 1e-06
MASKED = -1000000000.0
MESH = pl.DeviceIdType.MESH
F32 = jnp.float32
BF16 = jnp.bfloat16
MP = 4
GELU_C = 0.7978845608028654
GELU_A = 0.044715
VMEM_LIMIT = 66_000_000
KINDS = {"heads": (0, 3, 72), "out": (9, 12, 24), "hidden": (3, 9, 96)}


def nn(a, b):
    return lax.dot_general(a, b, (((1,), (0,)), ((), ())), preferred_element_type=F32)


def nt(a, b):
    return lax.dot_general(a, b, (((1,), (1,)), ((), ())), preferred_element_type=F32)


def tn(a, b):
    return lax.dot_general(a, b, (((0,), (0,)), ((), ())), preferred_element_type=F32)


def xor4(a, b):
    return (a % 2 + b % 2) % 2 + 2 * ((a // 2 + b // 2) % 2)


def places():
    d = lax.axis_index("dp")
    z = lax.axis_index("mp")
    p = d % 8
    kb, xb, yb = p % 2, (p // 2) % 2, (p // 4) % 2
    fc = d + (1 - 2 * kb)
    fx = d + 2 * (1 - 2 * xb)
    fy = d + 4 * (1 - 2 * yb)
    a = fx * (1 - kb) + fy * kb
    b = fy * (1 - kb) + fx * kb
    bit_a = xb * (1 - kb) + yb * kb
    bit_b = yb * (1 - kb) + xb * kb
    return d, z, p, kb, fc, a, b, bit_a, bit_b


def rows_at(start, size):
    return pl.ds(pl.multiple_of(start, size), size)


def norm_parts(h):
    centre = h - jnp.mean(h, axis=-1, keepdims=True)
    inverse = lax.rsqrt(jnp.mean(centre * centre, axis=-1, keepdims=True) + EPS)
    return centre * inverse, inverse


def norm_back(grad, normal, inverse, gain):
    scaled = grad * gain
    return inverse * (
        scaled
        - jnp.mean(scaled, axis=-1, keepdims=True)
        - normal * jnp.mean(scaled * normal, axis=-1, keepdims=True)
    )


def forward_kernel(
    count,
    x_hbm, cot_hbm, seg, wqkv_hbm, wo_hbm, wu_hbm, wd_hbm, bu_hbm, bqv, g1, s1_ref, bo, g2, s2_ref, bd,
    out_hbm, qkvr_hbm, e_hbm, n1_hbm, mixed_hbm, gres_hbm, waf_hbm, gw_ref, small,
    W, BQ, BU, xv, glv, n1v, mixv, acc, gn2, code_q, code_k, rstd, gwu, gwd, stq, str_, ste,
    load_sem, own_sem, stage_sem, out_sem, zsend, send, recv, bsend, brecv,
):
    d, z, p, kb, fc, a, b, bit_a, bit_b = places()
    chunks = count // 512
    rows = count // SEQ

    loads = []
    for c in range(chunks):
        part = pl.ds(c * 512, 512)
        loads.append((
            pltpu.make_async_copy(x_hbm.at[part], xv.at[part], load_sem.at[0, c]),
            pltpu.make_async_copy(cot_hbm.at[part], glv.at[part], load_sem.at[1, c]),
        ))
        loads[-1][0].start()
        loads[-1][1].start()
    own = [
        pltpu.make_async_copy(wqkv_hbm.at[2], W.at[z, pl.ds(0, 192)], own_sem.at[0]),
        pltpu.make_async_copy(wqkv_hbm.at[0], W.at[z, pl.ds(192, 192)], own_sem.at[1]),
        pltpu.make_async_copy(wqkv_hbm.at[1], W.at[z, pl.ds(384, 192)], own_sem.at[2]),
        pltpu.make_async_copy(wo_hbm, W.at[z, pl.ds(576, 192)], own_sem.at[3]),
        pltpu.make_async_copy(bu_hbm, BU.at[z, 0], own_sem.at[4]),
        pltpu.make_async_copy(wu_hbm, W.at[z, pl.ds(768, 768)], own_sem.at[5]),
        pltpu.make_async_copy(wd_hbm, W.at[z, pl.ds(1536, 768)], own_sem.at[6]),
    ]
    for copy in own:
        copy.start()
    BQ[z] = jnp.zeros((2, 256), F32)
    BQ[z, :, 0:192] = bqv[...]

    peers = [(d, xor4(z, s)) for s in (1, 2, 3)] + [(fc, z), (a, z), (b, z)]
    barrier = pltpu.get_barrier_semaphore()
    for peer in peers:
        pl.semaphore_signal(barrier, inc=1, device_id=peer, device_id_type=MESH)
    pl.semaphore_wait(barrier, len(peers))
    for copy in own:
        copy.wait()

    def remote(src, dst, ss, rs, to):
        return pltpu.make_async_remote_copy(
            src_ref=src, dst_ref=dst, send_sem=ss, recv_sem=rs, device_id=to, device_id_type=MESH
        )

    def piece_rows(base, size, which):
        return pl.ds(pl.multiple_of(base + size * which, 8), size)

    def step_of(kind, t):
        if kind == "heads":
            return xor4(z, t + 1), 0
        if kind == "out":
            return xor4(z, t - 8), 576
        return xor4(z, (t - 3) // 2 + 1), 768 + 768 * ((t - 3) % 2)

    zcopies = []
    for s in (1, 2, 3):
        to = (d, xor4(z, s))
        zcopies.append(remote(BQ.at[z], BQ.at[z], bsend.at[s - 1], brecv.at[s - 1], to))
        zcopies.append(remote(BU.at[z], BU.at[z], bsend.at[s + 2], brecv.at[s + 2], to))
    for kind, (first, last, size) in KINDS.items():
        for t in range(first, last):
            part = W.at[z, piece_rows(step_of(kind, t)[1], size, p)]
            zcopies.append(remote(part, part, zsend.at[t], recv.at[t, 0], (d, step_of(kind, t)[0])))
    for copy in zcopies:
        copy.start()

    def hop(kind, t, index, which, to):
        g, base = step_of(kind, t)
        part = W.at[g, piece_rows(base, KINDS[kind][2], which)]
        return remote(part, part, send.at[t, index], recv.at[t, index], to)

    pa, pb, pc = a % 8, b % 8, fc % 8
    pd = (a + b - d) % 8
    me = (d, z)

    def s1(kind, t):
        hop(kind, t, 0, p, me).wait_recv()
        hop(kind, t, 1, p, (a, z)).start()
        hop(kind, t, 2, p, (b, z)).start()
        hop(kind, t, 3, p, (fc, z)).start()

    def s2(kind, t):
        hop(kind, t, 1, pa, me).wait_recv()
        hop(kind, t, 4, pa, (b, z)).start()
        hop(kind, t, 5, pa, (fc, z)).start()
        hop(kind, t, 2, pb, me).wait_recv()
        hop(kind, t, 6, pb, (fc, z)).start()

    def s3(kind, t):
        hop(kind, t, 4, pd, me).wait_recv()
        hop(kind, t, 7, pd, (fc, z)).start()

    def core_flip(q):
        return q + 1 - 2 * (q % 2)

    def fin(kind, t):
        if kind == "heads":
            there = xor4(z, t + 1)
            for ref, first in ((BQ, 0), (BU, 3)):
                block = ref.at[there]
                remote(block, block, bsend.at[first + t], brecv.at[first + t], me).wait_recv()

        hop(kind, t, 3, core_flip(p), me).wait_recv()
        hop(kind, t, 5, core_flip(pb), me).wait_recv()
        hop(kind, t, 6, core_flip(pa), me).wait_recv()
        hop(kind, t, 7, core_flip(pd), me).wait_recv()

    small[...] = jnp.zeros_like(small)
    gain_one, shift_one, b_out, gain_two, shift_two, b_down = (
        ref[...].reshape(1, 768) for ref in (g1, s1_ref, bo, g2, s2_ref, bd)
    )

    lane = (lax.broadcasted_iota(jnp.int32, (SEQ, 128), 1) % HD).astype(F32)

    def head(r, carry):
        part = rows_at(r * SEQ, SEQ)
        normal, inverse = norm_parts(xv[part].astype(F32))
        n1v[part] = (normal * gain_one + shift_one).astype(BF16)
        seg_row = seg[pl.ds(r, 1)].astype(F32)
        seg_col = jnp.broadcast_to(seg_row, (128, SEQ)).T
        same = seg_col == lane
        code_q[part] = jnp.where(same, 0.0, MASKED).astype(BF16)
        code_k[part] = jnp.where(same, 1.0, 0.0).astype(BF16)
        for part6 in range(6):
            lanes = slice(part6 * 128, part6 * 128 + 128)
            masked = jnp.where(seg_col != 0.0, glv[part, lanes].astype(F32), 0.0)
            small[0:1, lanes] += jnp.sum(masked, axis=0, keepdims=True)
            glv[part, lanes] = masked.astype(BF16)
        return carry

    for pair in loads:
        pair[0].wait()
        pair[1].wait()
    lax.fori_loop(0, rows, head, 0)
    save_n1 = pltpu.make_async_copy(n1v, n1_hbm, out_sem.at[0, 0])
    save_n1.start()

    lo = lax.broadcasted_iota(jnp.int32, (SEQ, 128), 1) < HD
    lo_b = lo

    def unit_of(i):
        return xor4(z, i // 4) * 4 + i % 4

    def qkv_copy(slot, i):
        return pltpu.make_async_copy(stq.at[slot], qkvr_hbm.at[unit_of(i), pl.ds(0, 3)], stage_sem.at[0, slot])

    def soft_copies(slot, i):
        u = unit_of(i)
        return (
            pltpu.make_async_copy(str_.at[slot], qkvr_hbm.at[u, 3], stage_sem.at[1, slot]),
            pltpu.make_async_copy(ste.at[slot], e_hbm.at[u], stage_sem.at[2, slot]),
        )

    plan = (
        (s2, "heads", (3, 5, 8)),
        (s3, "heads", (3, 7, 10)),
        (s1, "heads", (1, 3, 5)),
        (s2, "out", (11, 12, 13)),
        (s3, "out", (13, 14, 15)),
        (s1, "out", (7, 8, 9)),
        (s2, "hidden", (13, 16, 18, 21, 23, 25)),
        (s3, "hidden", (16, 19, 21, 23, 26, 27)),
        (s1, "hidden", (10, 12, 15, 18, 20, 22)),
        (fin, "heads", (3, 7, 11)),
        (fin, "out", (16, 16, 16)),
        (fin, "hidden", (24, 24, 28, 28, 32, 32)),
    )

    def tick(i):
        for action, kind, whens in plan:
            def act(t, carry):
                action(kind, t)
                return carry

            first = KINDS[kind][0]
            start = sum((jnp.where(i > when, 1, 0) for when in whens), first)
            lax.fori_loop(start, sum((jnp.where(i >= when, 1, 0) for when in whens), first), act, 0)

    def project_heads(i, slot):
        g = xor4(z, i // 4 % 4)
        n1c = n1v[rows_at(i % 4 * 512, 512)]
        stq[slot, 0] = (nt(n1c, W[g, 0:256]) + BQ[g, 1:2]).astype(BF16)
        stq[slot, 1] = ((nt(n1c, W[g, 192:448]) + BQ[g, 0:1]) * (0.125 * LOG2E)).astype(BF16)
        stq[slot, 2, :, 0:192] = nt(n1c, W[g, 384:576]).astype(BF16)

    def attend(i, slot):
        g, c = xor4(z, i // 4), i % 4
        one = jnp.ones((SEQ, 128), BF16)
        for r in range(2):
            tr = slice(r * SEQ, r * SEQ + SEQ)
            dst = rows_at(c * 512 + r * SEQ, SEQ)
            cq, ck = code_q[dst], code_k[dst]

            def weights(qp, kp, h):
                sc = nt(qp, kp)
                e = jnp.exp2(sc - jnp.max(sc, axis=-1, keepdims=True)).astype(BF16)
                ste[slot, r * 3 + h] = e
                return e

            vp, qp, kp = (stq[slot, n, tr, 0:128] for n in range(3))
            e0 = weights(jnp.where(lo_b, qp, cq), jnp.where(lo_b, kp, ck), 0)
            o0 = nn(e0, jnp.where(lo_b, vp, one))
            e1 = weights(jnp.where(lo_b, cq, qp), jnp.where(lo_b, ck, kp), 1)
            o1 = nn(e1, jnp.where(lo_b, one, vp))
            r01 = 1.0 / pltpu.roll(jnp.where(lo, o1, o0), 64, 1)
            mix01 = jnp.where(lo, o0, o1) * r01
            vp, qp, kp = (stq[slot, n, tr, 128:256] for n in range(3))
            e2 = weights(jnp.where(lo_b, qp, cq), jnp.where(lo_b, kp, ck), 2)
            o2 = nn(e2, jnp.where(lo_b, vp, one))
            r2 = 1.0 / jnp.where(lo, pltpu.roll(o2, 64, 1), 1.0)
            mix2 = jnp.where(lo, o2 * r2, 0.0)
            mixv[g, dst, 0:128] = mix01.astype(BF16)
            mixv[g, dst, 128:256] = mix2.astype(BF16)
            str_[slot, tr, 0:128] = r01.astype(BF16)
            str_[slot, tr, 128:256] = r2.astype(BF16)

    def attend_pair(pair, carry):
        for slot in range(2):
            i = 2 * pair + slot
            tick(i)

            @pl.when(i >= 2)
            def _():
                for copy in soft_copies(slot, i):
                    copy.wait()

            @pl.when(i >= 1)
            def _():
                qkv_copy(1 - slot, i).wait()

            project_heads(i + 1, 1 - slot)
            attend(i, slot)
            for copy in soft_copies(slot, i):
                copy.start()

            @pl.when(i + 1 < 4 * chunks)
            def _():
                qkv_copy(1 - slot, i + 1).start()

        return carry

    for slot in range(2):
        stq[slot, 2, :, 128:256] = jnp.zeros((512, 128), BF16)
    project_heads(0, 0)
    qkv_copy(0, 0).start()
    lax.fori_loop(0, 2 * chunks, attend_pair, 0)
    qkv_copy(1, 0).wait()
    for slot in range(2):
        for copy in soft_copies(slot, 0):
            copy.wait()
    save_n1.wait()
    save_mixed = pltpu.make_async_copy(mixv, mixed_hbm, out_sem.at[0, 0])
    save_mixed.start()

    def project(c, carry):
        tick(4 * chunks + c)
        tok = rows_at(c * 512, 512)
        total = nn(mixv[0, tok, 0:192], W[0, 576:768])
        for g in range(1, MP):
            total = total + nn(mixv[g, tok, 0:192], W[g, 576:768])
        hidden = xv[tok].astype(F32) + total + b_out
        acc[tok] = hidden
        normal, inverse = norm_parts(hidden)
        xv[tok] = normal.astype(BF16)
        rstd[tok] = inverse
        n1v[tok] = (normal * gain_two + shift_two).astype(BF16)
        gn2[tok] = jnp.zeros((512, 768), F32)
        return carry

    lax.fori_loop(0, chunks, project, 0)
    save_wa = pltpu.make_async_copy(W.at[:, pl.ds(0, 768)], waf_hbm, out_sem.at[1, 0])
    save_wa.start()
    gwu[...] = jnp.zeros_like(gwu)
    gwd[...] = jnp.zeros_like(gwd)

    def feed(j, carry):
        tick(5 * chunks + j)
        g, c = xor4(z, j // 4), j % 4
        tok = rows_at(c * 512, 512)
        n2c = n1v[tok]
        glc = glv[tok]
        acts, lows, sums = [], [], []
        for n in range(3):
            cols = slice(n * 256, n * 256 + 256)
            pre = nn(n2c, W[g, 768:1536, cols]) + BU[g, 0:1, cols]
            grad_act = nt(glc, W[g, 1536 + n * 256 : 1792 + n * 256])
            square = pre * pre
            t = jnp.tanh(pre * (GELU_C + (GELU_C * GELU_A) * square))
            half = 0.5 + 0.5 * t
            slope = half + pre * (0.5 - 0.5 * (t * t)) * (GELU_C + (3.0 * GELU_C * GELU_A) * square)
            grad_pre = grad_act * slope
            acts.append((pre * half).astype(BF16))
            lows.append(grad_pre.astype(BF16))
            sums.append(jnp.sum(grad_pre, axis=0, keepdims=True))
        act = jnp.concatenate(acts, axis=1)
        low = jnp.concatenate(lows, axis=1)
        acc[tok] += nn(act, W[g, 1536:2304])
        gn2[tok] += nt(low, W[g, 768:1536])

        @pl.when(g == z)
        def _():
            gwu[...] += tn(n2c, low)
            gwd[...] += tn(act, glc)
            for n in range(3):
                small[1:2, n * 256 : n * 256 + 256] += sums[n]

        return carry

    lax.fori_loop(0, MP * chunks, feed, 0)
    gw_ref[0:768] = gwu[...].astype(BF16)
    gw_ref[768:1536] = gwd[...].astype(BF16)

    def closed_copies(r):
        tok = rows_at(r * SEQ, SEQ)
        return (
            pltpu.make_async_copy(xv.at[tok], out_hbm.at[tok], out_sem.at[0, 1 + r]),
            pltpu.make_async_copy(glv.at[tok], gres_hbm.at[tok], out_sem.at[1, 1 + r]),
        )

    def close(r, carry):
        tok = rows_at(r * SEQ, SEQ)
        normal = xv[tok].astype(F32)
        xv[tok] = (acc[tok] + b_down).astype(BF16)
        grad = gn2[tok]
        small[2:3] += jnp.sum(grad * normal, axis=0, keepdims=True)
        small[3:4] += jnp.sum(grad, axis=0, keepdims=True)
        total = glv[tok].astype(F32) + norm_back(grad, normal, rstd[tok], gain_two)
        small[4:5] += jnp.sum(total, axis=0, keepdims=True)
        glv[tok] = total.astype(BF16)
        for copy in closed_copies(r):
            copy.start()
        return carry

    lax.fori_loop(0, rows, close, 0)
    for copy in zcopies:
        copy.wait_send()
    for kind, (first, last, _) in KINDS.items():
        for t in range(first, last):
            hop(kind, t, 1, p, (a, z)).wait_send()
            hop(kind, t, 2, p, (b, z)).wait_send()
            hop(kind, t, 3, p, (fc, z)).wait_send()
            hop(kind, t, 4, pa, (b, z)).wait_send()
            hop(kind, t, 5, pa, (fc, z)).wait_send()
            hop(kind, t, 6, pb, (fc, z)).wait_send()
            hop(kind, t, 7, pd, (fc, z)).wait_send()
    save_mixed.wait()
    save_wa.wait()

    def closed(r, carry):
        for copy in closed_copies(r):
            copy.wait()
        return carry

    lax.fori_loop(0, rows, closed, 0)


def backward_kernel(
    count, extra,
    qkvr_hbm, e_hbm, n1_hbm, mixed_hbm, gres_hbm, x_hbm, waf_hbm, gw_hbm, small_in, g1,
    ig_hbm, gw_out, ga_out, small,
    WA, n1v, mixv, gresv, xv, dqkv, stq, ste,
    cur_w, ag_w, rec_w, cur_a, ag_a, rec_a, ga, head, head_rec, tail, tail_rec,
    load_sem, stage_sem, out_sem, row_sem, rs_send, rs_recv, ag_send, ag_recv, sm_send, sm_recv,
):
    d, z, p, kb, fc, a, b, bit_a, bit_b = places()
    xb, yb = p // 2 % 2, p // 4
    chunks = count // 512

    def load(src, dst, n):
        return pltpu.make_async_copy(src, dst, load_sem.at[n])

    top, rest = pl.ds(0, 512), pl.ds(512, count - 512)
    load_first = [
        load(waf_hbm.at[:, pl.ds(576, 192)], WA.at[:, pl.ds(576, 192)], 0),
        load(gres_hbm.at[top], gresv.at[top], 1),
        load(mixed_hbm.at[z], mixv.at[z], 2),
    ]
    load_grads = load(gw_hbm, cur_w, 3)
    load_next = [load(gres_hbm.at[rest], gresv.at[rest], 4)] + [
        load(mixed_hbm.at[xor4(z, s)], mixv.at[xor4(z, s)], 4 + s) for s in (1, 2, 3)
    ]
    load_n1 = load(n1_hbm, n1v, 8)
    load_last = [
        load(waf_hbm.at[:, pl.ds(0, 576)], WA.at[:, pl.ds(0, 576)], 9),
        load(x_hbm, xv, 10),
    ]

    def unit_of(i):
        return xor4(z, i // 4) * 4 + i % 4

    def fetch(i, slot):
        u = unit_of(i)
        return (
            pltpu.make_async_copy(qkvr_hbm.at[u], stq.at[slot], stage_sem.at[0, slot]),
            pltpu.make_async_copy(e_hbm.at[u], ste.at[slot], stage_sem.at[1, slot]),
        )

    for copy in fetch(0, 0):
        copy.start()
    for copy in load_first + [load_grads] + load_next + [load_n1] + load_last:
        copy.start()

    partners = [fc, a, b]
    bits = [kb, bit_a, bit_b]
    for m in range(extra):
        step = 8 << m
        partners.append(d + step * (1 - 2 * ((d // step) % 2)))
    peers = [
        d - p + (1 - kb if k % 2 else kb) + 2 * (1 - xb if k // 2 % 2 else xb) + 4 * (1 - yb if k // 4 else yb)
        for k in range(1, 8)
    ]
    barrier = pltpu.get_barrier_semaphore()
    for peer in peers + partners[3:]:
        pl.semaphore_signal(barrier, inc=1, device_id=(peer, z), device_id_type=MESH)
    pl.semaphore_wait(barrier, 7 + extra)

    def remote(src, dst, ss, rs, to):
        return pltpu.make_async_remote_copy(
            src_ref=src, dst_ref=dst, send_sem=ss, recv_sem=rs, device_id=to, device_id_type=MESH
        )

    class Reduce:
        def __init__(self, which, height, cur, ag, rec):
            self.which, self.cur, self.ag, self.rec = which, cur, ag, rec
            self.half = [height // 2, height // 4, height // 8]
            self.off = [0]
            for k in range(3):
                self.off.append(self.off[k] + bits[k] * self.half[k])
            self.place = [0, self.half[0], self.half[0] + self.half[1]]

        def at(self, ref, start, size):
            if isinstance(start, int):
                return ref.at[pl.ds(start, size)]
            return ref.at[pl.ds(pl.multiple_of(start, 32), size)]

        def rs(self, k):
            theirs = self.off[k] + (1 - bits[k]) * self.half[k]
            return remote(
                self.at(self.cur, theirs, self.half[k]),
                self.at(self.rec, self.place[k], self.half[k]),
                rs_send.at[self.which, k], rs_recv.at[self.which, k], (partners[k], z),
            )

        def send(self, k):
            self.rs(k).start()

        def add(self, start, place, size):
            for q in range(size // 96):
                mine = pl.ds(pl.multiple_of(start + q * 96, 32), 96)
                other = self.rec[place + q * 96 : place + q * 96 + 96]
                self.cur[mine] = (self.cur[mine].astype(F32) + other.astype(F32)).astype(BF16)

        def take(self, k):
            self.rs(k).wait_recv()
            self.add(self.off[k + 1], self.place[k], self.half[k])

        def middle(self):
            size = self.half[2]
            block = self.at(self.cur, self.off[3], size)
            for m in range(extra):
                place = self.place[2] + size * (m + 1)
                copy = remote(
                    block, self.at(self.rec, place, size),
                    rs_send.at[self.which, 3 + m], rs_recv.at[self.which, 3 + m], (partners[3 + m], z),
                )
                copy.start()
                copy.wait()
                self.add(self.off[3], place, size)
            mine = pl.ds(pl.multiple_of(self.off[3], 32), size)
            self.ag[mine] = self.cur[mine]

        def gather(self, k, start):
            part = self.at(self.ag, start, self.half[k])
            return remote(part, part, ag_send.at[self.which, k], ag_recv.at[self.which, k], (partners[k], z))

        def give(self, k):
            self.gather(k, self.off[k + 1]).start()

        def get(self, k):
            self.gather(k, self.off[k] + (1 - bits[k]) * self.half[k]).wait_recv()

        def drain(self):
            for k in range(3):
                self.rs(k).wait_send()
                self.gather(k, self.off[k + 1]).wait_send()

    big = Reduce(0, 1536, cur_w, ag_w, rec_w)
    att = Reduce(1, 768, cur_a, ag_a, rec_a)

    load_grads.wait()
    big.send(0)
    small[...] = small_in[...]
    tail[...] = jnp.zeros_like(tail)
    gain_one = g1[...].reshape(1, 768)
    lo = lax.broadcasted_iota(jnp.int32, (SEQ, 128), 1) < HD
    spread = (
        lax.broadcasted_iota(jnp.int32, (192, 384), 0) // HD
        == lax.broadcasted_iota(jnp.int32, (192, 384), 1) // 128
    ).astype(F32).astype(BF16)
    for copy in load_first:
        copy.wait()

    def own_ready():
        load_n1.wait()
        n1c = n1v[...]
        for c in range(3):
            ga[c * 192 : c * 192 + 192] = tn(dqkv[c, z, :, 0:192], n1c)
        ga[576:768] = tn(mixv[z, :, 0:192], gresv[...])
        for n, c in ((6, 1), (7, 0)):
            small[n : n + 1, 0:256] = jnp.sum(dqkv[c, z].astype(F32), axis=0, keepdims=True)
        cur_a[...] = ga[...].astype(BF16)
        att.send(0)

    def next_ready():
        for copy in load_next:
            copy.wait()

    plan = {
        1: next_ready,
        2: lambda: (big.take(0), big.send(1)),
        4: own_ready,
        6: lambda: (big.take(1), big.send(2)),
        7: lambda: (att.take(0), att.send(1)),
        9: lambda: (big.take(2), big.middle(), big.give(2)),
        10: lambda: (att.take(1), att.send(2)),
        12: lambda: (big.get(2), big.give(1)),
        13: lambda: (att.take(2), att.middle(), att.give(2)),
        15: lambda: (att.get(2),),
    }

    def unit(i, carry):
        for when, action in plan.items():
            @pl.when(i == when)
            def _():
                action()

        slot = i % 2
        for copy in fetch(i, slot):
            copy.wait()

        @pl.when(i + 1 < 4 * chunks)
        def _():
            for copy in fetch(i + 1, 1 - slot):
                copy.start()

        g, c = xor4(z, i // 4), i % 4
        tok = rows_at(c * 512, 512)
        low = gresv[tok]
        mixed = mixv[g, tok, 0:192]
        grad_mixed = nt(low, WA[g, 576:768]).astype(BF16).astype(F32)

        scaled = (grad_mixed * stq[slot, 3, :, 0:192].astype(F32)).astype(BF16)
        delta = nn((scaled.astype(F32) * mixed.astype(F32)).astype(BF16), spread)
        zero = jnp.zeros((SEQ, 128), BF16)
        for r in range(2):
            tr = slice(r * SEQ, r * SEQ + SEQ)
            dst = rows_at(c * 512 + r * SEQ, SEQ)
            vp, qp, kp = (stq[slot, n, tr, 0:128] for n in range(3))
            dp = scaled[tr, 0:128]
            res = []
            for h in range(2):
                e = ste[slot, r * 3 + h]
                mine = jnp.where(lo, vp, zero) if h == 0 else jnp.where(lo, zero, vp)
                dh = delta[tr, h * 128 : h * 128 + 128]
                grad = nt(dp, mine) - jnp.concatenate([dh, dh], axis=1)
                ds = (e.astype(F32) * grad).astype(BF16)
                res.append((tn(e, dp), nn(ds, kp), tn(ds, qp)))
            pairs = [jnp.where(lo, x0, x1) for x0, x1 in zip(res[0], res[1])]
            dv, dq, dk = pairs[0], pairs[1] * 0.125, pairs[2] * (1.0 / LOG2E)
            for n, value in enumerate((dv, dq, dk)):
                dqkv[n, g, dst, 0:128] = value.astype(BF16)

            v2, q2, k2 = (stq[slot, n, tr, 128:192] for n in range(3))
            d2 = scaled[tr, 128:192]
            e = ste[slot, r * 3 + 2]
            dh = delta[tr, 256:384]
            ds = (e.astype(F32) * (nt(d2, v2) - jnp.concatenate([dh, dh], axis=1))).astype(BF16)
            dv2, dq2, dk2 = tn(e, d2), nn(ds, k2) * 0.125, tn(ds, q2) * (1.0 / LOG2E)
            for n, value in enumerate((dv2, dq2, dk2)):
                dqkv[n, g, dst, 128:192] = value.astype(BF16)

        return carry

    lax.fori_loop(0, 4 * chunks, unit, 0)
    att.give(1)

    def exchange(ref, rec, which):
        mine = [remote(ref, rec.at[p], sm_send.at[which, k], sm_recv.at[which, p], (peer, z)) for k, peer in enumerate(peers)]
        for copy in mine:
            copy.start()
        return mine

    def total_of(ref, rec, which, mine):
        for copy in mine:
            copy.wait_send()
        for k, peer in enumerate(peers):
            other = peer - (d - p)
            remote(ref, rec.at[other], sm_send.at[which, k], sm_recv.at[which, other], (peer, z)).wait_recv()
        rec[p] = ref[...]
        ref[...] = sum(rec[k] for k in range(1, 8)) + rec[0]
        for m in range(extra):
            copy = remote(ref, rec.at[8 + m], sm_send.at[which, 7 + m], sm_recv.at[which, 8 + m], (partners[3 + m], z))
            copy.start()
            copy.wait()
            ref[...] += rec[8 + m]

    head[...] = small[0:8]
    sent_head = exchange(head, head_rec, 0)
    for copy in load_last:
        copy.wait()

    def save_rows(c):
        tok = rows_at(c * 512, 512)
        return pltpu.make_async_copy(xv.at[tok], ig_hbm.at[tok], row_sem.at[c])

    def last(c, carry):
        @pl.when(c == 1)
        def _():
            big.get(1)
            big.give(0)

        @pl.when(c == 3)
        def _():
            att.get(1)
            att.give(0)

        tok = rows_at(c * 512, 512)
        total = nn(dqkv[0, 0, tok, 0:192], WA[0, 0:192])
        for g in range(MP):
            for n in range(3):
                if g + n > 0:
                    total = total + nn(dqkv[n, g, tok, 0:192], WA[g, n * 192 : n * 192 + 192])
        normal, inverse = norm_parts(xv[tok].astype(F32))
        tail[0:1] += jnp.sum(total * normal, axis=0, keepdims=True)
        tail[1:2] += jnp.sum(total, axis=0, keepdims=True)
        xv[tok] = (gresv[tok].astype(F32) + norm_back(total, normal, inverse, gain_one)).astype(BF16)
        save_rows(c).start()
        return carry

    lax.fori_loop(0, chunks, last, 0)

    sent_tail = exchange(tail, tail_rec, 1)
    big.get(0)
    save_w = pltpu.make_async_copy(ag_w, gw_out, out_sem.at[0])
    save_w.start()
    att.get(0)
    save_a = pltpu.make_async_copy(ag_a, ga_out, out_sem.at[2])
    save_a.start()
    total_of(head, head_rec, 0, sent_head)
    small[0:8] = head[...]
    total_of(tail, tail_rec, 1, sent_tail)
    small[8:10] = tail[...]
    big.drain()
    att.drain()
    save_w.wait()
    for c in range(chunks):
        save_rows(c).wait()
    save_a.wait()


def finish_kernel(
    bo_in, ig_in, gw_in, ga_in, small,
    bo_out, ig_out, gqkv, gbqv, gwo, gwu, gwd, g_b_out, g_gain_one, g_shift_one, g_b_up, g_b_down, g_gain_two, g_shift_two,
    bov, igv, gwv, gav, fw, fa, in_sem, out_sem,
):
    half = bov.shape[0] // 2
    load_w = [
        pltpu.make_async_copy(gw_in.at[pl.ds(768 * h, 768)], gwv.at[pl.ds(768 * h, 768)], in_sem.at[h]) for h in range(2)
    ]
    load_a = pltpu.make_async_copy(ga_in, gav, in_sem.at[2])
    load_rows = []
    for src, buf, dst in ((bo_in, bov, bo_out), (ig_in, igv, ig_out)):
        for q in range(4):
            part = pl.ds(q * (half // 2), half // 2)
            copy = pltpu.make_async_copy(src.at[part], buf.at[part], in_sem.at[3 + len(load_rows)])
            load_rows.append((copy, buf.at[part], dst.at[part]))
    for copy in load_w + [load_a] + [rows[0] for rows in load_rows]:
        copy.start()
    gbqv[...] = small[6:8, 0 : gbqv.shape[1]]
    for ref, n in ((g_b_out, 4), (g_gain_one, 8), (g_shift_one, 9), (g_b_up, 1), (g_b_down, 0), (g_gain_two, 2), (g_shift_two, 3)):
        ref[...] = small[n : n + 1].reshape(768)
    saves = []

    def save(src, dst):
        saves.append(pltpu.make_async_copy(src, dst, out_sem.at[len(saves)]))
        saves[-1].start()

    for h, dst in enumerate((gwu, gwd)):
        load_w[h].wait()
        for q in range(2):
            part = pl.ds(768 * h + 384 * q, 384)
            fw[part] = gwv[part].astype(F32)
            save(fw.at[part], dst.at[pl.ds(384 * q, 384)])
    load_a.wait()
    for n, dst in enumerate((gqkv.at[2], gqkv.at[0], gqkv.at[1], gwo)):
        part = pl.ds(192 * n, 192)
        fa[part] = gav[part].astype(F32)
        save(fa.at[part], dst)
    for copy, buf, dst in load_rows:
        copy.wait()
        save(buf, dst)
    for copy in saves:
        copy.wait()


def layer(n_dp, tokens, segment_ids, cotangent, w_qkv, b_qv, w_out, b_out, gain_one, shift_one, w_up, b_up, w_down, b_down, gain_two, shift_two):
    count, width = tokens.shape[0], w_qkv.shape[2]
    rows = segment_ids.shape[0]
    units = MP * (count // 512)
    extra = (n_dp // 8).bit_length() - 1
    any_space = pl.BlockSpec(memory_space=pl.ANY)
    in_vmem = pl.BlockSpec(memory_space=pltpu.VMEM)
    wt = jnp.transpose(w_qkv, (0, 2, 1))
    dma = pltpu.SemaphoreType.DMA

    def sds(shape, dtype):
        return jax.ShapeDtypeStruct(shape, dtype)

    def fwd(*refs):
        return forward_kernel(count, *refs)

    block_out, qkvr, e, n1, mixed, gres, waf, gw, small = pl.pallas_call(
        fwd,
        name="forward",
        out_shape=(
            sds((count, 768), BF16),
            sds((units, 4, 512, 256), BF16),
            sds((units, 6, SEQ, SEQ), BF16),
            sds((count, 768), BF16),
            sds((MP, count, 256), BF16),
            sds((count, 768), BF16),
            sds((MP, 768, 768), BF16),
            sds((1536, 768), BF16),
            sds((16, 768), F32),
        ),
        in_specs=[any_space, any_space, in_vmem] + [any_space] * 5 + [in_vmem] * 7,
        out_specs=(any_space,) * 7 + (in_vmem, in_vmem),
        scratch_shapes=[
            pltpu.VMEM((MP, 2304, 768), BF16),
            pltpu.VMEM((MP, 2, 256), F32),
            pltpu.VMEM((MP, 1, 768), F32),
            pltpu.VMEM((count, 768), BF16),
            pltpu.VMEM((count, 768), BF16),
            pltpu.VMEM((count, 768), BF16),
            pltpu.VMEM((MP, count, 256), BF16),
            pltpu.VMEM((count, 768), F32),
            pltpu.VMEM((count, 768), F32),
            pltpu.VMEM((count, 128), BF16),
            pltpu.VMEM((count, 128), BF16),
            pltpu.VMEM((count, 1), F32),
            pltpu.VMEM((768, 768), F32),
            pltpu.VMEM((768, 768), F32),
            pltpu.VMEM((2, 3, 512, 256), BF16),
            pltpu.VMEM((2, 512, 256), BF16),
            pltpu.VMEM((2, 6, SEQ, SEQ), BF16),
            dma((2, count // 512)), dma((7,)), dma((3, 2)), dma((2, 1 + rows)),
            dma((12,)), dma((12, 8)), dma((12, 8)), dma((6,)), dma((6,)),
        ],
        compiler_params=pltpu.CompilerParams(collective_id=0, has_side_effects=True, vmem_limit_bytes=VMEM_LIMIT),
    )(
        tokens, cotangent, segment_ids, wt, w_out, w_up, w_down, b_up, b_qv,
        gain_one, shift_one, b_out, gain_two, shift_two, b_down,
    )

    def bwd(*refs):
        return backward_kernel(count, extra, *refs)

    input_grad, gw_full, ga_full, small = pl.pallas_call(
        bwd,
        name="backward",
        out_shape=(
            sds((count, 768), BF16),
            sds((1536, 768), BF16),
            sds((768, 768), BF16),
            sds((16, 768), F32),
        ),
        in_specs=[any_space] * 8 + [in_vmem, in_vmem],
        out_specs=(any_space,) * 3 + (in_vmem,),
        scratch_shapes=[
            pltpu.VMEM((MP, 768, 768), BF16),
            pltpu.VMEM((count, 768), BF16),
            pltpu.VMEM((MP, count, 256), BF16),
            pltpu.VMEM((count, 768), BF16),
            pltpu.VMEM((count, 768), BF16),
            pltpu.VMEM((3, MP, count, 256), BF16),
            pltpu.VMEM((2, 4, 512, 256), BF16),
            pltpu.VMEM((2, 6, SEQ, SEQ), BF16),
            pltpu.VMEM((1536, 768), BF16),
            pltpu.VMEM((1536, 768), BF16),
            pltpu.VMEM((1344 + 192 * extra, 768), BF16),
            pltpu.VMEM((768, 768), BF16),
            pltpu.VMEM((768, 768), BF16),
            pltpu.VMEM((672 + 96 * extra, 768), BF16),
            pltpu.VMEM((768, 768), F32),
            pltpu.VMEM((8, 768), F32),
            pltpu.VMEM((8 + extra, 8, 768), F32),
            pltpu.VMEM((2, 768), F32),
            pltpu.VMEM((8 + extra, 2, 768), F32),
            dma((11,)), dma((2, 2)), dma((3,)), dma((count // 512,)),
            dma((2, 3 + extra)), dma((2, 3 + extra)), dma((2, 3)), dma((2, 3)),
            dma((2, 7 + extra)), dma((2, 8 + extra)),
        ],
        compiler_params=pltpu.CompilerParams(collective_id=1, has_side_effects=True, vmem_limit_bytes=VMEM_LIMIT),
    )(qkvr, e, n1, mixed, gres, tokens, waf, gw, small, gain_one)

    row = sds((768,), F32)
    block_out, input_grad, grad_qkv, b_qv_grad, grad_out, grad_up, grad_down, *vectors = pl.pallas_call(
        finish_kernel,
        name="finish",
        out_shape=(
            sds((count, 768), BF16), sds((count, 768), BF16), sds((3, width, 768), F32), sds((2, width), F32),
            sds((width, 768), F32), sds((768, 768), F32), sds((768, 768), F32),
        ) + (row,) * 7,
        in_specs=[any_space] * 4 + [in_vmem],
        out_specs=(any_space,) * 3 + (in_vmem,) + (any_space,) * 3 + (in_vmem,) * 7,
        scratch_shapes=[
            pltpu.VMEM((count, 768), BF16), pltpu.VMEM((count, 768), BF16),
            pltpu.VMEM((1536, 768), BF16), pltpu.VMEM((768, 768), BF16),
            pltpu.VMEM((1536, 768), F32), pltpu.VMEM((768, 768), F32),
            dma((11,)), dma((16,)),
        ],
        compiler_params=pltpu.CompilerParams(vmem_limit_bytes=VMEM_LIMIT),
    )(block_out, input_grad, gw_full, ga_full, small)
    g_b_out, g_gain_one, g_shift_one, g_b_up, g_b_down, g_gain_two, g_shift_two = vectors
    return (
        block_out,
        input_grad,
        jnp.transpose(grad_qkv, (0, 2, 1)),
        b_qv_grad,
        grad_out,
        g_b_out,
        g_gain_one,
        g_shift_one,
        grad_up,
        g_b_up,
        grad_down,
        g_b_down,
        g_gain_two,
        g_shift_two,
    )


def solution(mesh):
    n_dp = mesh.shape["dp"]

    def run(*args):
        return layer(n_dp, *args)

    placed = (
        P("dp", None), P("dp", None), P("dp", None), P(None, None, "mp"), P(None, "mp"), P("mp", None), P(), P(), P(),
        P(None, "mp"), P("mp"), P("mp", None), P(), P(), P(),
    )
    return jax.shard_map(
        run,
        mesh=mesh,
        in_specs=placed,
        out_specs=(
            P("dp", None), P("dp", None), P(None, None, "mp"), P(None, "mp"), P("mp", None), P(), P(), P(),
            P(None, "mp"), P("mp"), P("mp", None), P(), P(), P(),
        ),
        check_vma=False,
    )
```
